32 devices in a mesh: dp: 4 (over y, x), row: 4 (over z), col: 2 (over core).
Axes of the slice: x: 2, y: 2, z: 4, core: 2. Of those that a mesh axis runs over, the one named last changes fastest.
Arguments:
- hidden_in: bfloat16 [8192, 1024], P(('dp', 'col'), 'row'), may hold values from -6 to 6
- segment_ids: int32 [16, 512], P(('dp', 'row')), may hold values from 0 to 16, as said below
- query_weight: bfloat16 [1024, 1024], P('row', 'col'), may hold values from -0.1875 to 0.1875
- query_bias: bfloat16 [1024], P('col'), may hold values from -3 to 3
- key_weight: bfloat16 [1024, 1024], P('row', 'col'), may hold values from -0.1875 to 0.1875
- value_weight: bfloat16 [1024, 1024], P('row', 'col'), may hold values from -0.1875 to 0.1875
- value_bias: bfloat16 [1024], P('col'), may hold values from -3 to 3
- attn_out_weight: bfloat16 [1024, 1024], P('col', 'row'), may hold values from -0.75 to 0.75
- attn_out_bias: bfloat16 [1024], P('row'), may hold values from -3 to 3
- norm1_gain: bfloat16 [1024], P('row'), may hold values from 0.099609375 to 1.8984375
- first_norm_offset: bfloat16 [1024], P('row'), may hold values from -3 to 3
- inner_weight: bfloat16 [1024, 4096], P('row', 'col'), may hold values from -0.1875 to 0.1875
- inner_bias: bfloat16 [4096], P('col'), may hold values from -3 to 3
- outer_weight: bfloat16 [4096, 1024], P('col', 'row'), may hold values from -0.1875 to 0.1875
- outer_bias: bfloat16 [1024], P('row'), may hold values from -3 to 3
- norm2_gain: bfloat16 [1024], P('row'), may hold values from 0.099609375 to 1.8984375
- second_norm_offset: bfloat16 [1024], P('row'), may hold values from -3 to 3
- cotangent: bfloat16 [8192, 1024], P(('dp', 'col'), 'row'), may hold values from -6 to 6
Outputs:
- layer_out: bfloat16 [8192, 1024], P(('dp', 'col'), 'row')
- input_grad: bfloat16 [8192, 1024], P(('dp', 'col'), 'row')
- query_weight_grad: float32 [1024, 1024], P('row', 'col')
- query_bias_grad: float32 [1024], P('col')
- key_weight_grad: float32 [1024, 1024], P('row', 'col')
- value_weight_grad: float32 [1024, 1024], P('row', 'col')
- value_bias_grad: float32 [1024], P('col')
- attn_out_weight_grad: float32 [1024, 1024], P('col', 'row')
- attn_out_bias_grad: float32 [1024], P('row')
- norm1_gain_grad: float32 [1024], P('row')
- norm1_shift_grad: float32 [1024], P('row')
- inner_weight_grad: float32 [1024, 4096], P('row', 'col')
- inner_bias_grad: float32 [4096], P('col')
- outer_weight_grad: float32 [4096, 1024], P('col', 'row')
- outer_bias_grad: float32 [1024], P('row')
- norm2_gain_grad: float32 [1024], P('row')
- norm2_shift_grad: float32 [1024], P('row')
The draws below stay inside these ranges and needn't reach their ends.
Inputs may be any that keep to these rules, and one draw needn't show every extreme that they name: `segment_ids`: within each sequence the ids start at 0 and rise by one at each document boundary; every document but the last of a sequence has 20 to 200 tokens, the last 1 to 200; in each sequence the first or the second document has exactly 200 tokens (others may have 200 too).
All inputs are finite; a program needn't handle non-finite values.
Results may differ from the reference program's by a relative error of at most 0.015.
Values may be sent and summed in bfloat16 or wider, within the bound.
A program may use at most 192 MiB of HBM per device.

```python
import math
import jax
import jax.numpy as jnp
from jax import lax

MODEL_WIDTH = 1024
FF = 4096
HD = 64
SEQ = 512
DOC_MIN = 20
DOC_MAX = 200
TOKENS = 8192
NSEQ = 16


def draw_segment_ids(key, part):
    count = SEQ // DOC_MIN + 1
    first_branch = jax.random.fold_in(key, 11)
    second_branch = jax.random.fold_in(key, 23)
    sizes = jax.random.randint(first_branch, (NSEQ, count), DOC_MIN, DOC_MAX + 1)
    picked = jax.random.randint(second_branch, (NSEQ, 1), 0, 2)
    leading = (jnp.arange(NSEQ) == 0)[:, None]
    sizes = jnp.where(leading, DOC_MIN, sizes)
    picked = jnp.where(leading, 0, picked)
    sizes = jnp.where(jnp.arange(count)[None, :] == picked, DOC_MAX, sizes)
    ends = jnp.cumsum(sizes, axis=1)
    places = jnp.arange(SEQ)
    return jnp.sum((ends[:, None, :] <= places[None, :, None]).astype(jnp.int32), axis=2).astype(jnp.int32)


def steps_of(key, shape, split, smallest, largest):
    loudness = 1.0
    for axis_at, shards_of in split:
        heights = jax.random.uniform(jax.random.fold_in(jax.random.fold_in(key, 6), axis_at), (shards_of,), jnp.float32, smallest / len(split), largest / len(split))
        loudness = loudness * jnp.repeat(jnp.exp(heights), shape[axis_at] // shards_of).reshape((-1,) + (1,) * (len(shape) - 1 - axis_at))
    return loudness


def gaussian(rng, extent, deviation, bound, pieces=(), kind=jnp.bfloat16):
    level = steps_of(rng, extent, pieces, -0.22, 0.18) if pieces else 1.0
    values = jax.random.normal(rng, extent, jnp.float32) * deviation * level
    return jnp.minimum(jnp.maximum(values, -bound), bound).astype(kind)


def setup_inputs(seed: int = 0) -> dict:
    splits = jax.random.split(jax.random.key(seed), 19)
    return {
        "hidden_in": gaussian(splits[0], (TOKENS, MODEL_WIDTH), 1.0, 6.0, ((0, 8), (1, 4))),
        "segment_ids": draw_segment_ids(jax.random.fold_in(splits[18], 71), 0),
        "query_weight": gaussian(splits[2], (MODEL_WIDTH, MODEL_WIDTH), MODEL_WIDTH ** -0.5, 0.1875, ((0, 4), (1, 2))),
        "query_bias": gaussian(splits[3], (MODEL_WIDTH,), 0.5, 3.0, ((0, 2),)),
        "key_weight": gaussian(splits[4], (MODEL_WIDTH, MODEL_WIDTH), MODEL_WIDTH ** -0.5, 0.1875, ((0, 4), (1, 2))),
        "value_weight": gaussian(splits[5], (MODEL_WIDTH, MODEL_WIDTH), MODEL_WIDTH ** -0.5, 0.1875, ((0, 4), (1, 2))),
        "value_bias": gaussian(splits[6], (MODEL_WIDTH,), 0.5, 3.0, ((0, 2),)),
        "attn_out_weight": gaussian(splits[7], (MODEL_WIDTH, MODEL_WIDTH), (MODEL_WIDTH // 16) ** -0.5, 0.75, ((0, 2), (1, 4))),
        "attn_out_bias": gaussian(splits[8], (MODEL_WIDTH,), 0.5, 3.0, ((0, 4),)),
        "norm1_gain": jnp.clip(1.0 + 0.18 * jax.random.normal(splits[9], (MODEL_WIDTH,), jnp.float32), 0.099609375, 1.8984375).astype(jnp.bfloat16),
        "first_norm_offset": gaussian(splits[10], (MODEL_WIDTH,), 0.5, 3.0, ((0, 4),)),
        "inner_weight": gaussian(splits[11], (MODEL_WIDTH, FF), MODEL_WIDTH ** -0.5, 0.1875, ((0, 4), (1, 2))),
        "inner_bias": gaussian(splits[12], (FF,), 0.5, 3.0, ((0, 2),)),
        "outer_weight": gaussian(splits[13], (FF, MODEL_WIDTH), (FF // 4) ** -0.5, 0.1875, ((0, 2), (1, 4))),
        "outer_bias": gaussian(splits[14], (MODEL_WIDTH,), 0.5, 3.0, ((0, 4),)),
        "norm2_gain": jnp.clip(1.0 + 0.18 * jax.random.normal(splits[15], (MODEL_WIDTH,), jnp.float32), 0.099609375, 1.8984375).astype(jnp.bfloat16),
        "second_norm_offset": gaussian(splits[16], (MODEL_WIDTH,), 0.5, 3.0, ((0, 4),)),
        "cotangent": gaussian(splits[17], (TOKENS, MODEL_WIDTH), 1.0, 6.0, ((0, 8), (1, 4))),
    }


@jax.custom_vjp
def low(v):
    return lax.optimization_barrier(v.astype(jnp.bfloat16)).astype(jnp.float32)

@jax.custom_vjp
def low_back(v):
    return v

def low_keep(v):
    return (low(v), None)

def low_pass(kept, incoming_gradient):
    return (incoming_gradient,)

def back_keep(v):
    return (v, None)

def back_low(kept, incoming_gradient):
    return (low(incoming_gradient),)
low.defvjp(low_keep, low_pass)
low_back.defvjp(back_keep, back_low)
norm_eps = 1e-12

def matmul(left, right):
    return jnp.dot(left, right, precision=lax.Precision.HIGHEST)

def layer_norm(values, norm_gain, norm_offset):
    row_mean = lax.optimization_barrier(jnp.mean(values, -1, keepdims=True))
    centred = values - row_mean
    var_val = lax.optimization_barrier(jnp.mean(centred * centred, -1, keepdims=True))
    return centred * lax.rsqrt(var_val + norm_eps) * norm_gain + norm_offset

def attend_sequence(items):
    queries, keys, values, segments = items
    qhead = queries.reshape(SEQ, MODEL_WIDTH // HD, HD)
    khead = keys.reshape(SEQ, MODEL_WIDTH // HD, HD)
    vhead = values.reshape(SEQ, MODEL_WIDTH // HD, HD)
    scores = jnp.einsum('qhd,khd->hqk', qhead, khead, precision=lax.Precision.HIGHEST)
    scores = low_back(scores * 0.125)
    same = segments[:, None] == segments[None, :]
    scores = jnp.where(same[None], scores, -1e+30)
    probs = jax.nn.softmax(scores, axis=-1)
    mixed = jnp.einsum('hqk,khd->qhd', low(probs), vhead, precision=lax.Precision.HIGHEST)
    return mixed.reshape(SEQ, MODEL_WIDTH)

def layer(params, rows, segments):
    wq, bq, wk, wv, bv, wo, bo, gain1, shift1, wi, bi, wout, bout, gain2, shift2 = params
    count = segments.shape[0]
    queries = low_back(low(matmul(rows, wq) + bq))
    keys = low_back(low(matmul(rows, wk)))
    values = low_back(low(matmul(rows, wv) + bv))
    mixed = lax.map(jax.checkpoint(attend_sequence), (queries.reshape(count, SEQ, MODEL_WIDTH), keys.reshape(count, SEQ, MODEL_WIDTH), values.reshape(count, SEQ, MODEL_WIDTH), segments))
    mixed = low_back(low(mixed.reshape(count * SEQ, MODEL_WIDTH)))
    attn = low_back(matmul(mixed, wo) + bo)
    hidden_state = layer_norm(rows + attn, gain1, shift1)
    inner = low_back(matmul(low(hidden_state), wi) + bi)
    active = low(jax.nn.gelu(inner, approximate=False))
    outer_product = low_back(matmul(active, wout) + bout)
    return layer_norm(hidden_state + outer_product, gain2, shift2)

def reference(hidden_in, segment_ids, query_weight, query_bias, key_weight, value_weight, value_bias, attn_out_weight, attn_out_bias, norm1_gain, first_norm_offset, inner_weight, inner_bias, outer_weight, outer_bias, norm2_gain, second_norm_offset, cotangent):
    params = tuple((p.astype(jnp.float32) for p in (query_weight, query_bias, key_weight, value_weight, value_bias, attn_out_weight, attn_out_bias, norm1_gain, first_norm_offset, inner_weight, inner_bias, outer_weight, outer_bias, norm2_gain, second_norm_offset)))
    per_block = math.gcd(NSEQ, max(1, 4096 // SEQ))
    blocks = NSEQ // per_block
    rows = hidden_in.astype(jnp.float32).reshape(blocks, per_block * SEQ, MODEL_WIDTH)
    grads_in = cotangent.astype(jnp.float32).reshape(blocks, per_block * SEQ, MODEL_WIDTH)
    segments = segment_ids.reshape(blocks, per_block, SEQ)

    def step(totals, items):
        block_rows, block_segments, block_grads = items
        result, pullback = jax.vjp(lambda p, r: layer(p, r, block_segments), params, block_rows)
        param_grads, row_grads = pullback(block_grads)
        totals = jax.tree.map(lambda a, b: a + b, totals, param_grads)
        return (totals, (result.astype(jnp.bfloat16), row_grads.astype(jnp.bfloat16)))
    start = jax.tree.map(jnp.zeros_like, params)
    totals, (outputs, in_grads) = lax.scan(step, start, (rows, segments, grads_in))
    g_wq, g_bq, g_wk, g_wv, g_bv, g_wo, g_bo, g_n1, g_s1, g_wi, g_bi, g_wout, g_bout, g_n2, g_s2 = totals
    return (outputs.reshape(TOKENS, MODEL_WIDTH), in_grads.reshape(TOKENS, MODEL_WIDTH), g_wq, g_bq, g_wk, g_wv, g_bv, g_wo, g_bo, g_n1, g_s1, g_wi, g_bi, g_wout, g_bout, g_n2, g_s2)
```

```python
import functools

import jax
import jax.numpy as jnp
from jax import lax
from jax.experimental import pallas as pl
from jax.experimental.pallas import tpu as pltpu
from jax.sharding import PartitionSpec as P

MODEL_WIDTH = 1024
HD = 64
SEQ = 512


norm_eps = 1e-12
inv_root_two = 0.7071067811865476
inv_root_two_pi = 0.3989422804014327


def product(left, right):
    return jnp.dot(left, right, preferred_element_type=jnp.float32)


def over_tokens(left, right):
    return lax.dot_general(
        left, right, (((0,), (0,)), ((), ())), preferred_element_type=jnp.float32
    )


def against(left, right):
    return lax.dot_general(
        left, right, (((1,), (1,)), ((), ())), preferred_element_type=jnp.float32
    )


def col_gather(values):
    return lax.all_gather(values, "col", axis=0, tiled=True)


def row_gather(values):
    return lax.all_gather(values, "row", axis=0, tiled=True)


def row_reduce(values):
    return lax.psum_scatter(values, "row", scatter_dimension=0, tiled=True)


def col_reduce(values):
    return lax.psum_scatter(values, "col", scatter_dimension=0, tiled=True)


def row_sum_values(first_branch, second_branch):
    return lax.psum((first_branch, second_branch), "row")


def apply_norm(preact_input, norm_gain, norm_offset):
    total, squares = row_sum_values(
        jnp.sum(preact_input, 1), jnp.sum(preact_input * preact_input, 1)
    )
    row_mean = total / MODEL_WIDTH
    inverse_deviation = lax.rsqrt(squares / MODEL_WIDTH - row_mean * row_mean + norm_eps)
    centred_rows = (preact_input - row_mean[:, None]) * inverse_deviation[:, None]
    return (centred_rows * norm_gain + norm_offset, centred_rows, inverse_deviation)


def norm_backward_pass(incoming_gradient, centred_rows, inverse_deviation, norm_gain):
    scaled_rows = incoming_gradient * norm_gain
    first_branch, second_branch = row_sum_values(
        jnp.sum(scaled_rows, 1), jnp.sum(scaled_rows * centred_rows, 1)
    )
    return inverse_deviation[:, None] * (
        scaled_rows
        - first_branch[:, None] / MODEL_WIDTH
        - centred_rows * second_branch[:, None] / MODEL_WIDTH
    )


def seg_mask(segments):
    return (segments[:, None] == segments[None, :])[None]


def attend_forward(items):
    queries, keys, values, segments = items
    scores = jnp.einsum("qhd,khd->hqk", queries, keys, preferred_element_type=jnp.float32) * 0.125
    scores = jnp.where(seg_mask(segments), scores, -1e30)
    peak = jnp.max(scores, -1, keepdims=True)
    expo = jnp.exp(scores - peak)
    total = jnp.sum(expo, -1, keepdims=True)
    probs = (expo / total).astype(jnp.bfloat16)
    mixed = jnp.einsum("hqk,khd->qhd", probs, values, preferred_element_type=jnp.float32)
    return (mixed.astype(jnp.bfloat16), (peak + jnp.log(total))[..., 0])


def attend_backward(items):
    queries, keys, values, segments, dmixed, lse = items
    scores = jnp.einsum("qhd,khd->hqk", queries, keys, preferred_element_type=jnp.float32) * 0.125
    probs = jnp.where(seg_mask(segments), jnp.exp(scores - lse[..., None]), 0.0)
    dvalues = jnp.einsum(
        "hqk,qhd->khd", probs.astype(jnp.bfloat16), dmixed, preferred_element_type=jnp.float32
    )
    dprobs = jnp.einsum("qhd,khd->hqk", dmixed, values, preferred_element_type=jnp.float32)
    middle = jnp.sum(probs * dprobs, -1, keepdims=True)
    dscores = (probs * (dprobs - middle)).astype(jnp.bfloat16)
    dqueries = jnp.einsum("hqk,khd->qhd", dscores, keys, preferred_element_type=jnp.float32) * 0.125
    dkeys = jnp.einsum("hqk,qhd->khd", dscores, queries, preferred_element_type=jnp.float32) * 0.125
    return (dqueries.astype(jnp.bfloat16), dkeys.astype(jnp.bfloat16), dvalues.astype(jnp.bfloat16))


def shards(
    hidden_in,
    segment_ids,
    query_weight,
    query_bias,
    key_weight,
    value_weight,
    value_bias,
    attn_out_weight,
    attn_out_bias,
    norm1_gain,
    first_norm_offset,
    inner_weight,
    inner_bias,
    outer_weight,
    outer_bias,
    norm2_gain,
    second_norm_offset,
    cotangent,
):
    local_seqs = segment_ids.shape[0]
    col_width = query_weight.shape[1]
    head_local = col_width // HD
    first_norm_gain = norm1_gain.astype(jnp.float32)
    second_norm_gain = norm2_gain.astype(jnp.float32)
    x_full = col_gather(hidden_in)
    part_q, part_k, part_v = (
        lax.psum_scatter(product(x_full, query_weight), "row", scatter_dimension=0, tiled=True),
        lax.psum_scatter(product(x_full, key_weight), "row", scatter_dimension=0, tiled=True),
        lax.psum_scatter(product(x_full, value_weight), "row", scatter_dimension=0, tiled=True),
    )
    queries = (part_q + query_bias).astype(jnp.bfloat16)
    keys = part_k.astype(jnp.bfloat16)
    values = (part_v + value_bias).astype(jnp.bfloat16)
    q_heads = queries.reshape(local_seqs, SEQ, head_local, HD)
    k_heads = keys.reshape(local_seqs, SEQ, head_local, HD)
    v_heads = values.reshape(local_seqs, SEQ, head_local, HD)
    mixed, lse = lax.map(attend_forward, (q_heads, k_heads, v_heads, segment_ids))
    mixed = mixed.reshape(local_seqs * SEQ, col_width)
    mixed_full = row_gather(mixed)
    attn = col_reduce(product(mixed_full, attn_out_weight)) + attn_out_bias
    first_preact = hidden_in.astype(jnp.float32) + attn
    hidden_state, first_centred_rows, first_inverse_deviation = apply_norm(
        first_preact, first_norm_gain, first_norm_offset
    )
    hidden_full = col_gather(hidden_state.astype(jnp.bfloat16))
    inner = row_reduce(product(hidden_full, inner_weight)) + inner_bias
    active = jax.nn.gelu(inner, approximate=False).astype(jnp.bfloat16)
    active_full = row_gather(active)
    outer_product = col_reduce(product(active_full, outer_weight)) + outer_bias
    closing_result, second_centred_rows, second_inverse_deviation = apply_norm(
        hidden_state + outer_product, second_norm_gain, second_norm_offset
    )
    layer_out = closing_result.astype(jnp.bfloat16)
    output_gradient = cotangent.astype(jnp.float32)
    second_gain_gradient = jnp.sum(output_gradient * second_centred_rows, 0)
    shift_two_grad = jnp.sum(output_gradient, 0)
    second_preact_grad = norm_backward_pass(
        output_gradient, second_centred_rows, second_inverse_deviation, second_norm_gain
    )
    dout_full = col_gather(second_preact_grad.astype(jnp.bfloat16))
    outer_bias_grad = jnp.sum(dout_full, 0, dtype=jnp.float32)
    outer_weight_grad = over_tokens(active_full, dout_full)
    dactive = row_reduce(against(dout_full, outer_weight))
    cdf = 0.5 * (1.0 + lax.erf(inner * inv_root_two))
    density = jnp.exp(-0.5 * inner * inner) * inv_root_two_pi
    dinner = (dactive * (cdf + inner * density)).astype(jnp.bfloat16)
    dinner_full = row_gather(dinner)
    inner_bias_grad = jnp.sum(dinner_full, 0, dtype=jnp.float32)
    inner_weight_grad = over_tokens(hidden_full, dinner_full)
    hidden_state_grad = second_preact_grad + col_reduce(against(dinner_full, inner_weight))
    first_gain_gradient = jnp.sum(hidden_state_grad * first_centred_rows, 0)
    shift_one_grad = jnp.sum(hidden_state_grad, 0)
    first_preact_grad = norm_backward_pass(
        hidden_state_grad, first_centred_rows, first_inverse_deviation, first_norm_gain
    )
    dattn_full = col_gather(first_preact_grad.astype(jnp.bfloat16))
    attn_out_bias_grad = jnp.sum(dattn_full, 0, dtype=jnp.float32)
    attn_out_weight_grad = over_tokens(mixed_full, dattn_full)
    dmixed = row_reduce(against(dattn_full, attn_out_weight)).astype(jnp.bfloat16)
    dq_heads, dk_heads, dv_heads = lax.map(
        attend_backward,
        (
            q_heads,
            k_heads,
            v_heads,
            segment_ids,
            dmixed.reshape(local_seqs, SEQ, head_local, HD),
            lse,
        ),
    )
    dq_rows = dq_heads.reshape(local_seqs * SEQ, col_width)
    dk_rows = dk_heads.reshape(local_seqs * SEQ, col_width)
    dv_rows = dv_heads.reshape(local_seqs * SEQ, col_width)
    dq_full, dk_full, dv_full = (
        lax.all_gather(dq_rows, "row", axis=0, tiled=True),
        lax.all_gather(dk_rows, "row", axis=0, tiled=True),
        lax.all_gather(dv_rows, "row", axis=0, tiled=True),
    )
    query_bias_grad = jnp.sum(dq_full, 0, dtype=jnp.float32)
    value_bias_grad = jnp.sum(dv_full, 0, dtype=jnp.float32)
    query_weight_grad = over_tokens(x_full, dq_full)
    key_weight_grad = over_tokens(x_full, dk_full)
    value_weight_grad = over_tokens(x_full, dv_full)
    dx_part = (
        against(dq_full, query_weight)
        + against(dk_full, key_weight)
        + against(dv_full, value_weight)
    )
    input_grad = (first_preact_grad + col_reduce(dx_part)).astype(jnp.bfloat16)
    summed = (
        lax.psum(query_weight_grad.astype(jnp.bfloat16), "dp").astype(jnp.float32),
        lax.psum(query_bias_grad.astype(jnp.bfloat16), "dp").astype(jnp.float32),
        lax.psum(key_weight_grad.astype(jnp.bfloat16), "dp").astype(jnp.float32),
        lax.psum(value_weight_grad.astype(jnp.bfloat16), "dp").astype(jnp.float32),
        lax.psum(value_bias_grad.astype(jnp.bfloat16), "dp").astype(jnp.float32),
        lax.psum(attn_out_weight_grad.astype(jnp.bfloat16), "dp").astype(jnp.float32),
        lax.psum(attn_out_bias_grad.astype(jnp.bfloat16), "dp").astype(jnp.float32),
        lax.psum(inner_weight_grad.astype(jnp.bfloat16), "dp").astype(jnp.float32),
        lax.psum(inner_bias_grad.astype(jnp.bfloat16), "dp").astype(jnp.float32),
        lax.psum(outer_weight_grad.astype(jnp.bfloat16), "dp").astype(jnp.float32),
        lax.psum(outer_bias_grad.astype(jnp.bfloat16), "dp").astype(jnp.float32),
    )
    norms = lax.psum(
        (first_gain_gradient, shift_one_grad, second_gain_gradient, shift_two_grad), ("dp", "col")
    )
    return (
        layer_out,
        input_grad,
        summed[0],
        summed[1],
        summed[2],
        summed[3],
        summed[4],
        summed[5],
        summed[6],
        norms[0],
        norms[1],
        summed[7],
        summed[8],
        summed[9],
        summed[10],
        norms[2],
        norms[3],
    )


IN_SPECS = (
    P(("dp", "col"), "row"),
    P(("dp", "row"), None),
    P("row", "col"),
    P("col"),
    P("row", "col"),
    P("row", "col"),
    P("col"),
    P("col", "row"),
    P("row"),
    P("row"),
    P("row"),
    P("row", "col"),
    P("col"),
    P("col", "row"),
    P("row"),
    P("row"),
    P("row"),
    P(("dp", "col"), "row"),
)
OUT_SPECS = (
    P(("dp", "col"), "row"),
    P(("dp", "col"), "row"),
    P("row", "col"),
    P("col"),
    P("row", "col"),
    P("row", "col"),
    P("col"),
    P("col", "row"),
    P("row"),
    P("row"),
    P("row"),
    P("row", "col"),
    P("col"),
    P("col", "row"),
    P("row"),
    P("row"),
    P("row"),
)


MESH = pl.DeviceIdType.MESH
LINE = 4
GROUPS = 4


class Spot:
    def __init__(self):
        self.dp = lax.axis_index("dp")
        self.row = lax.axis_index("row")
        self.col = lax.axis_index("col")
        k, r = self.dp, self.row
        self.dp_x = k + 1 - 2 * lax.rem(k, 2)
        self.dp_y = lax.rem(k + 2, 4)
        self.dp_d = 3 - k
        self.beside_x = (self.dp_x, r, self.col)
        self.beside_y = (self.dp_y, r, self.col)
        self.other_core = (k, r, 1 - self.col)
        self.inside = jnp.logical_and(r > 0, r < LINE - 1)
        first = jnp.where(r > 0, r - 1, 1)
        second = jnp.where(r == 0, 2, jnp.where(r == LINE - 1, 1, r + 1))
        third = jnp.where(r < 2, LINE - 1, 0)
        self.near = (first, second, third)

    def at_row(self, row):
        return (self.dp, row, self.col)


def remote(src, dst, send, recv, device):
    return pltpu.make_async_remote_copy(
        src_ref=src, dst_ref=dst, send_sem=send, recv_sem=recv, device_id=device, device_id_type=MESH
    )


def greet(spot):
    barrier = pltpu.get_barrier_semaphore()
    for away in range(LINE):
        row = lax.rem(spot.row + away, LINE)
        for core in range(2):
            if away == 0 and core == 0:
                continue
            col = lax.rem(spot.col + core, 2)
            pl.semaphore_signal(barrier, inc=1, device_id=(spot.dp, row, col), device_id_type=MESH)
    pl.semaphore_signal(barrier, inc=1, device_id=spot.beside_x, device_id_type=MESH)
    pl.semaphore_signal(barrier, inc=1, device_id=spot.beside_y, device_id_type=MESH)
    pl.semaphore_wait(barrier, 2 * LINE + 1)


class Gather:
    SEMS = (
        [pltpu.SemaphoreType.DMA((GROUPS, 2))]
        + [pltpu.SemaphoreType.DMA((GROUPS,))]
        + [pltpu.SemaphoreType.DMA((GROUPS, LINE))] * 12
    )

    def __init__(self, spot, shards, bufs, sems):
        self.spot, self.shards, self.bufs = spot, shards, bufs
        (self.own_s, self.own_l, self.zs, self.zr, self.xs, self.xr, self.ys, self.yr, self.fas, self.far, self.fbs, self.fbr, *_) = sems
        self.quarter = [s.shape[0] // 4 for s in shards]

    def piece(self, g, row, j, half=None):
        q = self.quarter[g]
        if half is None:
            return self.bufs[g].at[row, pl.ds(pl.multiple_of(j * q, q), q)]
        h = q // 2
        return self.bufs[g].at[row, pl.ds(pl.multiple_of(j * q + half * h, h), h)]

    def own_copy(self, g, up):
        s, q = self.spot, self.quarter[g]
        src = self.shards[g].at[pl.ds(pl.multiple_of(s.dp * q, q), q)]
        row = s.row + 1 if up else s.row - 1
        return remote(src, self.piece(g, s.row, s.dp), self.own_s.at[g, int(up)], self.zr.at[g, s.row], s.at_row(row))

    def local(self, g):
        return pltpu.make_async_copy(self.shards[g], self.bufs[g].at[self.spot.row], self.own_l.at[g])

    def start_own(self, g):
        s = self.spot

        @pl.when(s.row < LINE - 1)
        def _():
            self.own_copy(g, True).start()

        @pl.when(s.row > 0)
        def _():
            self.own_copy(g, False).start()

        self.local(g).start()

    def onward(self, g, n):
        s = self.spot
        row = s.near[n]
        p = self.piece(g, row, s.dp)
        to = jnp.where(row < s.row, s.row + 1, s.row - 1)
        return remote(p, p, self.zs.at[g, row], self.zr.at[g, row], s.at_row(to))

    def across(self, g, n):
        s = self.spot
        row = s.near[n]
        p = self.piece(g, row, s.dp)
        return (
            remote(p, p, self.xs.at[g, row], self.xr.at[g, row], s.beside_x),
            remote(p, p, self.ys.at[g, row], self.yr.at[g, row], s.beside_y),
        )

    def relays(self, g, n):
        s = self.spot
        row = s.near[n]
        a = self.piece(g, row, s.dp_y, 0)
        b = self.piece(g, row, s.dp_x, 1)
        return (
            remote(a, a, self.fas.at[g, row], self.far.at[g, row], s.beside_x),
            remote(b, b, self.fbs.at[g, row], self.fbr.at[g, row], s.beside_y),
        )

    def z_step(self, g, n):
        self.onward(g, n).wait_recv()

        @pl.when(self.spot.inside)
        def _():
            self.onward(g, n).start()

        for c in self.across(g, n):
            c.start()

    def xy_step(self, g, n):
        x, y = self.across(g, n)
        a, b = self.relays(g, n)
        s = self.spot
        row = s.near[n]
        px, py = self.piece(g, row, s.dp_x), self.piece(g, row, s.dp_y)
        remote(px, px, self.xs.at[g, row], self.xr.at[g, row], s.beside_x).wait_recv()
        b.start()
        remote(py, py, self.ys.at[g, row], self.yr.at[g, row], s.beside_y).wait_recv()
        a.start()

    def arrive(self, g, n):
        s = self.spot
        row = s.near[n]
        a, b = self.piece(g, row, s.dp_d, 0), self.piece(g, row, s.dp_d, 1)
        remote(a, a, self.fas.at[g, row], self.far.at[g, row], s.beside_x).wait_recv()
        remote(b, b, self.fbs.at[g, row], self.fbr.at[g, row], s.beside_y).wait_recv()

    def drain(self):
        s = self.spot
        for g in range(GROUPS):

            @pl.when(s.row < LINE - 1)
            def _():
                self.own_copy(g, True).wait_send()

            @pl.when(s.row > 0)
            def _():
                self.own_copy(g, False).wait_send()

            for n in range(LINE - 1):

                @pl.when(s.inside)
                def _():
                    self.onward(g, n).wait_send()

                for c in self.across(g, n) + self.relays(g, n):
                    c.wait_send()


class Tokens:
    SEMS = [pltpu.SemaphoreType.DMA((2,)), pltpu.SemaphoreType.DMA((LINE,))] + [pltpu.SemaphoreType.DMA((LINE,))] * 2 + [
        pltpu.SemaphoreType.DMA((2, 2)),
        pltpu.SemaphoreType.DMA((LINE,)),
        pltpu.SemaphoreType.DMA((LINE,)),
        pltpu.SemaphoreType.DMA((LINE,)),
    ]

    def __init__(self, spot, x, ct, par, xs, cts, pars, sems):
        self.spot = spot
        self.x, self.ct, self.par, self.xs, self.cts, self.pars = x, ct, par, xs, cts, pars
        (self.x_s, self.x_r, self.x_fs, self.x_fr, self.c_s, self.c_r, self.p_s, self.p_r) = sems
        self.seq = x.shape[0] // 2
        self.wide = x.shape[1]

    def cols(self, ref, row):
        return ref.at[:, pl.ds(pl.multiple_of(row * self.wide, self.wide), self.wide)]

    def each(self, i, do_remote, do_local, row, here):
        @pl.when(here)
        def _():
            do_local()

        @pl.when(jnp.logical_not(here))
        def _():
            do_remote()

    def x_copy(self, i, local):
        s = self.spot
        row = 2 * s.col + i
        src = self.x.at[pl.ds(i * self.seq, self.seq)]
        dst = self.cols(self.xs, s.row)
        if local:
            return pltpu.make_async_copy(src, dst, self.x_r.at[s.row])
        return remote(src, dst, self.x_s.at[i], self.x_r.at[s.row], s.at_row(row))

    def ct_copy(self, i, core, local):
        s = self.spot
        half = self.seq // 2
        row = 2 * s.col + i
        src = self.ct.at[pl.ds(i * self.seq + core * half, half)]
        dst = self.cols(self.cts, s.row)
        if local:
            return pltpu.make_async_copy(src, dst, self.c_r.at[s.row])
        return remote(src, dst, self.c_s.at[i, core], self.c_r.at[s.row], (s.dp, row, jnp.int32(core)))

    def par_copy(self, away):
        s = self.spot
        row = lax.rem(s.row + away, LINE)
        if away == 0:
            return pltpu.make_async_copy(self.par, self.pars.at[s.row], self.p_r.at[s.row])
        return remote(self.par, self.pars.at[s.row], self.p_s.at[away], self.p_r.at[s.row], s.at_row(row))

    def start_x(self):
        s = self.spot
        for i in range(2):
            here = 2 * s.col + i == s.row

            @pl.when(here)
            def _():
                self.x_copy(i, True).start()

            @pl.when(jnp.logical_not(here))
            def _():
                self.x_copy(i, False).start()

    def start_par(self):
        for away in range(LINE):
            self.par_copy(away).start()

    def start_ct(self):
        s = self.spot
        for i in range(2):
            for core in range(2):
                here = jnp.logical_and(2 * s.col + i == s.row, s.col == core)

                @pl.when(here)
                def _():
                    self.ct_copy(i, core, True).start()

                @pl.when(jnp.logical_not(here))
                def _():
                    self.ct_copy(i, core, False).start()

    def rows(self):
        return (self.spot.row,) + self.spot.near

    def relay(self, row):
        block = self.cols(self.xs, row)
        return remote(block, block, self.x_fs.at[row], self.x_fr.at[row], self.spot.other_core)

    def wait_x(self):
        s = self.spot
        first = s.row // 2 == s.col
        for row in self.rows():

            @pl.when(first)
            def _():
                block = self.cols(self.xs, row)
                pltpu.make_async_copy(block, block, self.x_r.at[row]).wait()
                self.relay(row).start()

        for row in self.rows():

            @pl.when(jnp.logical_not(first))
            def _():
                self.relay(row).wait_recv()

    def wait_ct(self):
        for row in self.rows():
            block = self.cols(self.cts, row)
            pltpu.make_async_copy(block, block, self.c_r.at[row]).wait()

    def wait_par(self):
        for row in self.rows():
            block = self.pars.at[row]
            pltpu.make_async_copy(block, block, self.p_r.at[row]).wait()

    def drain(self):
        s = self.spot
        for i in range(2):

            @pl.when(jnp.logical_not(2 * s.col + i == s.row))
            def _():
                self.x_copy(i, False).wait_send()

            for core in range(2):

                @pl.when(jnp.logical_not(jnp.logical_and(2 * s.col + i == s.row, s.col == core)))
                def _():
                    self.ct_copy(i, core, False).wait_send()

        for away in range(1, LINE):
            self.par_copy(away).wait_send()

        @pl.when(s.row // 2 == s.col)
        def _():
            for row in self.rows():
                self.relay(row).wait_send()


ROWS_AT_ONCE = {1536: 16, 2048: 16, 256: 64}


class Scatter:
    SEMS = [pltpu.SemaphoreType.DMA((GROUPS, LINE))] * 14 + [pltpu.SemaphoreType.DMA((GROUPS,))] * 10

    def __init__(self, spot, parts, rel_a, rel_b, from_x, from_y, line, final, sems):
        self.spot, self.parts, self.rel_a, self.rel_b = spot, parts, rel_a, rel_b
        self.from_x, self.from_y, self.line, self.final = from_x, from_y, line, final
        (
            self.ra_s, self.ra_r, self.rb_s, self.rb_r,
            self.xa_s, self.xa_r, self.xb_s, self.xb_r,
            self.ya_s, self.ya_r, self.yb_s, self.yb_r,
            self.z_s, self.z_r,
            self.above_r, self.fx_s, self.fx_r, self.fy_s, self.fy_r,
            self.ha_s, self.ha_r, self.hb_s, self.hb_r, self.spare,
        ) = sems
        self.quarter = [p.shape[1] // 4 for p in parts]
        self.order = (spot.near[2], spot.near[1], spot.near[0], spot.row)

    def part(self, g, row, j, half=None):
        q = self.quarter[g]
        if half is None:
            return self.parts[g].at[row, pl.ds(pl.multiple_of(j * q, q), q)]
        h = q // 2
        return self.parts[g].at[row, pl.ds(pl.multiple_of(j * q + half * h, h), h)]

    def half(self, ref, g, row, half):
        h = self.quarter[g] // 2
        return ref[g].at[row, pl.ds(half * h, h)]

    def send_a(self, g, t):
        s, row = self.spot, self.order[t]
        return remote(self.part(g, row, s.dp_d, 0), self.rel_a[g].at[row], self.ra_s.at[g, row], self.ra_r.at[g, row], s.beside_y)

    def send_b(self, g, t):
        s, row = self.spot, self.order[t]
        return remote(self.part(g, row, s.dp_d, 1), self.rel_b[g].at[row], self.rb_s.at[g, row], self.rb_r.at[g, row], s.beside_x)

    def send_xa(self, g, t):
        s, row = self.spot, self.order[t]
        return remote(self.part(g, row, s.dp_x, 0), self.half(self.from_x, g, row, 0), self.xa_s.at[g, row], self.xa_r.at[g, row], s.beside_x)

    def send_xb(self, g, t):
        s, row = self.spot, self.order[t]
        return remote(self.part(g, row, s.dp_x, 1), self.half(self.from_x, g, row, 1), self.xb_s.at[g, row], self.xb_r.at[g, row], s.beside_x)

    def send_ya(self, g, t):
        s, row = self.spot, self.order[t]
        return remote(self.part(g, row, s.dp_y, 0), self.half(self.from_y, g, row, 0), self.ya_s.at[g, row], self.ya_r.at[g, row], s.beside_y)

    def send_yb(self, g, t):
        s, row = self.spot, self.order[t]
        return remote(self.part(g, row, s.dp_y, 1), self.half(self.from_y, g, row, 1), self.yb_s.at[g, row], self.yb_r.at[g, row], s.beside_y)

    def add(self, g, rows, out, terms):
        wide = out.shape[-1]
        step = min(ROWS_AT_ONCE[wide], rows)

        def body(i, carry):
            at = pl.ds(pl.multiple_of(i * step, step), step)
            total = terms[0][at, :].astype(jnp.float32)
            for t in terms[1:]:
                total = total + t[at, :].astype(jnp.float32)
            out[at, :] = total.astype(jnp.bfloat16)
            return carry

        lax.fori_loop(0, rows // step, body, 0)

    def first(self, g, t):
        self.send_a(g, t).start()
        self.send_b(g, t).start()
        self.send_xb(g, t).start()
        self.send_ya(g, t).start()

    def second(self, g, t):
        s, row = self.spot, self.order[t]
        h = self.quarter[g] // 2
        self.send_a(g, t).wait_recv()
        mine = self.part(g, row, s.dp_x, 0)
        self.add(g, h, mine, (mine, self.rel_a[g].at[row]))
        self.send_xa(g, t).start()
        self.send_b(g, t).wait_recv()
        mine = self.part(g, row, s.dp_y, 1)
        self.add(g, h, mine, (mine, self.rel_b[g].at[row]))
        self.send_yb(g, t).start()

    def onward(self, g, t):
        s, row = self.spot, self.order[t]
        to = jnp.where(row > s.row, s.row + 1, s.row - 1)
        slot = jnp.where(row == s.row - 1, LINE, row)
        last = row == s.row - 1
        piece = self.part(g, row, s.dp)

        def copy(recv):
            return remote(piece, self.line[g].at[slot], self.z_s.at[g, row], recv, s.at_row(to))

        return last, copy(self.above_r.at[g]), copy(self.z_r.at[g, row])

    def third(self, g, t):
        s, row = self.spot, self.order[t]
        q = self.quarter[g]
        for c in (self.send_xa(g, t), self.send_xb(g, t), self.send_ya(g, t), self.send_yb(g, t)):
            c.wait_recv()
        mine = self.part(g, row, s.dp)
        terms = (mine, self.from_x[g].at[row], self.from_y[g].at[row])
        if t < LINE - 1:
            passed = jnp.logical_or(jnp.logical_and(row > s.row, s.row > 0), jnp.logical_and(row < s.row, s.row < LINE - 1))
            last, above, along = self.onward(g, t)

            @pl.when(passed)
            def _():
                along.wait_recv()
                self.add(g, q, mine, terms + (self.line[g].at[row],))

            @pl.when(jnp.logical_not(passed))
            def _():
                self.add(g, q, mine, terms)

            @pl.when(last)
            def _():
                above.start()

            @pl.when(jnp.logical_not(last))
            def _():
                along.start()
        else:
            below, over = self.line[g].at[s.row], self.line[g].at[LINE]
            whole = self.fin(g, s.dp)

            def wait_below():
                remote(below, below, self.z_s.at[g, s.row], self.z_r.at[g, s.row], s.beside_x).wait_recv()

            def wait_over():
                remote(over, over, self.z_s.at[g, s.row], self.above_r.at[g], s.beside_x).wait_recv()

            @pl.when(s.inside)
            def _():
                wait_below()
                wait_over()
                self.add(g, q, whole, terms + (below, over))

            @pl.when(s.row == 0)
            def _():
                wait_over()
                self.add(g, q, whole, terms + (over,))

            @pl.when(s.row == LINE - 1)
            def _():
                wait_below()
                self.add(g, q, whole, terms + (below,))

            for c in self.spread(g):
                c.start()

    def fin(self, g, j, half=None):
        q = self.quarter[g]
        if half is None:
            return self.final[g].at[pl.ds(pl.multiple_of(j * q, q), q)]
        h = q // 2
        return self.final[g].at[pl.ds(pl.multiple_of(j * q + half * h, h), h)]

    def spread(self, g):
        s = self.spot
        p = self.fin(g, s.dp)
        return (
            remote(p, p, self.fx_s.at[g], self.fx_r.at[g], s.beside_x),
            remote(p, p, self.fy_s.at[g], self.fy_r.at[g], s.beside_y),
        )

    def relays(self, g):
        s = self.spot
        a, b = self.fin(g, s.dp_y, 0), self.fin(g, s.dp_x, 1)
        return (
            remote(a, a, self.ha_s.at[g], self.ha_r.at[g], s.beside_x),
            remote(b, b, self.hb_s.at[g], self.hb_r.at[g], s.beside_y),
        )

    def fourth(self, g):
        s = self.spot
        px, py = self.fin(g, s.dp_x), self.fin(g, s.dp_y)
        a, b = self.relays(g)
        remote(px, px, self.fx_s.at[g], self.fx_r.at[g], s.beside_x).wait_recv()
        b.start()
        remote(py, py, self.fy_s.at[g], self.fy_r.at[g], s.beside_y).wait_recv()
        a.start()

    def fifth(self, g):
        s = self.spot
        a, b = self.fin(g, s.dp_d, 0), self.fin(g, s.dp_d, 1)
        remote(a, a, self.ha_s.at[g], self.ha_r.at[g], s.beside_x).wait_recv()
        remote(b, b, self.hb_s.at[g], self.hb_r.at[g], s.beside_y).wait_recv()

    def drain(self):
        for g in range(GROUPS):
            for t in range(LINE):
                for c in (
                    self.send_a(g, t), self.send_b(g, t), self.send_xa(g, t),
                    self.send_xb(g, t), self.send_ya(g, t), self.send_yb(g, t),
                ):
                    c.wait_send()
                if t < LINE - 1:
                    self.onward(g, t)[2].wait_send()
            for c in self.spread(g) + self.relays(g):
                c.wait_send()


class Spread:
    SEMS = [pltpu.SemaphoreType.DMA((LINE,)), pltpu.SemaphoreType.DMA((4,))]

    def __init__(self, spot, src, out, sems):
        self.spot, self.src, self.out = spot, src, out
        self.s, self.r = sems
        self.count, wide = src.shape
        self.cut = wide // LINE

    def slot(self, n):
        return self.out.at[pl.ds(pl.multiple_of(n * self.count, self.count), self.count)]

    def copy(self, away, local=False):
        s = self.spot
        row = lax.rem(s.row + away, LINE)
        src = self.src.at[:, pl.ds(pl.multiple_of(row * self.cut, self.cut), self.cut)]
        n = 2 * lax.rem(s.row, 2) + s.col
        if local:
            return pltpu.make_async_copy(src, self.slot(n), self.r.at[n])
        return remote(src, self.slot(n), self.s.at[away], self.r.at[n], (s.dp, row, s.row // 2))

    def start(self):
        s = self.spot
        here = s.row // 2 == s.col

        @pl.when(here)
        def _():
            self.copy(0, True).start()

        @pl.when(jnp.logical_not(here))
        def _():
            self.copy(0).start()

        for away in range(1, LINE):
            self.copy(away).start()

    def wait(self):
        s = self.spot
        for n in range(4):
            pltpu.make_async_copy(self.slot(n), self.slot(n), self.r.at[n]).wait()

        @pl.when(jnp.logical_not(s.row // 2 == s.col))
        def _():
            self.copy(0).wait_send()

        for away in range(1, LINE):
            self.copy(away).wait_send()


def gather_kernel(n_tok, n_gat, *refs):
    x, ct, par, *rest = refs
    shards, rest = rest[:GROUPS], rest[GROUPS:]
    xs, cts, pars, *rest = rest
    bufs, rest = rest[:GROUPS], rest[GROUPS:]
    tok_sems, gat_sems = rest[:n_tok], rest[n_tok:]
    spot = Spot()
    greet(spot)
    tokens = Tokens(spot, x, ct, par, xs, cts, pars, tok_sems)
    gather = Gather(spot, shards, bufs, gat_sems)
    gather.start_own(0)
    tokens.start_x()
    tokens.start_par()
    todo = [(g, n) for g in range(GROUPS) for n in range(LINE - 1)]
    for i, (g, n) in enumerate(todo):
        if n == 0 and g + 1 < GROUPS:
            gather.start_own(g + 1)
        gather.z_step(g, n)
        if i == 1:
            tokens.wait_x()
            tokens.start_ct()
        if i >= 2:
            gather.xy_step(*todo[i - 2])
    for u in todo[-2:]:
        gather.xy_step(*u)
    for u in todo:
        gather.arrive(*u)
    for g in range(GROUPS):
        gather.local(g).wait()
    tokens.wait_ct()
    tokens.wait_par()
    gather.drain()
    tokens.drain()


def gather_all(x, ct, par, shards):
    tokens, wide = x.shape
    seq = tokens // 2
    tok, gat = Tokens.SEMS, Gather.SEMS
    outs = [
        jax.ShapeDtypeStruct((seq, LINE * wide), x.dtype),
        jax.ShapeDtypeStruct((seq // 2, LINE * wide), x.dtype),
        jax.ShapeDtypeStruct((LINE,) + par.shape, par.dtype),
    ] + [jax.ShapeDtypeStruct((LINE,) + s.shape, s.dtype) for s in shards]
    anywhere = pl.BlockSpec(memory_space=pl.ANY)
    return pl.pallas_call(
        functools.partial(gather_kernel, len(tok), len(gat)),
        name="gather",
        out_shape=outs,
        in_specs=[anywhere] * (3 + GROUPS),
        out_specs=[anywhere] * len(outs),
        scratch_shapes=tok + gat,
        compiler_params=pltpu.CompilerParams(collective_id=0, has_side_effects=True),
    )(x, ct, par, *shards)


def scatter_kernel(n_sem, *refs):
    grads, out, dx, rest = refs[:GROUPS], refs[GROUPS], refs[GROUPS + 1], refs[GROUPS + 2 :]
    outs, placed_out, placed_dx, rest = rest[:GROUPS], rest[GROUPS], rest[GROUPS + 1], rest[GROUPS + 2 :]
    parts, rel_a, rel_b, from_x, from_y, line, final = (rest[i * GROUPS : (i + 1) * GROUPS] for i in range(7))
    sems = rest[7 * GROUPS : 7 * GROUPS + n_sem]
    load = rest[7 * GROUPS + n_sem]
    sems_out, sems_dx = rest[-4:-2], rest[-2:]
    spot = Spot()
    for g in range(GROUPS):
        pltpu.make_async_copy(grads[g], parts[g], load.at[g]).start()
    greet(spot)
    places = Spread(spot, out, placed_out, sems_out), Spread(spot, dx, placed_dx, sems_dx)
    scatter = Scatter(spot, parts, rel_a, rel_b, from_x, from_y, line, final, sems)
    todo = [(g, t) for g in range(GROUPS) for t in range(LINE)]
    count = len(todo)
    for p in places:
        p.start()
    for i in range(count + 6):
        if i < count:
            g, t = todo[i]
            if t == 0:
                pltpu.make_async_copy(grads[g], parts[g], load.at[g]).wait()
            scatter.first(g, t)
        if 0 <= i - 1 < count:
            scatter.second(*todo[i - 1])
        if 0 <= i - 3 < count:
            scatter.third(*todo[i - 3])
        if 0 <= i - 5 < count and todo[i - 5][1] == LINE - 1:
            scatter.fourth(todo[i - 5][0])
    for g in range(GROUPS):
        scatter.fifth(g)
        pltpu.make_async_copy(final[g], outs[g], load.at[g]).start()
    for g in range(GROUPS):
        pltpu.make_async_copy(final[g], outs[g], load.at[g]).wait()
    scatter.drain()
    for p in places:
        p.wait()


def scatter_scratch(shapes):
    def each(f):
        return [pltpu.VMEM(f(*s), jnp.bfloat16) for s in shapes]

    return (
        each(lambda n, r, c: (n, r, c))
        + each(lambda n, r, c: (n, r // 8, c)) * 2
        + each(lambda n, r, c: (n, r // 4, c)) * 2
        + each(lambda n, r, c: (n + 1, r // 4, c))
        + each(lambda n, r, c: (r, c))
    )


def scatter_all(grads, out, dx):
    placed = jax.ShapeDtypeStruct((4 * out.shape[0], out.shape[1] // LINE), out.dtype)
    anywhere = pl.BlockSpec(memory_space=pl.ANY)
    return pl.pallas_call(
        functools.partial(scatter_kernel, len(Scatter.SEMS)),
        name="scatter",
        out_shape=[jax.ShapeDtypeStruct(g.shape[1:], g.dtype) for g in grads] + [placed] * 2,
        in_specs=[anywhere] * (GROUPS + 2),
        out_specs=[anywhere] * (GROUPS + 2),
        scratch_shapes=scatter_scratch([g.shape for g in grads]) + Scatter.SEMS + [pltpu.SemaphoreType.DMA((GROUPS,))] + Spread.SEMS * 2,
        compiler_params=pltpu.CompilerParams(collective_id=1, has_side_effects=True, vmem_limit_bytes=60 * 2**20),
    )(*grads, out, dx)


def norm_whole(values, gain, offset):
    mean = jnp.mean(values, 1, keepdims=True)
    centred = values - mean
    inverse = lax.rsqrt(jnp.mean(centred * centred, 1, keepdims=True) + norm_eps)
    unit = centred * inverse
    return unit * gain + offset, unit, inverse


def norm_whole_back(grad, unit, inverse, gain):
    scaled = grad * gain
    return inverse * (scaled - jnp.mean(scaled, 1, keepdims=True) - unit * jnp.mean(scaled * unit, 1, keepdims=True))


def per_chip(
    hidden_in, segment_ids, query_weight, query_bias, key_weight, value_weight, value_bias, attn_out_weight,
    attn_out_bias, norm1_gain, first_norm_offset, inner_weight, inner_bias, outer_weight, outer_bias, norm2_gain,
    second_norm_offset, cotangent,
):
    f32, low = jnp.float32, jnp.bfloat16
    half = query_weight.shape[1]
    heads = half // HD
    row, col = lax.axis_index("row"), lax.axis_index("col")
    blocks = (attn_out_bias, norm1_gain, first_norm_offset, outer_bias, norm2_gain, second_norm_offset)
    par = jnp.zeros((16, MODEL_WIDTH // LINE), low).at[:6].set(jnp.stack(blocks))
    shards = (
        jnp.concatenate((query_weight, key_weight, value_weight), 1), attn_out_weight, inner_weight, outer_weight,
    )
    x, ct, pars, wqkv, wo, wi, wout = gather_all(hidden_in, cotangent, par, shards)
    bo, g1, b1, bout, g2, b2 = jnp.transpose(pars, (1, 0, 2)).reshape(16, MODEL_WIDTH)[:6].astype(f32)
    wqkv = wqkv.reshape(MODEL_WIDTH, 3 * half)
    wi = wi.reshape(MODEL_WIDTH, -1)
    qkv = product(x, wqkv)
    q = (qkv[:, :half] + query_bias).astype(low)
    k = qkv[:, half : 2 * half].astype(low)
    v = (qkv[:, 2 * half :] + value_bias).astype(low)
    qh, kh, vh = (t.reshape(SEQ, heads, HD) for t in (q, k, v))
    mixed, lse = attend_forward((qh, kh, vh, segment_ids[0]))
    mixed = mixed.reshape(SEQ, half)
    wo_n = jnp.transpose(wo, (1, 0, 2)).reshape(half, MODEL_WIDTH)
    wout_n = jnp.transpose(wout, (1, 0, 2)).reshape(-1, MODEL_WIDTH)
    attn = col_reduce(product(mixed, wo_n)) + bo
    x_own = lax.dynamic_slice_in_dim(x, col * (SEQ // 2), SEQ // 2, 0).astype(f32)
    h1, unit1, inv1 = norm_whole(x_own + attn, g1, b1)
    h1_low = col_gather(h1.astype(low))
    inner = product(h1_low, wi) + inner_bias
    cdf = 0.5 * (1.0 + lax.erf(inner * inv_root_two))
    act = (inner * cdf).astype(low)
    slope = cdf + inner * jnp.exp(-0.5 * inner * inner) * inv_root_two_pi
    outer = col_reduce(product(act, wout_n)) + bout
    out, unit2, inv2 = norm_whole(h1 + outer, g2, b2)
    dy = ct.astype(f32)
    g2_grad, b2_grad = jnp.sum(dy * unit2, 0), jnp.sum(dy, 0)
    dpre2 = norm_whole_back(dy, unit2, inv2, g2)
    dout2 = dpre2.astype(low)
    bout_grad = jnp.sum(dout2, 0, dtype=f32)
    dout2 = col_gather(dout2)
    wout_grad = over_tokens(act, dout2)
    dinner = (against(dout2, wout_n) * slope).astype(low)
    bi_grad = jnp.sum(dinner, 0, dtype=f32)
    wi_grad = over_tokens(h1_low, dinner)
    dh1 = dpre2 + col_reduce(against(dinner, wi))
    g1_grad, b1_grad = jnp.sum(dh1 * unit1, 0), jnp.sum(dh1, 0)
    dpre1 = norm_whole_back(dh1, unit1, inv1, g1)
    dattn = dpre1.astype(low)
    bo_grad = jnp.sum(dattn, 0, dtype=f32)
    dattn = col_gather(dattn)
    wo_grad = over_tokens(mixed, dattn)
    dmixed = against(dattn, wo_n).astype(low)
    dq, dk, dv = attend_backward((qh, kh, vh, segment_ids[0], dmixed.reshape(SEQ, heads, HD), lse))
    dq, dk, dv = (t.reshape(SEQ, half) for t in (dq, dk, dv))
    bq_grad, bv_grad = jnp.sum(dq, 0, dtype=f32), jnp.sum(dv, 0, dtype=f32)
    dqkv = jnp.concatenate((dq, dk, dv), 1)
    wqkv_grad = over_tokens(x, dqkv)
    dx = (dpre1 + col_reduce(against(dqkv, wqkv))).astype(low)

    def blocks_of(w):
        return jnp.transpose(w.reshape(-1, LINE, MODEL_WIDTH // LINE), (1, 0, 2)).astype(low)

    grads = (
        wqkv_grad.reshape(LINE, MODEL_WIDTH // LINE, -1).astype(low), blocks_of(wo_grad),
        wi_grad.reshape(LINE, MODEL_WIDTH // LINE, -1).astype(low), blocks_of(wout_grad),
    )
    order = (3, 2, 1, 0)
    *summed, layer_out, input_grad = scatter_all([grads[i] for i in order], out.astype(low), dx)
    summed = [summed[order.index(i)].astype(f32) for i in range(GROUPS)]
    rows_sum = lax.psum((bq_grad, bv_grad, bi_grad), ("dp", "row"))
    wide = lax.psum((bo_grad, g1_grad, b1_grad, bout_grad, g2_grad, b2_grad), ("dp", "row", "col"))
    cut = MODEL_WIDTH // LINE
    bo_g, g1_g, b1_g, bout_g, g2_g, b2_g = (lax.dynamic_slice_in_dim(w, row * cut, cut) for w in wide)

    wq_g, wk_g, wv_g = jnp.split(summed[0], 3, 1)
    return (
        layer_out, input_grad, wq_g, rows_sum[0], wk_g, wv_g, rows_sum[1], summed[1], bo_g, g1_g, b1_g,
        summed[2], rows_sum[2], summed[3], bout_g, g2_g, b2_g,
    )


def solution(mesh):
    def whole(*args):
        x, segments, wq = args[0], args[1], args[2]
        sizes = tuple(mesh.shape[a] for a in ("dp", "row", "col"))
        fits = sizes == (4, LINE, 2) and segments.shape == (16, SEQ) and wq.shape[0] == MODEL_WIDTH
        body = per_chip if fits else shards
        return jax.shard_map(body, mesh=mesh, in_specs=IN_SPECS, out_specs=OUT_SPECS, check_vma=False)(*args)

    return whole
```

```python
import functools

import jax
import jax.numpy as jnp
from jax import lax
from jax.experimental import pallas as pl
from jax.experimental.pallas import tpu as pltpu
from jax.sharding import PartitionSpec as P

MODEL_WIDTH = 1024
HD = 64
SEQ = 512


norm_eps = 1e-12
inv_root_two = 0.7071067811865476
inv_root_two_pi = 0.3989422804014327


def product(left, right):
    return jnp.dot(left, right, preferred_element_type=jnp.float32)


def over_tokens(left, right):
    return lax.dot_general(
        left, right, (((0,), (0,)), ((), ())), preferred_element_type=jnp.float32
    )


def against(left, right):
    return lax.dot_general(
        left, right, (((1,), (1,)), ((), ())), preferred_element_type=jnp.float32
    )


def col_gather(values):
    return lax.all_gather(values, "col", axis=0, tiled=True)


def row_gather(values):
    return lax.all_gather(values, "row", axis=0, tiled=True)


def row_reduce(values):
    return lax.psum_scatter(values, "row", scatter_dimension=0, tiled=True)


def col_reduce(values):
    return lax.psum_scatter(values, "col", scatter_dimension=0, tiled=True)


def row_sum_values(first_branch, second_branch):
    return lax.psum((first_branch, second_branch), "row")


def apply_norm(preact_input, norm_gain, norm_offset):
    total, squares = row_sum_values(
        jnp.sum(preact_input, 1), jnp.sum(preact_input * preact_input, 1)
    )
    row_mean = total / MODEL_WIDTH
    inverse_deviation = lax.rsqrt(squares / MODEL_WIDTH - row_mean * row_mean + norm_eps)
    centred_rows = (preact_input - row_mean[:, None]) * inverse_deviation[:, None]
    return (centred_rows * norm_gain + norm_offset, centred_rows, inverse_deviation)


def norm_backward_pass(incoming_gradient, centred_rows, inverse_deviation, norm_gain):
    scaled_rows = incoming_gradient * norm_gain
    first_branch, second_branch = row_sum_values(
        jnp.sum(scaled_rows, 1), jnp.sum(scaled_rows * centred_rows, 1)
    )
    return inverse_deviation[:, None] * (
        scaled_rows
        - first_branch[:, None] / MODEL_WIDTH
        - centred_rows * second_branch[:, None] / MODEL_WIDTH
    )


def seg_mask(segments):
    return (segments[:, None] == segments[None, :])[None]


def attend_forward(items):
    queries, keys, values, segments = items
    scores = jnp.einsum("qhd,khd->hqk", queries, keys, preferred_element_type=jnp.float32) * 0.125
    scores = jnp.where(seg_mask(segments), scores, -1e30)
    peak = jnp.max(scores, -1, keepdims=True)
    expo = jnp.exp(scores - peak)
    total = jnp.sum(expo, -1, keepdims=True)
    probs = (expo / total).astype(jnp.bfloat16)
    mixed = jnp.einsum("hqk,khd->qhd", probs, values, preferred_element_type=jnp.float32)
    return (mixed.astype(jnp.bfloat16), (peak + jnp.log(total))[..., 0])


def attend_backward(items):
    queries, keys, values, segments, dmixed, lse = items
    scores = jnp.einsum("qhd,khd->hqk", queries, keys, preferred_element_type=jnp.float32) * 0.125
    probs = jnp.where(seg_mask(segments), jnp.exp(scores - lse[..., None]), 0.0)
    dvalues = jnp.einsum(
        "hqk,qhd->khd", probs.astype(jnp.bfloat16), dmixed, preferred_element_type=jnp.float32
    )
    dprobs = jnp.einsum("qhd,khd->hqk", dmixed, values, preferred_element_type=jnp.float32)
    middle = jnp.sum(probs * dprobs, -1, keepdims=True)
    dscores = (probs * (dprobs - middle)).astype(jnp.bfloat16)
    dqueries = jnp.einsum("hqk,khd->qhd", dscores, keys, preferred_element_type=jnp.float32) * 0.125
    dkeys = jnp.einsum("hqk,qhd->khd", dscores, queries, preferred_element_type=jnp.float32) * 0.125
    return (dqueries.astype(jnp.bfloat16), dkeys.astype(jnp.bfloat16), dvalues.astype(jnp.bfloat16))


def shards(
    hidden_in,
    segment_ids,
    query_weight,
    query_bias,
    key_weight,
    value_weight,
    value_bias,
    attn_out_weight,
    attn_out_bias,
    norm1_gain,
    first_norm_offset,
    inner_weight,
    inner_bias,
    outer_weight,
    outer_bias,
    norm2_gain,
    second_norm_offset,
    cotangent,
):
    local_seqs = segment_ids.shape[0]
    col_width = query_weight.shape[1]
    head_local = col_width // HD
    first_norm_gain = norm1_gain.astype(jnp.float32)
    second_norm_gain = norm2_gain.astype(jnp.float32)
    x_full = col_gather(hidden_in)
    part_q, part_k, part_v = (
        lax.psum_scatter(product(x_full, query_weight), "row", scatter_dimension=0, tiled=True),
        lax.psum_scatter(product(x_full, key_weight), "row", scatter_dimension=0, tiled=True),
        lax.psum_scatter(product(x_full, value_weight), "row", scatter_dimension=0, tiled=True),
    )
    queries = (part_q + query_bias).astype(jnp.bfloat16)
    keys = part_k.astype(jnp.bfloat16)
    values = (part_v + value_bias).astype(jnp.bfloat16)
    q_heads = queries.reshape(local_seqs, SEQ, head_local, HD)
    k_heads = keys.reshape(local_seqs, SEQ, head_local, HD)
    v_heads = values.reshape(local_seqs, SEQ, head_local, HD)
    mixed, lse = lax.map(attend_forward, (q_heads, k_heads, v_heads, segment_ids))
    mixed = mixed.reshape(local_seqs * SEQ, col_width)
    mixed_full = row_gather(mixed)
    attn = col_reduce(product(mixed_full, attn_out_weight)) + attn_out_bias
    first_preact = hidden_in.astype(jnp.float32) + attn
    hidden_state, first_centred_rows, first_inverse_deviation = apply_norm(
        first_preact, first_norm_gain, first_norm_offset
    )
    hidden_full = col_gather(hidden_state.astype(jnp.bfloat16))
    inner = row_reduce(product(hidden_full, inner_weight)) + inner_bias
    active = jax.nn.gelu(inner, approximate=False).astype(jnp.bfloat16)
    active_full = row_gather(active)
    outer_product = col_reduce(product(active_full, outer_weight)) + outer_bias
    closing_result, second_centred_rows, second_inverse_deviation = apply_norm(
        hidden_state + outer_product, second_norm_gain, second_norm_offset
    )
    layer_out = closing_result.astype(jnp.bfloat16)
    output_gradient = cotangent.astype(jnp.float32)
    second_gain_gradient = jnp.sum(output_gradient * second_centred_rows, 0)
    shift_two_grad = jnp.sum(output_gradient, 0)
    second_preact_grad = norm_backward_pass(
        output_gradient, second_centred_rows, second_inverse_deviation, second_norm_gain
    )
    dout_full = col_gather(second_preact_grad.astype(jnp.bfloat16))
    outer_bias_grad = jnp.sum(dout_full, 0, dtype=jnp.float32)
    outer_weight_grad = over_tokens(active_full, dout_full)
    dactive = row_reduce(against(dout_full, outer_weight))
    cdf = 0.5 * (1.0 + lax.erf(inner * inv_root_two))
    density = jnp.exp(-0.5 * inner * inner) * inv_root_two_pi
    dinner = (dactive * (cdf + inner * density)).astype(jnp.bfloat16)
    dinner_full = row_gather(dinner)
    inner_bias_grad = jnp.sum(dinner_full, 0, dtype=jnp.float32)
    inner_weight_grad = over_tokens(hidden_full, dinner_full)
    hidden_state_grad = second_preact_grad + col_reduce(against(dinner_full, inner_weight))
    first_gain_gradient = jnp.sum(hidden_state_grad * first_centred_rows, 0)
    shift_one_grad = jnp.sum(hidden_state_grad, 0)
    first_preact_grad = norm_backward_pass(
        hidden_state_grad, first_centred_rows, first_inverse_deviation, first_norm_gain
    )
    dattn_full = col_gather(first_preact_grad.astype(jnp.bfloat16))
    attn_out_bias_grad = jnp.sum(dattn_full, 0, dtype=jnp.float32)
    attn_out_weight_grad = over_tokens(mixed_full, dattn_full)
    dmixed = row_reduce(against(dattn_full, attn_out_weight)).astype(jnp.bfloat16)
    dq_heads, dk_heads, dv_heads = lax.map(
        attend_backward,
        (
            q_heads,
            k_heads,
            v_heads,
            segment_ids,
            dmixed.reshape(local_seqs, SEQ, head_local, HD),
            lse,
        ),
    )
    dq_rows = dq_heads.reshape(local_seqs * SEQ, col_width)
    dk_rows = dk_heads.reshape(local_seqs * SEQ, col_width)
    dv_rows = dv_heads.reshape(local_seqs * SEQ, col_width)
    dq_full, dk_full, dv_full = (
        lax.all_gather(dq_rows, "row", axis=0, tiled=True),
        lax.all_gather(dk_rows, "row", axis=0, tiled=True),
        lax.all_gather(dv_rows, "row", axis=0, tiled=True),
    )
    query_bias_grad = jnp.sum(dq_full, 0, dtype=jnp.float32)
    value_bias_grad = jnp.sum(dv_full, 0, dtype=jnp.float32)
    query_weight_grad = over_tokens(x_full, dq_full)
    key_weight_grad = over_tokens(x_full, dk_full)
    value_weight_grad = over_tokens(x_full, dv_full)
    dx_part = (
        against(dq_full, query_weight)
        + against(dk_full, key_weight)
        + against(dv_full, value_weight)
    )
    input_grad = (first_preact_grad + col_reduce(dx_part)).astype(jnp.bfloat16)
    summed = (
        lax.psum(query_weight_grad.astype(jnp.bfloat16), "dp").astype(jnp.float32),
        lax.psum(query_bias_grad.astype(jnp.bfloat16), "dp").astype(jnp.float32),
        lax.psum(key_weight_grad.astype(jnp.bfloat16), "dp").astype(jnp.float32),
        lax.psum(value_weight_grad.astype(jnp.bfloat16), "dp").astype(jnp.float32),
        lax.psum(value_bias_grad.astype(jnp.bfloat16), "dp").astype(jnp.float32),
        lax.psum(attn_out_weight_grad.astype(jnp.bfloat16), "dp").astype(jnp.float32),
        lax.psum(attn_out_bias_grad.astype(jnp.bfloat16), "dp").astype(jnp.float32),
        lax.psum(inner_weight_grad.astype(jnp.bfloat16), "dp").astype(jnp.float32),
        lax.psum(inner_bias_grad.astype(jnp.bfloat16), "dp").astype(jnp.float32),
        lax.psum(outer_weight_grad.astype(jnp.bfloat16), "dp").astype(jnp.float32),
        lax.psum(outer_bias_grad.astype(jnp.bfloat16), "dp").astype(jnp.float32),
    )
    norms = lax.psum(
        (first_gain_gradient, shift_one_grad, second_gain_gradient, shift_two_grad), ("dp", "col")
    )
    return (
        layer_out,
        input_grad,
        summed[0],
        summed[1],
        summed[2],
        summed[3],
        summed[4],
        summed[5],
        summed[6],
        norms[0],
        norms[1],
        summed[7],
        summed[8],
        summed[9],
        summed[10],
        norms[2],
        norms[3],
    )


IN_SPECS = (
    P(("dp", "col"), "row"),
    P(("dp", "row"), None),
    P("row", "col"),
    P("col"),
    P("row", "col"),
    P("row", "col"),
    P("col"),
    P("col", "row"),
    P("row"),
    P("row"),
    P("row"),
    P("row", "col"),
    P("col"),
    P("col", "row"),
    P("row"),
    P("row"),
    P("row"),
    P(("dp", "col"), "row"),
)
OUT_SPECS = (
    P(("dp", "col"), "row"),
    P(("dp", "col"), "row"),
    P("row", "col"),
    P("col"),
    P("row", "col"),
    P("row", "col"),
    P("col"),
    P("col", "row"),
    P("row"),
    P("row"),
    P("row"),
    P("row", "col"),
    P("col"),
    P("col", "row"),
    P("row"),
    P("row"),
    P("row"),
)


MESH = pl.DeviceIdType.MESH
LINE = 4
GROUPS = 4


class Spot:
    def __init__(self):
        self.dp = lax.axis_index("dp")
        self.row = lax.axis_index("row")
        self.col = lax.axis_index("col")
        k, r = self.dp, self.row
        self.dp_x = k + 1 - 2 * lax.rem(k, 2)
        self.dp_y = lax.rem(k + 2, 4)
        self.dp_d = 3 - k
        self.beside_x = (self.dp_x, r, self.col)
        self.beside_y = (self.dp_y, r, self.col)
        self.other_core = (k, r, 1 - self.col)
        self.inside = jnp.logical_and(r > 0, r < LINE - 1)
        first = jnp.where(r > 0, r - 1, 1)
        second = jnp.where(r == 0, 2, jnp.where(r == LINE - 1, 1, r + 1))
        third = jnp.where(r < 2, LINE - 1, 0)
        self.near = (first, second, third)

    def at_row(self, row):
        return (self.dp, row, self.col)


def remote(src, dst, send, recv, device):
    return pltpu.make_async_remote_copy(
        src_ref=src, dst_ref=dst, send_sem=send, recv_sem=recv, device_id=device, device_id_type=MESH
    )


def greet(spot):
    barrier = pltpu.get_barrier_semaphore()
    for away in range(LINE):
        row = lax.rem(spot.row + away, LINE)
        for core in range(2):
            if away == 0 and core == 0:
                continue
            col = lax.rem(spot.col + core, 2)
            pl.semaphore_signal(barrier, inc=1, device_id=(spot.dp, row, col), device_id_type=MESH)
    pl.semaphore_signal(barrier, inc=1, device_id=spot.beside_x, device_id_type=MESH)
    pl.semaphore_signal(barrier, inc=1, device_id=spot.beside_y, device_id_type=MESH)
    pl.semaphore_wait(barrier, 2 * LINE + 1)


class Gather:
    SEMS = (
        [pltpu.SemaphoreType.DMA((GROUPS, 2))]
        + [pltpu.SemaphoreType.DMA((GROUPS, 3))]
        + [pltpu.SemaphoreType.DMA((GROUPS, LINE))] * 10
    )

    def __init__(self, spot, shards, bufs, sems):
        self.spot, self.shards, self.bufs = spot, shards, bufs
        (self.own_s, self.own_l, self.zs, self.zr, self.xs, self.xr, self.ys, self.yr, self.fas, self.far, self.fbs, self.fbr) = sems
        self.quarter = [b.shape[1] // 4 for b in bufs]

    def piece(self, g, row, j, half=None):
        q = self.quarter[g]
        if half is None:
            return self.bufs[g].at[row, pl.ds(pl.multiple_of(j * q, q), q)]
        h = q // 2
        return self.bufs[g].at[row, pl.ds(pl.multiple_of(j * q + half * h, h), h)]

    def own_copy(self, g, up):
        s = self.spot
        piece = self.piece(g, s.row, s.dp)
        row = s.row + 1 if up else s.row - 1
        return remote(piece, piece, self.own_s.at[g, int(up)], self.zr.at[g, s.row], s.at_row(row))

    def local(self, g):
        mine = self.bufs[g].at[self.spot.row]
        wide = self.shards[g][0].shape[1]
        return [
            pltpu.make_async_copy(part, mine.at[:, pl.ds(i * wide, wide)], self.own_l.at[g, i])
            for i, part in enumerate(self.shards[g])
        ]

    def load(self):
        for g in range(GROUPS):
            for c in self.local(g):
                c.start()

    def start_own(self, g):
        s = self.spot
        for c in self.local(g):
            c.wait()

        @pl.when(s.row < LINE - 1)
        def _():
            self.own_copy(g, True).start()

        @pl.when(s.row > 0)
        def _():
            self.own_copy(g, False).start()

    def onward(self, g, n):
        s = self.spot
        row = s.near[n]
        p = self.piece(g, row, s.dp)
        to = jnp.where(row < s.row, s.row + 1, s.row - 1)
        return remote(p, p, self.zs.at[g, row], self.zr.at[g, row], s.at_row(to))

    def across(self, g, n):
        s = self.spot
        row = s.near[n]
        p = self.piece(g, row, s.dp)
        return (
            remote(p, p, self.xs.at[g, row], self.xr.at[g, row], s.beside_x),
            remote(p, p, self.ys.at[g, row], self.yr.at[g, row], s.beside_y),
        )

    def relays(self, g, n):
        s = self.spot
        row = s.near[n]
        a = self.piece(g, row, s.dp_y, 0)
        b = self.piece(g, row, s.dp_x, 1)
        return (
            remote(a, a, self.fas.at[g, row], self.far.at[g, row], s.beside_x),
            remote(b, b, self.fbs.at[g, row], self.fbr.at[g, row], s.beside_y),
        )

    def z_step(self, g, n):
        self.onward(g, n).wait_recv()

        @pl.when(self.spot.inside)
        def _():
            self.onward(g, n).start()

        for c in self.across(g, n):
            c.start()

    def xy_step(self, g, n):
        a, b = self.relays(g, n)
        s = self.spot
        row = s.near[n]
        px, py = self.piece(g, row, s.dp_x), self.piece(g, row, s.dp_y)
        remote(px, px, self.xs.at[g, row], self.xr.at[g, row], s.beside_x).wait_recv()
        b.start()
        remote(py, py, self.ys.at[g, row], self.yr.at[g, row], s.beside_y).wait_recv()
        a.start()

    def arrive(self, g, n):
        s = self.spot
        row = s.near[n]
        a, b = self.piece(g, row, s.dp_d, 0), self.piece(g, row, s.dp_d, 1)
        remote(a, a, self.fas.at[g, row], self.far.at[g, row], s.beside_x).wait_recv()
        remote(b, b, self.fbs.at[g, row], self.fbr.at[g, row], s.beside_y).wait_recv()

    def drain(self):
        s = self.spot
        for g in range(GROUPS):

            @pl.when(s.row < LINE - 1)
            def _():
                self.own_copy(g, True).wait_send()

            @pl.when(s.row > 0)
            def _():
                self.own_copy(g, False).wait_send()

            for n in range(LINE - 1):

                @pl.when(s.inside)
                def _():
                    self.onward(g, n).wait_send()

                for c in self.across(g, n) + self.relays(g, n):
                    c.wait_send()


class Tokens:
    SEMS = [pltpu.SemaphoreType.DMA((2,)), pltpu.SemaphoreType.DMA((LINE,))] + [pltpu.SemaphoreType.DMA((LINE,))] * 2 + [
        pltpu.SemaphoreType.DMA((2, 2)),
        pltpu.SemaphoreType.DMA((LINE,)),
        pltpu.SemaphoreType.DMA((LINE,)),
        pltpu.SemaphoreType.DMA((LINE,)),
    ]

    def __init__(self, spot, x, ct, xs, cts, pars, sems):
        self.spot = spot
        self.x, self.ct, self.xs, self.cts, self.pars = x, ct, xs, cts, pars
        (self.x_s, self.x_r, self.x_fs, self.x_fr, self.c_s, self.c_r, self.p_s, self.p_r) = sems
        self.seq = x.shape[0] // 2
        self.wide = x.shape[1]

    def cols(self, ref, row):
        return ref.at[:, pl.ds(pl.multiple_of(row * self.wide, self.wide), self.wide)]

    def x_copy(self, i, local):
        s = self.spot
        row = 2 * s.col + i
        src = self.x.at[pl.ds(i * self.seq, self.seq)]
        dst = self.cols(self.xs, s.row)
        if local:
            return pltpu.make_async_copy(src, dst, self.x_r.at[s.row])
        return remote(src, dst, self.x_s.at[i], self.x_r.at[s.row], s.at_row(row))

    def ct_copy(self, i, core, local):
        s = self.spot
        half = self.seq // 2
        row = 2 * s.col + i
        src = self.ct.at[pl.ds(i * self.seq + core * half, half)]
        dst = self.cols(self.cts, s.row)
        if local:
            return pltpu.make_async_copy(src, dst, self.c_r.at[s.row])
        return remote(src, dst, self.c_s.at[i, core], self.c_r.at[s.row], (s.dp, row, jnp.int32(core)))

    def par_copy(self, away):
        s = self.spot
        row = lax.rem(s.row + away, LINE)
        mine = self.pars.at[s.row]
        return remote(mine, mine, self.p_s.at[away], self.p_r.at[s.row], s.at_row(row))

    def start_x(self):
        s = self.spot
        for i in range(2):
            here = 2 * s.col + i == s.row

            @pl.when(here)
            def _():
                self.x_copy(i, True).start()

            @pl.when(jnp.logical_not(here))
            def _():
                self.x_copy(i, False).start()

    def start_par(self):
        for away in range(1, LINE):
            self.par_copy(away).start()

    def start_ct(self):
        s = self.spot
        for i in range(2):
            for core in range(2):
                here = jnp.logical_and(2 * s.col + i == s.row, s.col == core)

                @pl.when(here)
                def _():
                    self.ct_copy(i, core, True).start()

                @pl.when(jnp.logical_not(here))
                def _():
                    self.ct_copy(i, core, False).start()

    def rows(self):
        return (self.spot.row,) + self.spot.near

    def relay(self, row):
        block = self.cols(self.xs, row)
        return remote(block, block, self.x_fs.at[row], self.x_fr.at[row], self.spot.other_core)

    def wait_x(self):
        s = self.spot
        first = s.row // 2 == s.col
        for row in self.rows():

            @pl.when(first)
            def _():
                block = self.cols(self.xs, row)
                pltpu.make_async_copy(block, block, self.x_r.at[row]).wait()
                self.relay(row).start()

        for row in self.rows():

            @pl.when(jnp.logical_not(first))
            def _():
                self.relay(row).wait_recv()

    def wait_ct(self):
        for row in self.rows():
            block = self.cols(self.cts, row)
            pltpu.make_async_copy(block, block, self.c_r.at[row]).wait()

    def wait_par(self):
        for row in self.spot.near:
            block = self.pars.at[row]
            pltpu.make_async_copy(block, block, self.p_r.at[row]).wait()

    def drain(self):
        s = self.spot
        for i in range(2):

            @pl.when(jnp.logical_not(2 * s.col + i == s.row))
            def _():
                self.x_copy(i, False).wait_send()

            for core in range(2):

                @pl.when(jnp.logical_not(jnp.logical_and(2 * s.col + i == s.row, s.col == core)))
                def _():
                    self.ct_copy(i, core, False).wait_send()

        for away in range(1, LINE):
            self.par_copy(away).wait_send()

        @pl.when(s.row // 2 == s.col)
        def _():
            for row in self.rows():
                self.relay(row).wait_send()


ROWS_AT_ONCE = {1536: 16, 2048: 16, 256: 64}


class Scatter:
    SEMS = [pltpu.SemaphoreType.DMA((GROUPS, LINE))] * 14 + [pltpu.SemaphoreType.DMA((GROUPS,))] * 10

    def __init__(self, spot, parts, rel_a, rel_b, from_x, from_y, line, stage, final, sems):
        self.spot, self.parts, self.rel_a, self.rel_b = spot, parts, rel_a, rel_b
        self.from_x, self.from_y, self.line, self.stage, self.final = from_x, from_y, line, stage, final
        (
            self.ra_s, self.ra_r, self.rb_s, self.rb_r,
            self.xa_s, self.xa_r, self.xb_s, self.xb_r,
            self.ya_s, self.ya_r, self.yb_s, self.yb_r,
            self.z_s, self.z_r,
            self.above_r, self.fx_s, self.fx_r, self.fy_s, self.fy_r,
            self.ha_s, self.ha_r, self.hb_s, self.hb_r, self.own_s,
        ) = sems
        self.quarter = [p.shape[1] // 4 for p in parts]
        self.order = (spot.near[2], spot.near[1], spot.near[0], spot.row)

    def part(self, g, row, j, half=None):
        q = self.quarter[g]
        if half is None:
            return self.parts[g].at[row, pl.ds(pl.multiple_of(j * q, q), q)]
        h = q // 2
        return self.parts[g].at[row, pl.ds(pl.multiple_of(j * q + half * h, h), h)]

    def half(self, ref, g, row, half):
        h = self.quarter[g] // 2
        return ref[g].at[row, pl.ds(half * h, h)]

    def send_a(self, g, t):
        s, row = self.spot, self.order[t]
        return remote(self.part(g, row, s.dp_d, 0), self.rel_a[g].at[row], self.ra_s.at[g, row], self.ra_r.at[g, row], s.beside_y)

    def send_b(self, g, t):
        s, row = self.spot, self.order[t]
        return remote(self.part(g, row, s.dp_d, 1), self.rel_b[g].at[row], self.rb_s.at[g, row], self.rb_r.at[g, row], s.beside_x)

    def send_xa(self, g, t):
        s, row = self.spot, self.order[t]
        return remote(self.part(g, row, s.dp_x, 0), self.half(self.from_x, g, row, 0), self.xa_s.at[g, row], self.xa_r.at[g, row], s.beside_x)

    def send_xb(self, g, t):
        s, row = self.spot, self.order[t]
        return remote(self.part(g, row, s.dp_x, 1), self.half(self.from_x, g, row, 1), self.xb_s.at[g, row], self.xb_r.at[g, row], s.beside_x)

    def send_ya(self, g, t):
        s, row = self.spot, self.order[t]
        return remote(self.part(g, row, s.dp_y, 0), self.half(self.from_y, g, row, 0), self.ya_s.at[g, row], self.ya_r.at[g, row], s.beside_y)

    def send_yb(self, g, t):
        s, row = self.spot, self.order[t]
        return remote(self.part(g, row, s.dp_y, 1), self.half(self.from_y, g, row, 1), self.yb_s.at[g, row], self.yb_r.at[g, row], s.beside_y)

    def add(self, g, rows, out, terms):
        wide = out.shape[-1]
        step = min(ROWS_AT_ONCE[wide], rows)

        def body(i, carry):
            at = pl.ds(pl.multiple_of(i * step, step), step)
            total = terms[0][at, :].astype(jnp.float32)
            for t in terms[1:]:
                total = total + t[at, :].astype(jnp.float32)
            out[at, :] = total.astype(jnp.bfloat16)
            return carry

        lax.fori_loop(0, rows // step, body, 0)

    def first(self, g, t):
        self.send_a(g, t).start()
        self.send_b(g, t).start()

    def direct(self, g, t):
        self.send_xb(g, t).start()
        self.send_ya(g, t).start()

    def second(self, g, t):
        s, row = self.spot, self.order[t]
        h = self.quarter[g] // 2
        self.send_a(g, t).wait_recv()
        mine = self.part(g, row, s.dp_x, 0)
        self.add(g, h, mine, (mine, self.rel_a[g].at[row]))
        self.send_xa(g, t).start()
        self.send_b(g, t).wait_recv()
        mine = self.part(g, row, s.dp_y, 1)
        self.add(g, h, mine, (mine, self.rel_b[g].at[row]))
        self.send_yb(g, t).start()

    def onward(self, g, t, above=False):
        s, row = self.spot, self.order[t]
        to = jnp.where(row > s.row, s.row + 1, s.row - 1)
        slot = jnp.where(row == s.row - 1, LINE, row)
        piece = self.part(g, row, s.dp)
        recv = self.above_r.at[g] if above else self.z_r.at[g, row]
        return remote(piece, self.line[g].at[slot], self.z_s.at[g, row], recv, s.at_row(to))

    def third(self, g, t):
        s, row = self.spot, self.order[t]
        q = self.quarter[g]
        for c in (self.send_xa(g, t), self.send_xb(g, t), self.send_ya(g, t), self.send_yb(g, t)):
            c.wait_recv()
        mine = self.part(g, row, s.dp)
        terms = (mine, self.from_x[g].at[row], self.from_y[g].at[row])
        if t < LINE - 1:
            passed = jnp.logical_or(jnp.logical_and(row > s.row, s.row > 0), jnp.logical_and(row < s.row, s.row < LINE - 1))
            last = row == s.row - 1

            @pl.when(passed)
            def _():
                self.onward(g, t).wait_recv()
                self.add(g, q, mine, terms + (self.line[g].at[row],))

            @pl.when(jnp.logical_not(passed))
            def _():
                self.add(g, q, mine, terms)

            @pl.when(last)
            def _():
                self.onward(g, t, True).start()

            @pl.when(jnp.logical_not(last))
            def _():
                self.onward(g, t).start()
        else:
            below, over = self.line[g].at[s.row], self.line[g].at[LINE]
            whole = self.stage[g]

            def wait_below():
                remote(below, below, self.z_s.at[g, s.row], self.z_r.at[g, s.row], s.beside_x).wait_recv()

            def wait_over():
                remote(over, over, self.z_s.at[g, s.row], self.above_r.at[g], s.beside_x).wait_recv()

            @pl.when(s.inside)
            def _():
                wait_below()
                wait_over()
                self.add(g, q, whole, terms + (below, over))

            @pl.when(s.row == 0)
            def _():
                wait_over()
                self.add(g, q, whole, terms + (over,))

            @pl.when(s.row == LINE - 1)
            def _():
                wait_below()
                self.add(g, q, whole, terms + (below,))

            for c in self.spread(g):
                c.start()
            self.settle(g).start()

    def fin(self, g, j, half=None):
        q = self.quarter[g]
        if half is None:
            return self.final[g].at[pl.ds(pl.multiple_of(j * q, q), q)]
        h = q // 2
        return self.final[g].at[pl.ds(pl.multiple_of(j * q + half * h, h), h)]

    def spread(self, g):
        s = self.spot
        p = self.fin(g, s.dp)
        mine = self.stage[g]
        return (
            remote(mine, p, self.fx_s.at[g], self.fx_r.at[g], s.beside_x),
            remote(mine, p, self.fy_s.at[g], self.fy_r.at[g], s.beside_y),
        )

    def settle(self, g):
        return pltpu.make_async_copy(self.stage[g], self.fin(g, self.spot.dp), self.own_s.at[g])

    def relays(self, g):
        s = self.spot
        a, b = self.fin(g, s.dp_y, 0), self.fin(g, s.dp_x, 1)
        return (
            remote(a, a, self.ha_s.at[g], self.ha_r.at[g], s.beside_x),
            remote(b, b, self.hb_s.at[g], self.hb_r.at[g], s.beside_y),
        )

    def fourth(self, g):
        s = self.spot
        px, py = self.fin(g, s.dp_x), self.fin(g, s.dp_y)
        a, b = self.relays(g)
        remote(px, px, self.fx_s.at[g], self.fx_r.at[g], s.beside_x).wait_recv()
        b.start()
        remote(py, py, self.fy_s.at[g], self.fy_r.at[g], s.beside_y).wait_recv()
        a.start()

    def fifth(self, g):
        s = self.spot
        a, b = self.fin(g, s.dp_d, 0), self.fin(g, s.dp_d, 1)
        remote(a, a, self.ha_s.at[g], self.ha_r.at[g], s.beside_x).wait_recv()
        remote(b, b, self.hb_s.at[g], self.hb_r.at[g], s.beside_y).wait_recv()

    def drain(self):
        for g in range(GROUPS):
            for t in range(LINE):
                for c in (
                    self.send_a(g, t), self.send_b(g, t), self.send_xa(g, t),
                    self.send_xb(g, t), self.send_ya(g, t), self.send_yb(g, t),
                ):
                    c.wait_send()
                if t < LINE - 1:
                    self.onward(g, t).wait_send()
            for c in self.spread(g) + self.relays(g):
                c.wait_send()
            self.settle(g).wait()


class Spread:
    SEMS = [pltpu.SemaphoreType.DMA((LINE,)), pltpu.SemaphoreType.DMA((4,))]

    def __init__(self, spot, src, out, sems):
        self.spot, self.src, self.out = spot, src, out
        self.s, self.r = sems
        self.count, wide = src.shape
        self.cut = wide // LINE

    def slot(self, n):
        return self.out.at[pl.ds(pl.multiple_of(n * self.count, self.count), self.count)]

    def copy(self, away, local=False):
        s = self.spot
        row = lax.rem(s.row + away, LINE)
        src = self.src.at[:, pl.ds(pl.multiple_of(row * self.cut, self.cut), self.cut)]
        n = 2 * lax.rem(s.row, 2) + s.col
        if local:
            return pltpu.make_async_copy(src, self.slot(n), self.r.at[n])
        return remote(src, self.slot(n), self.s.at[away], self.r.at[n], (s.dp, row, s.row // 2))

    def start(self):
        s = self.spot
        here = s.row // 2 == s.col

        @pl.when(here)
        def _():
            self.copy(0, True).start()

        @pl.when(jnp.logical_not(here))
        def _():
            self.copy(0).start()

        for away in range(1, LINE):
            self.copy(away).start()

    def wait(self):
        s = self.spot
        for n in range(4):
            pltpu.make_async_copy(self.slot(n), self.slot(n), self.r.at[n]).wait()

        @pl.when(jnp.logical_not(s.row // 2 == s.col))
        def _():
            self.copy(0).wait_send()

        for away in range(1, LINE):
            self.copy(away).wait_send()


F32, LOW = jnp.float32, jnp.bfloat16
ANYWHERE = pl.BlockSpec(memory_space=pl.ANY)
IN_VMEM = pl.BlockSpec(memory_space=pltpu.VMEM)
LANES = 128
BLOCK = 32


def at(start, size):
    return pl.ds(pl.multiple_of(start * size, size), size)


def dot(a, b):
    return jnp.dot(a, b, preferred_element_type=F32)


def dot_t(a, b):
    return lax.dot_general(a, b, (((1,), (1,)), ((), ())), preferred_element_type=F32)


def loop(count, body):
    def step(i, carry):
        body(i)
        return carry

    lax.fori_loop(0, count, step, 0)


def head_lanes(half, dtype):
    lane = lax.broadcasted_iota(jnp.int32, (1, LANES), 1)
    return jnp.where((lane < HD) == (half == 0), 1.0, 0.0).astype(dtype)


def fold(values):
    return jnp.sum(values.reshape(values.shape[0] // 8, 8, values.shape[1]), 0)


def forward_kernel(*refs):
    it = iter(refs)

    def take(n):
        return [next(it) for _ in range(n)]

    x, ct, wq, wk, wv, wo_s, wi_s, wout_s = take(8)
    seg, bq, bv, bi = take(4)
    small = take(6)
    out_w = take(GROUPS)
    o_xt, o_qkv, o_probs, o_mixed_t, o_unit, o_inv, o_h_t, o_slope, o_act_t, o_dpre, o_dout, o_pars, o_out, o_sums = take(14)
    bufs = take(GROUPS)
    xs, cts, pars4, pars, qkv, qkv_bias, probs, mask, mixed, part, recv1, recv2 = take(12)
    unit, inv, h1, h_low, inner, slope, act, act_t, h_t, x_t, mixed_t, dpre, dout, out, sums = take(15)
    tok_sems, gat_sems = take(len(Tokens.SEMS)), take(len(Gather.SEMS))
    core_s, core_r, save = take(3)

    spot = Spot()
    gather = Gather(spot, ((wq, wk, wv), (wo_s,), (wi_s,), (wout_s,)), bufs, gat_sems)
    tokens = Tokens(spot, x, ct, xs, cts, pars4, tok_sems)
    wqkv, wo, wi, wout = bufs
    seq, width = xs.shape
    own = seq // 2
    half = qkv.shape[1] // 3
    mine, theirs = spot.col * own, (1 - spot.col) * own

    def rows_of(base, start, size):
        return pl.ds(pl.multiple_of(base + start * size, size), size)

    gather.load()
    pars4[spot.row] = jnp.zeros(pars4.shape[1:], F32)
    for i, p in enumerate(small):
        pars4[spot.row, pl.ds(i, 1), :] = p[...].astype(F32).reshape(1, -1)
    greet(spot)

    saves = []

    def keep(src, dst):
        c = pltpu.make_async_copy(src, dst, save.at[len(saves)])
        c.start()
        saves.append(c)

    def to_other(n, src, dst):
        return remote(src, dst, core_s.at[n], core_r.at[n], spot.other_core)

    def make_mask():
        values = seg[...].astype(F32)
        for i in range(seq // LANES):
            down = jnp.broadcast_to(values[:, i * LANES : (i + 1) * LANES], (LANES, LANES)).T
            for j in range(seq // LANES):
                across = values[:, j * LANES : (j + 1) * LANES]
                mask[pl.ds(i * LANES, LANES), pl.ds(j * LANES, LANES)] = jnp.where(down == across, 0.0, -1e30)
        qkv_bias[:, pl.ds(0, half)] = jnp.broadcast_to(bq[...].astype(F32).reshape(1, half), (8, half))
        qkv_bias[:, pl.ds(half, half)] = jnp.zeros((8, half), F32)
        qkv_bias[:, pl.ds(2 * half, half)] = jnp.broadcast_to(bv[...].astype(F32).reshape(1, half), (8, half))

    def spread_pars():
        for r in range(LINE):
            pars[:, pl.ds(r * (width // LINE), width // LINE)] = pars4[r]

    def project():
        def chunk(c):
            cols = at(c, 256)
            w = wqkv[:, :, cols].reshape(width, 256)
            value = (dot(xs[...], w) + qkv_bias[0:1, cols]).astype(LOW).astype(F32)
            qkv[:, cols] = (value * jnp.where(c < half // 256, 0.125, 1.0)).astype(LOW)

        loop(3 * half // 256, chunk)

    def transpose_x():
        loop(width // LANES, lambda c: x_t.__setitem__((at(c, LANES), slice(None)), xs[:, at(c, LANES)].T))

    def attend(pair):
        lanes = pl.ds(pair * LANES, LANES)
        keys = qkv[:, pl.ds(half + pair * LANES, LANES)]
        values = qkv[:, pl.ds(2 * half + pair * LANES, LANES)]

        def block(i):
            rows = at(i, LANES)
            queries = qkv[rows, lanes]
            total = None
            for h in range(2):
                scores = dot_t(queries * head_lanes(h, LOW), keys) + mask[rows, :]
                expo = jnp.exp(scores - jnp.max(scores, 1, keepdims=True))
                p = (expo / jnp.sum(expo, 1, keepdims=True)).astype(LOW)
                probs[2 * pair + h, rows, :] = p
                head = dot(p, values) * head_lanes(h, F32)
                total = head if total is None else total + head
            mixed[rows, lanes] = total.astype(LOW)

        loop(seq // LANES, block)
        mixed_t[lanes, :] = mixed[:, lanes].T

    def attn_out(r):
        part[:, pl.ds(r * 256, 256)] = dot(mixed[...], wo[r])

    def first_norm():
        def block(i):
            rows, there = at(i, BLOCK), rows_of(mine, i, BLOCK)
            value = xs[there, :].astype(F32) + (part[there, :] + recv1[rows, :] + pars[0:1, :])
            centred = value - jnp.mean(value, 1, keepdims=True)
            scale = lax.rsqrt(jnp.mean(centred * centred, 1, keepdims=True) + norm_eps)
            one = centred * scale
            unit[rows, :] = one
            inv[rows, :] = jnp.broadcast_to(scale, (BLOCK, LANES))
            h = one * pars[1:2, :] + pars[2:3, :]
            h1[rows, :] = h
            h_low[there, :] = h.astype(LOW)

        loop(own // BLOCK, block)

    def transpose_h():
        loop(width // LANES, lambda c: h_t.__setitem__((at(c, LANES), slice(None)), h_low[:, at(c, LANES)].T))

    def grow(c):
        cols = at(c, 256)
        inner[...] = dot(h_low[...], wi[:, :, cols].reshape(width, 256))
        bias = bi[cols].astype(F32).reshape(1, 256)

        def block(i):
            rows = at(i, 64)
            v = inner[rows, :] + bias
            cdf = 0.5 * (1.0 + lax.erf(v * inv_root_two))
            slope[rows, cols] = cdf + v * (jnp.exp(-0.5 * v * v) * inv_root_two_pi)
            act[rows, cols] = (v * cdf).astype(LOW)

        loop(seq // 64, block)
        act_t[cols, :] = act[:, cols].T

    def shrink(r):
        part[:, at(r, 256)] = dot(act[...], wout[r])

    def second_norm():
        sums[...] = jnp.zeros_like(sums)

        def block(i):
            rows, there = at(i, BLOCK), rows_of(mine, i, BLOCK)
            value = h1[rows, :] + (part[there, :] + recv2[rows, :] + pars[3:4, :])
            centred = value - jnp.mean(value, 1, keepdims=True)
            scale = lax.rsqrt(jnp.mean(centred * centred, 1, keepdims=True) + norm_eps)
            one = centred * scale
            out[rows, :] = (one * pars[4:5, :] + pars[5:6, :]).astype(LOW)
            dy = cts[rows, :].astype(F32)
            s = dy * pars[4:5, :]
            d = scale * (s - jnp.mean(s, 1, keepdims=True) - one * jnp.mean(s * one, 1, keepdims=True))
            dpre[rows, :] = d
            d_low = d.astype(LOW)
            dout[there, :] = d_low
            sums[0] += fold(d_low.astype(F32))
            sums[1] += fold(dy * one)
            sums[2] += fold(dy)

        loop(own // BLOCK, block)

    z = [(g, n) for g in range(GROUPS) for n in range(LINE - 1)]
    done_z, done_xy = [0], [0]

    def advance(n_z, n_xy):
        while done_z[0] < n_z or done_xy[0] < n_xy:
            if done_z[0] < n_z and done_z[0] - done_xy[0] < 3 or done_xy[0] >= n_xy:
                g, n = z[done_z[0]]
                if n == 0 and g + 1 < GROUPS:
                    gather.start_own(g + 1)
                gather.z_step(g, n)
                done_z[0] += 1
            else:
                gather.xy_step(*z[done_xy[0]])
                done_xy[0] += 1

    def arrive(g):
        for n in range(LINE - 1):
            gather.arrive(g, n)

    gather.start_own(0)
    tokens.start_x()
    tokens.start_par()
    make_mask()
    advance(2, 0)
    tokens.wait_x()
    advance(3, 1)
    transpose_x()
    keep(x_t, o_xt)
    advance(5, 3)
    arrive(0)
    tokens.wait_par()
    spread_pars()
    project()
    keep(wqkv, out_w[0])
    keep(qkv, o_qkv)
    keep(pars, o_pars)
    tokens.start_ct()
    for pair in range(half // LANES):
        attend(pair)
        advance(6 + pair // 2, 4 + pair // 2)
    keep(probs, o_probs)
    keep(mixed_t, o_mixed_t)
    advance(8, 6)
    arrive(1)
    keep(wo, out_w[1])
    for r in range(LINE):
        attn_out(r)
    first = to_other(0, part.at[pl.ds(pl.multiple_of(theirs, own), own)], recv1)
    first.start()
    advance(9, 7)
    first.wait_recv()
    first_norm()
    pass_h = to_other(1, *[h_low.at[pl.ds(pl.multiple_of(mine, own), own)]] * 2)
    pass_h.start()
    keep(unit, o_unit)
    keep(inv, o_inv)
    advance(10, 8)
    pass_h.wait_recv()
    transpose_h()
    keep(h_t, o_h_t)
    advance(11, 9)
    arrive(2)
    keep(wi, out_w[2])
    advance(12, 9)
    first.wait_send()
    loop(3, grow)
    advance(12, 10)
    loop(3, lambda c: grow(c + 3))
    advance(12, 11)
    loop(2, lambda c: grow(c + 6))
    keep(slope, o_slope)
    keep(act_t, o_act_t)
    tokens.wait_ct()
    for n in range(LINE):
        if n == 0:
            r = spot.row
        else:
            r = spot.near[n - 1]
            if n == LINE - 1:
                advance(12, 12)
            gather.arrive(3, n - 1)
        shrink(r)
    keep(wout, out_w[3])
    second = to_other(2, part.at[pl.ds(pl.multiple_of(theirs, own), own)], recv2)
    second.start()
    second.wait_recv()
    second_norm()
    pass_d = to_other(3, *[dout.at[pl.ds(pl.multiple_of(mine, own), own)]] * 2)
    pass_d.start()
    keep(dpre, o_dpre)
    keep(out, o_out)
    keep(sums, o_sums)
    pass_d.wait_recv()
    keep(dout, o_dout)
    second.wait_send()
    pass_h.wait_send()
    pass_d.wait_send()
    gather.drain()
    tokens.drain()
    for c in saves:
        c.wait()


def forward(x, ct, wq, wk, wv, wo, wi, wout, seg, bq, bv, bi, small):
    half, hidden = wq.shape[1], wi.shape[1]
    seq, width = x.shape[0] // 2, MODEL_WIDTH
    own, heads = seq // 2, half // HD
    weights = [((LINE, wq.shape[0], 3 * half), LOW), ((LINE,) + wo.shape, LOW), ((LINE,) + wi.shape, LOW), ((LINE,) + wout.shape, LOW)]
    named = dict(
        xs=((seq, width), LOW), cts=((own, width), LOW), pars4=((LINE, 8, width // LINE), F32), pars=((8, width), F32),
        qkv=((seq, 3 * half), LOW), qkv_bias=((8, 3 * half), F32), probs=((heads, seq, seq), LOW), mask=((seq, seq), F32),
        mixed=((seq, half), LOW), part=((seq, width), F32), recv1=((own, width), F32), recv2=((own, width), F32),
        unit=((own, width), F32), inv=((own, LANES), F32), h1=((own, width), F32), h_low=((seq, width), LOW),
        inner=((seq, 256), F32), slope=((seq, hidden), F32), act=((seq, hidden), LOW), act_t=((hidden, seq), LOW),
        h_t=((width, seq), LOW), x_t=((width, seq), LOW), mixed_t=((half, seq), LOW), dpre=((own, width), F32),
        dout=((seq, width), LOW), out=((own, width), LOW), sums=((3, 8, width), F32),
    )
    saved = ("x_t", "qkv", "probs", "mixed_t", "unit", "inv", "h_t", "slope", "act_t", "dpre", "dout", "pars", "out", "sums")
    outs = weights + [named[n] for n in saved]
    res = pl.pallas_call(
        forward_kernel,
        name="forward",
        out_shape=[jax.ShapeDtypeStruct(*o) for o in outs],
        in_specs=[ANYWHERE] * 8 + [IN_VMEM] * (4 + len(small)),
        out_specs=[ANYWHERE] * len(outs),
        scratch_shapes=[pltpu.VMEM(*w) for w in weights]
        + [pltpu.VMEM(*named[n]) for n in named]
        + Tokens.SEMS
        + Gather.SEMS
        + [pltpu.SemaphoreType.DMA((4,)), pltpu.SemaphoreType.DMA((4,)), pltpu.SemaphoreType.DMA((len(outs),))],
        compiler_params=pltpu.CompilerParams(collective_id=0, has_side_effects=True, vmem_limit_bytes=60 * 2**20),
    )(x, ct, wq, wk, wv, wo, wi, wout, seg, bq, bv, bi, *small)
    return res[:GROUPS], dict(zip(saved, res[GROUPS:]))


class Sums:
    SEMS = [pltpu.SemaphoreType.DMA((3,)), pltpu.SemaphoreType.DMA((3,)), pltpu.SemaphoreType.DMA((LINE,)), pltpu.SemaphoreType.DMA((LINE,))]

    def __init__(self, spot, vec, from_core, with_x, from_x, with_y, from_y, from_line, sems):
        self.spot, self.vec, self.from_core, self.with_x = spot, vec, from_core, with_x
        self.from_x, self.with_y, self.from_y, self.from_line = from_x, with_y, from_y, from_line
        self.s, self.r, self.z_s, self.z_r = sems

    def hop(self, n):
        s = self.spot
        src, dst, to = (
            (self.vec.at[pl.ds(0, 8)], self.from_core, s.other_core),
            (self.with_x, self.from_x, s.beside_x),
            (self.with_y, self.from_y, s.beside_y),
        )[n]
        return remote(src, dst, self.s.at[n], self.r.at[n], to)

    def line(self, away):
        s = self.spot
        row = lax.rem(s.row + away, LINE)
        return remote(self.from_line.at[s.row], self.from_line.at[s.row], self.z_s.at[away], self.z_r.at[s.row], s.at_row(row))

    def step(self, n):
        if n == 0:
            self.hop(0).start()
        elif n == 1:
            self.hop(0).wait_recv()
            self.with_x[pl.ds(0, 8), :] = self.vec[pl.ds(0, 8), :] + self.from_core[...]
            self.with_x[pl.ds(8, 8), :] = self.vec[pl.ds(8, 8), :]
            self.hop(1).start()
        elif n == 2:
            self.hop(1).wait_recv()
            self.with_y[...] = self.with_x[...] + self.from_x[...]
            self.hop(2).start()
        elif n == 3:
            self.hop(2).wait_recv()
            self.from_line[self.spot.row] = self.with_y[...] + self.from_y[...]
            for away in range(1, LINE):
                self.line(away).start()

    def total(self):
        s = self.spot
        for row in s.near:
            block = self.from_line.at[row]
            pltpu.make_async_copy(block, block, self.z_r.at[row]).wait()
        return self.from_line[0] + self.from_line[1] + self.from_line[2] + self.from_line[3]

    def drain(self):
        for n in range(3):
            self.hop(n).wait_send()
        for away in range(1, LINE):
            self.line(away).wait_send()


SAVED = ("x_t", "qkv", "probs", "mixed_t", "unit", "inv", "h_t", "slope", "act_t", "dpre", "dout", "pars", "out")


def backward_kernel(*refs):
    it = iter(refs)

    def take(n):
        return [next(it) for _ in range(n)]

    wqkv_h, wo_h, wi_h, wout_h = take(GROUPS)
    saved = dict(zip(SAVED, take(len(SAVED))))
    (sums2,) = take(1)
    final = take(GROUPS)
    placed_out, placed_dx, o_norms, o_bias = take(4)
    wo, wi, wout, wst = take(4)
    parts, rel_a, rel_b, from_x, from_y, line, stage = (take(GROUPS) for _ in range(7))
    act_t, dout, h_t, dpre, unit, inv, pars, mixed_t, qkv = take(9)
    slope, probs, ds, dinner, part, recv1, recv2, dattn, dmixed, dqkv, dx = take(11)
    vecs = take(7)
    scat_sems, sum_sems = take(len(Scatter.SEMS)), take(len(Sums.SEMS))
    out_sems, dx_sems = take(2), take(2)
    core_s, core_r, load, st_sem, sl_sem, pr_sem = take(6)

    spot = Spot()
    scatter = Scatter(spot, parts, rel_a, rel_b, from_x, from_y, line, stage, final, scat_sems)
    totals = Sums(spot, *vecs, sum_sems)
    vec = vecs[0]
    place_out, place_dx = Spread(spot, saved["out"], placed_out, out_sems), Spread(spot, dx, placed_dx, dx_sems)
    seq, width = dout.shape
    hidden = dinner.shape[1]
    half = qkv.shape[1] // 3
    own = seq // 2
    cut = width // LINE
    mine, theirs = spot.col * own, (1 - spot.col) * own

    def rows_of(base, start, size):
        return pl.ds(pl.multiple_of(base + start * size, size), size)

    fetches = {}

    def fetch(name, src, dst):
        fetches[name] = pltpu.make_async_copy(src, dst, load.at[len(fetches)])
        fetches[name].start()

    def ready(*names):
        for n in names:
            fetches[n].wait()

    def to_other(n, src, dst):
        return remote(src, dst, core_s.at[n], core_r.at[n], spot.other_core)

    units = [(g, t) for g in range(GROUPS) for t in range(LINE)]
    second, third, fourth = [0], [0], [0]

    def serve(n2, n3):
        while second[0] < n2 or third[0] < n3:
            if second[0] < n2 and (second[0] - third[0] < 2 or third[0] >= n3):
                scatter.second(*units[second[0]])
                second[0] += 1
            else:
                scatter.third(*units[third[0]])
                third[0] += 1
                while fourth[0] < GROUPS and third[0] >= LINE * (fourth[0] + 1) + 2:
                    scatter.fourth(fourth[0])
                    fourth[0] += 1

    def send(g):
        for t in range(LINE):
            scatter.first(g, t)
        for t in range(LINE):
            scatter.direct(g, t)

    def wout_grad(f):
        rows = at(f, 512)
        for r in range(LINE):
            parts[0][r, rows, :] = dot(act_t[rows, :], dout[:, pl.ds(r * cut, cut)]).astype(LOW)

    def slope_copy(f):
        slot = lax.rem(f, 2)
        return pltpu.make_async_copy(saved["slope"].at[:, at(f, 256)], slope.at[slot], sl_sem.at[slot])

    def inner_grad(f):
        rows = at(f, 256)

        @pl.when(f + 1 < hidden // 256)
        def _():
            slope_copy(f + 1).start()

        total = dot_t(dout[:, pl.ds(0, cut)], wout[0, rows, :])
        for r in range(1, LINE):
            total += dot_t(dout[:, pl.ds(r * cut, cut)], wout[r, rows, :])
        slope_copy(f).wait()
        part[:, pl.ds(0, 256)] = total
        part[pl.ds(0, 8), pl.ds(256, 256)] = jnp.zeros((8, 256), F32)

        def block(i):
            here = at(i, 64)
            d = (part[here, pl.ds(0, 256)] * slope[lax.rem(f, 2), here, :]).astype(LOW)
            dinner[here, rows] = d
            part[pl.ds(0, 8), pl.ds(256, 256)] += fold(d.astype(F32))

        loop(seq // 64, block)
        row, col = f // 4, lax.rem(f, 4)
        vec[pl.ds(9 + row, 1), at(col, 256)] = jnp.sum(part[pl.ds(0, 8), pl.ds(256, 256)], 0, keepdims=True)

    def hidden_grad(r):
        part[:, at(r, cut)] = dot_t(dinner[...], wi[r])

    def wi_grad(t):
        row = scatter.order[t]

        def chunk(n):
            cols = at(n, 512)
            parts[1][row, :, cols] = dot(h_t[at(row, cut), :], dinner[:, cols]).astype(LOW)

        loop(hidden // 512, chunk)

    def first_norm_back():
        part_sums = jnp.zeros((8, width), F32)

        def block(i, carry):
            b_sum, g_sum, s_sum = carry
            rows, there = at(i, BLOCK), rows_of(mine, i, BLOCK)
            dh = dpre[rows, :] + (part[there, :] + recv1[rows, :])
            one = unit[rows, :]
            s = dh * pars[1:2, :]
            scale = inv[rows, :][:, 0:1]
            d = scale * (s - jnp.mean(s, 1, keepdims=True) - one * jnp.mean(s * one, 1, keepdims=True))
            dpre[rows, :] = d
            d_low = d.astype(LOW)
            dattn[there, :] = d_low
            return b_sum + fold(d_low.astype(F32)), g_sum + fold(dh * one), s_sum + fold(dh)

        b_sum, g_sum, s_sum = lax.fori_loop(0, own // BLOCK, block, (part_sums, part_sums, part_sums))
        for i, v in enumerate((b_sum, g_sum, s_sum)):
            vec[pl.ds(i, 1), :] = jnp.sum(v, 0, keepdims=True)

    def mixed_grad(n):
        rows = at(n, 256)
        total = dot_t(dattn[:, pl.ds(0, cut)], wo[0, rows, :])
        for r in range(1, LINE):
            total += dot_t(dattn[:, pl.ds(r * cut, cut)], wo[r, rows, :])
        dmixed[:, rows] = total.astype(LOW)

    def wo_grad(r):
        parts[2][r] = dot(mixed_t[...], dattn[:, at(r, cut)]).astype(LOW)

    def probs_copy(head):
        return pltpu.make_async_copy(saved["probs"].at[head], probs.at[head % 4], pr_sem.at[head % 4])

    def attend_back(pair):
        lanes = pl.ds(pair * LANES, LANES)
        keys_at, values_at = pl.ds(half + pair * LANES, LANES), pl.ds(2 * half + pair * LANES, LANES)
        slots = [(2 * pair + h) % 4 for h in range(2)]

        def block(i):
            rows = at(i, LANES)
            grad = dmixed[rows, lanes]
            total = None
            for h in range(2):
                dp = dot_t(grad * head_lanes(h, LOW), qkv[:, values_at])
                p = probs[slots[h], rows, :].astype(F32)
                d = (p * (dp - jnp.sum(p * dp, 1, keepdims=True))).astype(LOW)
                ds[h, rows, :] = d
                head = dot(d, qkv[:, keys_at]) * head_lanes(h, F32)
                total = head if total is None else total + head
            dqkv[rows, lanes] = (total * 0.125).astype(LOW)

        loop(seq // LANES, block)
        queries_t, grad_t = qkv[:, lanes].T, dmixed[:, lanes].T
        dk = jnp.concatenate([dot(queries_t[h * HD : (h + 1) * HD], ds[h]) for h in range(2)], 0)
        dqkv[:, keys_at] = dk.astype(LOW).T
        dv = jnp.concatenate([dot(grad_t[h * HD : (h + 1) * HD], probs[slots[h]]) for h in range(2)], 0)
        dqkv[:, values_at] = dv.astype(LOW).T

    def qkv_sums():
        for i, base in enumerate((0, 2 * half)):
            cols = pl.ds(base, half)

            def block(n, carry):
                return carry + fold(dqkv[at(n, 64), cols].astype(F32))

            v = lax.fori_loop(0, seq // 64, block, jnp.zeros((8, half), F32))
            vec[pl.ds(8, 1), pl.ds(i * half, half)] = jnp.sum(v, 0, keepdims=True)

    def wqkv_grad(t):
        row = scatter.order[t]

        def chunk(n):
            cols = at(n, 512)
            parts[3][row, :, cols] = dot(h_t[at(row, cut), :], dqkv[:, cols]).astype(LOW)

        loop(3 * half // 512, chunk)

    def weight_copy(r):
        return pltpu.make_async_copy(wqkv_h.at[r], wst.at[r % 2], st_sem.at[r % 2])

    def input_grad(r):
        weight_copy(r).wait()
        part[:, pl.ds(r * cut, cut)] = dot_t(dqkv[...], wst[r % 2])
        if r + 2 < LINE:
            weight_copy(r + 2).start()

    def finish_input():
        def block(i):
            rows, there = at(i, BLOCK), rows_of(mine, i, BLOCK)
            dx[rows, :] = (dpre[rows, :] + (part[there, :] + recv2[rows, :])).astype(LOW)

        loop(own // BLOCK, block)

    their_half = part.at[pl.ds(pl.multiple_of(theirs, own), own)]
    my_rows = pl.ds(pl.multiple_of(mine, own), own)

    fetch("dout", saved["dout"], dout)
    fetch("act_t", saved["act_t"], act_t)
    greet(spot)
    place_out.start()
    ready("dout", "act_t")
    fetch("wout", wout_h, wout)
    slope_copy(0).start()
    loop(hidden // 512, wout_grad)
    send(0)
    fetch("wi", wi_h, wi)
    fetch("h_t", saved["h_t"], h_t)
    for name, dst in (("dpre", dpre), ("unit", unit), ("inv", inv), ("pars", pars)):
        fetch(name, saved[name], dst)
    fetch("wo", wo_h, wo)
    fetch("mixed_t", saved["mixed_t"], mixed_t)
    fetch("qkv", saved["qkv"], qkv)
    for head in range(4):
        probs_copy(head).start()
    weight_copy(0).start()
    weight_copy(1).start()
    vec[...] = jnp.zeros_like(vec)
    for i in range(3):
        vec[pl.ds(3 + i, 1), :] = jnp.sum(sums2[i], 0, keepdims=True)
    ready("wout")
    loop(hidden // 256, inner_grad)
    ready("wi", "h_t")
    loop(LINE, hidden_grad)
    swap1 = to_other(0, their_half, recv1)
    swap1.start()
    serve(1, 0)
    for t in range(LINE):
        wi_grad(t)
    send(1)
    fetch("x_t", saved["x_t"], h_t)
    serve(2, 0)
    ready("dpre", "unit", "inv", "pars")
    swap1.wait_recv()
    first_norm_back()
    pass_d = to_other(1, dattn.at[my_rows], dattn.at[my_rows])
    pass_d.start()
    serve(4, 1)
    ready("wo", "mixed_t", "qkv")
    pass_d.wait_recv()
    loop(half // 256, mixed_grad)
    loop(LINE, wo_grad)
    send(2)
    for pair in range(half // LANES):
        for h in range(2):
            probs_copy(2 * pair + h).wait()
        attend_back(pair)
        for h in range(2):
            if 2 * pair + h + 4 < half // HD:
                probs_copy(2 * pair + h + 4).start()
        serve(4 + (pair + 1) // 2, 2 + pair // 2)
    ready("x_t")
    for t in range(LINE):
        wqkv_grad(t)
    send(3)
    serve(6, 4)
    swap1.wait_send()
    for r in range(LINE):
        input_grad(r)
    swap2 = to_other(2, their_half, recv2)
    swap2.start()
    qkv_sums()
    totals.step(0)
    serve(7, 5)
    swap2.wait_recv()
    finish_input()
    place_dx.start()
    for n in range(1, 4):
        totals.step(n)
        serve(7 + n, 5 + n)
    serve(len(units), len(units))
    whole = totals.total()
    totals.drain()
    for i in range(8):
        o_bias[pl.ds(i, 1), :] = whole[8 + i : 9 + i, :]
    vecs[-1][0] = whole
    o_norms[...] = vecs[-1][0, pl.ds(0, 8), at(spot.row, cut)]
    while fourth[0] < GROUPS:
        scatter.fourth(fourth[0])
        fourth[0] += 1
    for g in range(GROUPS):
        scatter.fifth(g)
    scatter.drain()
    for c in (swap2, pass_d):
        c.wait_send()
    place_out.wait()
    place_dx.wait()


def backward(weights, saved):
    wqkv, wo, wi, wout = weights
    shapes = [w.shape for w in (wout, wi, wo, wqkv)]
    seq, width = saved["dout"].shape
    half, hidden, own = wo.shape[1], wi.shape[2], seq // 2
    cut = width // LINE

    def each(f):
        return [pltpu.VMEM(f(*s), LOW) for s in shapes]

    def like(name):
        return pltpu.VMEM(saved[name].shape, saved[name].dtype)

    placed = jax.ShapeDtypeStruct((2 * seq, cut), LOW)
    scratch = (
        [pltpu.VMEM(w.shape, LOW) for w in (wo, wi, wout)]
        + [pltpu.VMEM((2,) + wqkv.shape[1:], LOW)]
        + each(lambda n, r, c: (n, r, c))
        + each(lambda n, r, c: (n, r // 8, c)) * 2
        + each(lambda n, r, c: (n, r // 4, c)) * 2
        + each(lambda n, r, c: (n + 1, r // 4, c))
        + each(lambda n, r, c: (r // 4, c))
        + [like(n) for n in ("act_t", "dout", "h_t", "dpre", "unit", "inv", "pars", "mixed_t", "qkv")]
        + [
            pltpu.VMEM((2, seq, 256), F32), pltpu.VMEM((4, seq, seq), LOW), pltpu.VMEM((2, seq, seq), LOW),
            pltpu.VMEM((seq, hidden), LOW), pltpu.VMEM((seq, width), F32), pltpu.VMEM((own, width), F32),
            pltpu.VMEM((own, width), F32), pltpu.VMEM((seq, width), LOW), pltpu.VMEM((seq, half), LOW),
            pltpu.VMEM((seq, 3 * half), LOW), pltpu.VMEM((own, width), LOW),
        ]
        + [pltpu.VMEM(s, F32) for s in ((16, width), (8, width)) + ((16, width),) * 4 + ((LINE, 16, width),)]
        + Scatter.SEMS
        + Sums.SEMS
        + Spread.SEMS * 2
        + [pltpu.SemaphoreType.DMA((n,)) for n in (3, 3, 16, 2, 2, 4)]
    )
    res = pl.pallas_call(
        backward_kernel,
        name="backward",
        out_shape=[jax.ShapeDtypeStruct(s[1:], LOW) for s in shapes]
        + [placed] * 2
        + [jax.ShapeDtypeStruct((8, cut), F32), jax.ShapeDtypeStruct((8, width), F32)],
        in_specs=[ANYWHERE] * (GROUPS + len(SAVED)) + [IN_VMEM],
        out_specs=[ANYWHERE] * (GROUPS + 2) + [IN_VMEM] * 2,
        scratch_shapes=scratch,
        compiler_params=pltpu.CompilerParams(collective_id=1, has_side_effects=True, vmem_limit_bytes=63 * 2**20),
    )(*weights, *[saved[n] for n in SAVED], saved["sums"])
    return res


def per_chip(
    hidden_in, segment_ids, query_weight, query_bias, key_weight, value_weight, value_bias, attn_out_weight,
    attn_out_bias, norm1_gain, first_norm_offset, inner_weight, inner_bias, outer_weight, outer_bias, norm2_gain,
    second_norm_offset, cotangent,
):
    half = query_weight.shape[1]
    small = (attn_out_bias, norm1_gain, first_norm_offset, outer_bias, norm2_gain, second_norm_offset)
    weights, saved = forward(
        hidden_in, cotangent, query_weight, key_weight, value_weight, attn_out_weight, inner_weight, outer_weight,
        segment_ids, query_bias, value_bias, inner_bias, small,
    )
    wout, wi, wo, wqkv, layer_out, input_grad, norms, biases = backward(weights, saved)
    wq, wk, wv = jnp.split(wqkv.astype(F32), 3, 1)
    return (
        layer_out, input_grad, wq, biases[0, :half], wk, wv, biases[0, half:], wo.astype(F32), norms[0], norms[1],
        norms[2], wi.astype(F32), biases[1:3].reshape(-1), wout.astype(F32), norms[3], norms[4], norms[5],
    )


def solution(mesh):
    def whole(*args):
        segments, wq = args[1], args[2]
        sizes = tuple(mesh.shape[a] for a in ("dp", "row", "col"))
        fits = sizes == (4, LINE, 2) and segments.shape == (16, SEQ) and wq.shape[0] == MODEL_WIDTH
        body = per_chip if fits else shards
        return jax.shard_map(body, mesh=mesh, in_specs=IN_SPECS, out_specs=OUT_SPECS, check_vma=False)(*args)

    return whole
```

```python
import functools

import jax
import jax.numpy as jnp
from jax import lax
from jax.experimental import pallas as pl
from jax.experimental.pallas import tpu as pltpu
from jax.sharding import PartitionSpec as P

MODEL_WIDTH = 1024
HD = 64
SEQ = 512


norm_eps = 1e-12
inv_root_two = 0.7071067811865476
inv_root_two_pi = 0.3989422804014327


def product(left, right):
    return jnp.dot(left, right, preferred_element_type=jnp.float32)


def over_tokens(left, right):
    return lax.dot_general(
        left, right, (((0,), (0,)), ((), ())), preferred_element_type=jnp.float32
    )


def against(left, right):
    return lax.dot_general(
        left, right, (((1,), (1,)), ((), ())), preferred_element_type=jnp.float32
    )


def col_gather(values):
    return lax.all_gather(values, "col", axis=0, tiled=True)


def row_gather(values):
    return lax.all_gather(values, "row", axis=0, tiled=True)


def row_reduce(values):
    return lax.psum_scatter(values, "row", scatter_dimension=0, tiled=True)


def col_reduce(values):
    return lax.psum_scatter(values, "col", scatter_dimension=0, tiled=True)


def row_sum_values(first_branch, second_branch):
    return lax.psum((first_branch, second_branch), "row")


def apply_norm(preact_input, norm_gain, norm_offset):
    total, squares = row_sum_values(
        jnp.sum(preact_input, 1), jnp.sum(preact_input * preact_input, 1)
    )
    row_mean = total / MODEL_WIDTH
    inverse_deviation = lax.rsqrt(squares / MODEL_WIDTH - row_mean * row_mean + norm_eps)
    centred_rows = (preact_input - row_mean[:, None]) * inverse_deviation[:, None]
    return (centred_rows * norm_gain + norm_offset, centred_rows, inverse_deviation)


def norm_backward_pass(incoming_gradient, centred_rows, inverse_deviation, norm_gain):
    scaled_rows = incoming_gradient * norm_gain
    first_branch, second_branch = row_sum_values(
        jnp.sum(scaled_rows, 1), jnp.sum(scaled_rows * centred_rows, 1)
    )
    return inverse_deviation[:, None] * (
        scaled_rows
        - first_branch[:, None] / MODEL_WIDTH
        - centred_rows * second_branch[:, None] / MODEL_WIDTH
    )


def seg_mask(segments):
    return (segments[:, None] == segments[None, :])[None]


def attend_forward(items):
    queries, keys, values, segments = items
    scores = jnp.einsum("qhd,khd->hqk", queries, keys, preferred_element_type=jnp.float32) * 0.125
    scores = jnp.where(seg_mask(segments), scores, -1e30)
    peak = jnp.max(scores, -1, keepdims=True)
    expo = jnp.exp(scores - peak)
    total = jnp.sum(expo, -1, keepdims=True)
    probs = (expo / total).astype(jnp.bfloat16)
    mixed = jnp.einsum("hqk,khd->qhd", probs, values, preferred_element_type=jnp.float32)
    return (mixed.astype(jnp.bfloat16), (peak + jnp.log(total))[..., 0])


def attend_backward(items):
    queries, keys, values, segments, dmixed, lse = items
    scores = jnp.einsum("qhd,khd->hqk", queries, keys, preferred_element_type=jnp.float32) * 0.125
    probs = jnp.where(seg_mask(segments), jnp.exp(scores - lse[..., None]), 0.0)
    dvalues = jnp.einsum(
        "hqk,qhd->khd", probs.astype(jnp.bfloat16), dmixed, preferred_element_type=jnp.float32
    )
    dprobs = jnp.einsum("qhd,khd->hqk", dmixed, values, preferred_element_type=jnp.float32)
    middle = jnp.sum(probs * dprobs, -1, keepdims=True)
    dscores = (probs * (dprobs - middle)).astype(jnp.bfloat16)
    dqueries = jnp.einsum("hqk,khd->qhd", dscores, keys, preferred_element_type=jnp.float32) * 0.125
    dkeys = jnp.einsum("hqk,qhd->khd", dscores, queries, preferred_element_type=jnp.float32) * 0.125
    return (dqueries.astype(jnp.bfloat16), dkeys.astype(jnp.bfloat16), dvalues.astype(jnp.bfloat16))


def shards(
    hidden_in,
    segment_ids,
    query_weight,
    query_bias,
    key_weight,
    value_weight,
    value_bias,
    attn_out_weight,
    attn_out_bias,
    norm1_gain,
    first_norm_offset,
    inner_weight,
    inner_bias,
    outer_weight,
    outer_bias,
    norm2_gain,
    second_norm_offset,
    cotangent,
):
    local_seqs = segment_ids.shape[0]
    col_width = query_weight.shape[1]
    head_local = col_width // HD
    first_norm_gain = norm1_gain.astype(jnp.float32)
    second_norm_gain = norm2_gain.astype(jnp.float32)
    x_full = col_gather(hidden_in)
    part_q, part_k, part_v = (
        lax.psum_scatter(product(x_full, query_weight), "row", scatter_dimension=0, tiled=True),
        lax.psum_scatter(product(x_full, key_weight), "row", scatter_dimension=0, tiled=True),
        lax.psum_scatter(product(x_full, value_weight), "row", scatter_dimension=0, tiled=True),
    )
    queries = (part_q + query_bias).astype(jnp.bfloat16)
    keys = part_k.astype(jnp.bfloat16)
    values = (part_v + value_bias).astype(jnp.bfloat16)
    q_heads = queries.reshape(local_seqs, SEQ, head_local, HD)
    k_heads = keys.reshape(local_seqs, SEQ, head_local, HD)
    v_heads = values.reshape(local_seqs, SEQ, head_local, HD)
    mixed, lse = lax.map(attend_forward, (q_heads, k_heads, v_heads, segment_ids))
    mixed = mixed.reshape(local_seqs * SEQ, col_width)
    mixed_full = row_gather(mixed)
    attn = col_reduce(product(mixed_full, attn_out_weight)) + attn_out_bias
    first_preact = hidden_in.astype(jnp.float32) + attn
    hidden_state, first_centred_rows, first_inverse_deviation = apply_norm(
        first_preact, first_norm_gain, first_norm_offset
    )
    hidden_full = col_gather(hidden_state.astype(jnp.bfloat16))
    inner = row_reduce(product(hidden_full, inner_weight)) + inner_bias
    active = jax.nn.gelu(inner, approximate=False).astype(jnp.bfloat16)
    active_full = row_gather(active)
    outer_product = col_reduce(product(active_full, outer_weight)) + outer_bias
    closing_result, second_centred_rows, second_inverse_deviation = apply_norm(
        hidden_state + outer_product, second_norm_gain, second_norm_offset
    )
    layer_out = closing_result.astype(jnp.bfloat16)
    output_gradient = cotangent.astype(jnp.float32)
    second_gain_gradient = jnp.sum(output_gradient * second_centred_rows, 0)
    shift_two_grad = jnp.sum(output_gradient, 0)
    second_preact_grad = norm_backward_pass(
        output_gradient, second_centred_rows, second_inverse_deviation, second_norm_gain
    )
    dout_full = col_gather(second_preact_grad.astype(jnp.bfloat16))
    outer_bias_grad = jnp.sum(dout_full, 0, dtype=jnp.float32)
    outer_weight_grad = over_tokens(active_full, dout_full)
    dactive = row_reduce(against(dout_full, outer_weight))
    cdf = 0.5 * (1.0 + lax.erf(inner * inv_root_two))
    density = jnp.exp(-0.5 * inner * inner) * inv_root_two_pi
    dinner = (dactive * (cdf + inner * density)).astype(jnp.bfloat16)
    dinner_full = row_gather(dinner)
    inner_bias_grad = jnp.sum(dinner_full, 0, dtype=jnp.float32)
    inner_weight_grad = over_tokens(hidden_full, dinner_full)
    hidden_state_grad = second_preact_grad + col_reduce(against(dinner_full, inner_weight))
    first_gain_gradient = jnp.sum(hidden_state_grad * first_centred_rows, 0)
    shift_one_grad = jnp.sum(hidden_state_grad, 0)
    first_preact_grad = norm_backward_pass(
        hidden_state_grad, first_centred_rows, first_inverse_deviation, first_norm_gain
    )
    dattn_full = col_gather(first_preact_grad.astype(jnp.bfloat16))
    attn_out_bias_grad = jnp.sum(dattn_full, 0, dtype=jnp.float32)
    attn_out_weight_grad = over_tokens(mixed_full, dattn_full)
    dmixed = row_reduce(against(dattn_full, attn_out_weight)).astype(jnp.bfloat16)
    dq_heads, dk_heads, dv_heads = lax.map(
        attend_backward,
        (
            q_heads,
            k_heads,
            v_heads,
            segment_ids,
            dmixed.reshape(local_seqs, SEQ, head_local, HD),
            lse,
        ),
    )
    dq_rows = dq_heads.reshape(local_seqs * SEQ, col_width)
    dk_rows = dk_heads.reshape(local_seqs * SEQ, col_width)
    dv_rows = dv_heads.reshape(local_seqs * SEQ, col_width)
    dq_full, dk_full, dv_full = (
        lax.all_gather(dq_rows, "row", axis=0, tiled=True),
        lax.all_gather(dk_rows, "row", axis=0, tiled=True),
        lax.all_gather(dv_rows, "row", axis=0, tiled=True),
    )
    query_bias_grad = jnp.sum(dq_full, 0, dtype=jnp.float32)
    value_bias_grad = jnp.sum(dv_full, 0, dtype=jnp.float32)
    query_weight_grad = over_tokens(x_full, dq_full)
    key_weight_grad = over_tokens(x_full, dk_full)
    value_weight_grad = over_tokens(x_full, dv_full)
    dx_part = (
        against(dq_full, query_weight)
        + against(dk_full, key_weight)
        + against(dv_full, value_weight)
    )
    input_grad = (first_preact_grad + col_reduce(dx_part)).astype(jnp.bfloat16)
    summed = (
        lax.psum(query_weight_grad.astype(jnp.bfloat16), "dp").astype(jnp.float32),
        lax.psum(query_bias_grad.astype(jnp.bfloat16), "dp").astype(jnp.float32),
        lax.psum(key_weight_grad.astype(jnp.bfloat16), "dp").astype(jnp.float32),
        lax.psum(value_weight_grad.astype(jnp.bfloat16), "dp").astype(jnp.float32),
        lax.psum(value_bias_grad.astype(jnp.bfloat16), "dp").astype(jnp.float32),
        lax.psum(attn_out_weight_grad.astype(jnp.bfloat16), "dp").astype(jnp.float32),
        lax.psum(attn_out_bias_grad.astype(jnp.bfloat16), "dp").astype(jnp.float32),
        lax.psum(inner_weight_grad.astype(jnp.bfloat16), "dp").astype(jnp.float32),
        lax.psum(inner_bias_grad.astype(jnp.bfloat16), "dp").astype(jnp.float32),
        lax.psum(outer_weight_grad.astype(jnp.bfloat16), "dp").astype(jnp.float32),
        lax.psum(outer_bias_grad.astype(jnp.bfloat16), "dp").astype(jnp.float32),
    )
    norms = lax.psum(
        (first_gain_gradient, shift_one_grad, second_gain_gradient, shift_two_grad), ("dp", "col")
    )
    return (
        layer_out,
        input_grad,
        summed[0],
        summed[1],
        summed[2],
        summed[3],
        summed[4],
        summed[5],
        summed[6],
        norms[0],
        norms[1],
        summed[7],
        summed[8],
        summed[9],
        summed[10],
        norms[2],
        norms[3],
    )


IN_SPECS = (
    P(("dp", "col"), "row"),
    P(("dp", "row"), None),
    P("row", "col"),
    P("col"),
    P("row", "col"),
    P("row", "col"),
    P("col"),
    P("col", "row"),
    P("row"),
    P("row"),
    P("row"),
    P("row", "col"),
    P("col"),
    P("col", "row"),
    P("row"),
    P("row"),
    P("row"),
    P(("dp", "col"), "row"),
)
OUT_SPECS = (
    P(("dp", "col"), "row"),
    P(("dp", "col"), "row"),
    P("row", "col"),
    P("col"),
    P("row", "col"),
    P("row", "col"),
    P("col"),
    P("col", "row"),
    P("row"),
    P("row"),
    P("row"),
    P("row", "col"),
    P("col"),
    P("col", "row"),
    P("row"),
    P("row"),
    P("row"),
)


MESH = pl.DeviceIdType.MESH
LINE = 4
GROUPS = 4
GATHERED = ((1, 0, 8), (0, 0, 8), (2, 0, 4), (2, 4, 4), (3, 0, 4), (3, 4, 4))
SCATTERED = (
    (0, 0, 4, True), (0, 4, 4, False), (1, 0, 8, False), (3, 0, 4, False), (3, 4, 4, False), (2, 0, 8, False),
)


class Spot:
    def __init__(self):
        self.dp = lax.axis_index("dp")
        self.row = lax.axis_index("row")
        self.col = lax.axis_index("col")
        k, r = self.dp, self.row
        self.dp_x = k + 1 - 2 * lax.rem(k, 2)
        self.dp_y = lax.rem(k + 2, 4)
        self.dp_d = 3 - k
        self.beside_x = (self.dp_x, r, self.col)
        self.beside_y = (self.dp_y, r, self.col)
        self.other_core = (k, r, 1 - self.col)
        self.inside = jnp.logical_and(r > 0, r < LINE - 1)
        first = jnp.where(r > 0, r - 1, 1)
        second = jnp.where(r == 0, 2, jnp.where(r == LINE - 1, 1, r + 1))
        third = jnp.where(r < 2, LINE - 1, 0)
        self.near = (first, second, third)

    def at_row(self, row):
        return (self.dp, row, self.col)


def remote(src, dst, send, recv, device):
    return pltpu.make_async_remote_copy(
        src_ref=src, dst_ref=dst, send_sem=send, recv_sem=recv, device_id=device, device_id_type=MESH
    )


def greet(spot):
    barrier = pltpu.get_barrier_semaphore()
    for away in range(LINE):
        row = lax.rem(spot.row + away, LINE)
        for core in range(2):
            if away == 0 and core == 0:
                continue
            col = lax.rem(spot.col + core, 2)
            pl.semaphore_signal(barrier, inc=1, device_id=(spot.dp, row, col), device_id_type=MESH)
    pl.semaphore_signal(barrier, inc=1, device_id=spot.beside_x, device_id_type=MESH)
    pl.semaphore_signal(barrier, inc=1, device_id=spot.beside_y, device_id_type=MESH)
    pl.semaphore_wait(barrier, 2 * LINE + 1)


class Gather:
    SEMS = (
        [pltpu.SemaphoreType.DMA((len(GATHERED), 2))]
        + [pltpu.SemaphoreType.DMA((GROUPS, 3))]
        + [pltpu.SemaphoreType.DMA((len(GATHERED), LINE))] * 10
    )

    def __init__(self, spot, shards, bufs, sems):
        self.spot, self.shards, self.bufs = spot, shards, bufs
        (self.own_s, self.own_l, self.zs, self.zr, self.xs, self.xr, self.ys, self.yr, self.fas, self.far, self.fbs, self.fbr) = sems
        self.loaded = set()

    def piece(self, g, row, j, half=None):
        which, first, count = GATHERED[g]
        eighth = self.bufs[which].shape[1] // 8
        q = eighth * count // 4
        size = q if half is None else q // 2
        start = first * eighth + j * q + (0 if half is None else half * size)
        return self.bufs[which].at[row, pl.ds(pl.multiple_of(start, size), size)]

    def own_copy(self, g, up):
        s = self.spot
        piece = self.piece(g, s.row, s.dp)
        row = s.row + 1 if up else s.row - 1
        return remote(piece, piece, self.own_s.at[g, int(up)], self.zr.at[g, s.row], s.at_row(row))

    def local(self, g):
        mine = self.bufs[g].at[self.spot.row]
        wide = self.shards[g][0].shape[1]
        return [
            pltpu.make_async_copy(part, mine.at[:, pl.ds(i * wide, wide)], self.own_l.at[g, i])
            for i, part in enumerate(self.shards[g])
        ]

    def load(self):
        for g in (1, 0, 2, 3):
            for c in self.local(g):
                c.start()

    def start_own(self, g):
        s = self.spot
        which = GATHERED[g][0]
        if which not in self.loaded:
            self.loaded.add(which)
            for c in self.local(which):
                c.wait()

        @pl.when(s.row < LINE - 1)
        def _():
            self.own_copy(g, True).start()

        @pl.when(s.row > 0)
        def _():
            self.own_copy(g, False).start()

    def onward(self, g, n):
        s = self.spot
        row = s.near[n]
        p = self.piece(g, row, s.dp)
        to = jnp.where(row < s.row, s.row + 1, s.row - 1)
        return remote(p, p, self.zs.at[g, row], self.zr.at[g, row], s.at_row(to))

    def across(self, g, n):
        s = self.spot
        row = s.near[n]
        p = self.piece(g, row, s.dp)
        return (
            remote(p, p, self.xs.at[g, row], self.xr.at[g, row], s.beside_x),
            remote(p, p, self.ys.at[g, row], self.yr.at[g, row], s.beside_y),
        )

    def relays(self, g, n):
        s = self.spot
        row = s.near[n]
        a = self.piece(g, row, s.dp_y, 0)
        b = self.piece(g, row, s.dp_x, 1)
        return (
            remote(a, a, self.fas.at[g, row], self.far.at[g, row], s.beside_x),
            remote(b, b, self.fbs.at[g, row], self.fbr.at[g, row], s.beside_y),
        )

    def z_step(self, g, n):
        self.onward(g, n).wait_recv()

        @pl.when(self.spot.inside)
        def _():
            self.onward(g, n).start()

        for c in self.across(g, n):
            c.start()

    def x_step(self, g, n):
        s = self.spot
        row = s.near[n]
        p = self.piece(g, row, s.dp_x)
        remote(p, p, self.xs.at[g, row], self.xr.at[g, row], s.beside_x).wait_recv()
        self.relays(g, n)[1].start()

    def y_step(self, g, n):
        s = self.spot
        row = s.near[n]
        p = self.piece(g, row, s.dp_y)
        remote(p, p, self.ys.at[g, row], self.yr.at[g, row], s.beside_y).wait_recv()
        self.relays(g, n)[0].start()

    def arrive(self, g, n):
        s = self.spot
        row = s.near[n]
        a, b = self.piece(g, row, s.dp_d, 0), self.piece(g, row, s.dp_d, 1)
        remote(a, a, self.fas.at[g, row], self.far.at[g, row], s.beside_x).wait_recv()
        remote(b, b, self.fbs.at[g, row], self.fbr.at[g, row], s.beside_y).wait_recv()

    def drain(self):
        s = self.spot
        for g in range(len(GATHERED)):

            @pl.when(s.row < LINE - 1)
            def _():
                self.own_copy(g, True).wait_send()

            @pl.when(s.row > 0)
            def _():
                self.own_copy(g, False).wait_send()

            for n in range(LINE - 1):

                @pl.when(s.inside)
                def _():
                    self.onward(g, n).wait_send()

                for c in self.across(g, n) + self.relays(g, n):
                    c.wait_send()


class Tokens:
    SEMS = [pltpu.SemaphoreType.DMA((2,)), pltpu.SemaphoreType.DMA((LINE,))] + [pltpu.SemaphoreType.DMA((LINE,))] * 2 + [
        pltpu.SemaphoreType.DMA((2, 2)),
        pltpu.SemaphoreType.DMA((LINE,)),
        pltpu.SemaphoreType.DMA((LINE,)),
        pltpu.SemaphoreType.DMA((LINE,)),
    ]

    def __init__(self, spot, x, ct, xs, cts, pars, sems):
        self.spot = spot
        self.x, self.ct, self.xs, self.cts, self.pars = x, ct, xs, cts, pars
        (self.x_s, self.x_r, self.x_fs, self.x_fr, self.c_s, self.c_r, self.p_s, self.p_r) = sems
        self.seq = x.shape[0] // 2
        self.wide = x.shape[1]

    def cols(self, ref, row):
        return ref.at[:, pl.ds(pl.multiple_of(row * self.wide, self.wide), self.wide)]

    def x_copy(self, i, local):
        s = self.spot
        row = 2 * s.col + i
        src = self.x.at[pl.ds(i * self.seq, self.seq)]
        dst = self.cols(self.xs, s.row)
        if local:
            return pltpu.make_async_copy(src, dst, self.x_r.at[s.row])
        return remote(src, dst, self.x_s.at[i], self.x_r.at[s.row], s.at_row(row))

    def ct_copy(self, i, core, local):
        s = self.spot
        half = self.seq // 2
        row = 2 * s.col + i
        src = self.ct.at[pl.ds(i * self.seq + core * half, half)]
        dst = self.cols(self.cts, s.row)
        if local:
            return pltpu.make_async_copy(src, dst, self.c_r.at[s.row])
        return remote(src, dst, self.c_s.at[i, core], self.c_r.at[s.row], (s.dp, row, jnp.int32(core)))

    def par_copy(self, away):
        s = self.spot
        row = lax.rem(s.row + away, LINE)
        mine = self.pars.at[s.row]
        return remote(mine, mine, self.p_s.at[away], self.p_r.at[s.row], s.at_row(row))

    def start_x(self):
        s = self.spot
        for i in range(2):
            here = 2 * s.col + i == s.row

            @pl.when(here)
            def _():
                self.x_copy(i, True).start()

            @pl.when(jnp.logical_not(here))
            def _():
                self.x_copy(i, False).start()

    def start_par(self):
        for away in range(1, LINE):
            self.par_copy(away).start()

    def start_ct(self):
        s = self.spot
        for i in range(2):
            for core in range(2):
                here = jnp.logical_and(2 * s.col + i == s.row, s.col == core)

                @pl.when(here)
                def _():
                    self.ct_copy(i, core, True).start()

                @pl.when(jnp.logical_not(here))
                def _():
                    self.ct_copy(i, core, False).start()

    def rows(self):
        return (self.spot.row,) + self.spot.near

    def relay(self, row):
        block = self.cols(self.xs, row)
        return remote(block, block, self.x_fs.at[row], self.x_fr.at[row], self.spot.other_core)

    def wait_x(self):
        s = self.spot
        first = s.row // 2 == s.col
        for row in self.rows():

            @pl.when(first)
            def _():
                block = self.cols(self.xs, row)
                pltpu.make_async_copy(block, block, self.x_r.at[row]).wait()
                self.relay(row).start()

    def wait_relayed(self):
        s = self.spot
        first = s.row // 2 == s.col
        for row in self.rows():

            @pl.when(jnp.logical_not(first))
            def _():
                self.relay(row).wait_recv()

    def wait_ct(self):
        for row in self.rows():
            block = self.cols(self.cts, row)
            pltpu.make_async_copy(block, block, self.c_r.at[row]).wait()

    def wait_par(self):
        for row in self.spot.near:
            block = self.pars.at[row]
            pltpu.make_async_copy(block, block, self.p_r.at[row]).wait()

    def drain(self):
        s = self.spot
        for i in range(2):

            @pl.when(jnp.logical_not(2 * s.col + i == s.row))
            def _():
                self.x_copy(i, False).wait_send()

            for core in range(2):

                @pl.when(jnp.logical_not(jnp.logical_and(2 * s.col + i == s.row, s.col == core)))
                def _():
                    self.ct_copy(i, core, False).wait_send()

        for away in range(1, LINE):
            self.par_copy(away).wait_send()

        @pl.when(s.row // 2 == s.col)
        def _():
            for row in self.rows():
                self.relay(row).wait_send()


ROWS_AT_ONCE = {1536: 16, 2048: 16, 256: 64}


class Scatter:
    SEMS = [pltpu.SemaphoreType.DMA((len(SCATTERED), LINE))] * 14 + [pltpu.SemaphoreType.DMA((len(SCATTERED),))] * 10

    @staticmethod
    def sizes(shapes):
        return [(shapes[b][1] // 8 * n, shapes[b][2], 1 if line else LINE) for b, _, n, line in SCATTERED]

    def __init__(self, spot, parts, rel_a, rel_b, from_x, from_y, line, stage, final, sems):
        self.spot, self.parts, self.rel_a, self.rel_b = spot, parts, rel_a, rel_b
        self.from_x, self.from_y, self.line, self.stage, self.final = from_x, from_y, line, stage, final
        (
            self.ra_s, self.ra_r, self.rb_s, self.rb_r,
            self.xa_s, self.xa_r, self.xb_s, self.xb_r,
            self.ya_s, self.ya_r, self.yb_s, self.yb_r,
            self.z_s, self.z_r,
            self.above_r, self.fx_s, self.fx_r, self.fy_s, self.fy_r,
            self.ha_s, self.ha_r, self.hb_s, self.hb_r, self.own_s,
        ) = sems
        self.order = (spot.near[2], spot.near[1], spot.near[0], spot.row)

    def rows(self, g, j, half):
        which, first, count, _ = SCATTERED[g]
        eighth = self.parts[which].shape[1] // 8
        if j is None:
            return pl.ds(first * eighth, count * eighth)
        q = eighth * count // 4
        size = q if half is None else q // 2
        start = first * eighth + j * q + (0 if half is None else half * size)
        return pl.ds(pl.multiple_of(start, size), size)

    def part(self, g, row, j=None, half=None):
        return self.parts[SCATTERED[g][0]].at[row, self.rows(g, j, half)]

    def fin(self, g, j, half=None):
        return self.final[SCATTERED[g][0]].at[self.rows(g, j, half)]

    def slot(self, g, t):
        return 0 if SCATTERED[g][3] else self.order[t]

    def half(self, ref, g, t, half):
        h = ref[g].shape[1] // 2
        return ref[g].at[self.slot(g, t), pl.ds(half * h, h)]

    def send_a(self, g, t):
        s, row = self.spot, self.order[t]
        return remote(self.part(g, row, s.dp_d, 0), self.rel_a[g].at[self.slot(g, t)], self.ra_s.at[g, row], self.ra_r.at[g, row], s.beside_y)

    def send_b(self, g, t):
        s, row = self.spot, self.order[t]
        return remote(self.part(g, row, s.dp_d, 1), self.rel_b[g].at[self.slot(g, t)], self.rb_s.at[g, row], self.rb_r.at[g, row], s.beside_x)

    def send_xa(self, g, t):
        s, row = self.spot, self.order[t]
        return remote(self.part(g, row, s.dp_x, 0), self.half(self.from_x, g, t, 0), self.xa_s.at[g, row], self.xa_r.at[g, row], s.beside_x)

    def send_xb(self, g, t):
        s, row = self.spot, self.order[t]
        return remote(self.part(g, row, s.dp_x, 1), self.half(self.from_x, g, t, 1), self.xb_s.at[g, row], self.xb_r.at[g, row], s.beside_x)

    def send_ya(self, g, t):
        s, row = self.spot, self.order[t]
        return remote(self.part(g, row, s.dp_y, 0), self.half(self.from_y, g, t, 0), self.ya_s.at[g, row], self.ya_r.at[g, row], s.beside_y)

    def send_yb(self, g, t):
        s, row = self.spot, self.order[t]
        return remote(self.part(g, row, s.dp_y, 1), self.half(self.from_y, g, t, 1), self.yb_s.at[g, row], self.yb_r.at[g, row], s.beside_y)

    def add(self, out, terms):
        rows, wide = out.shape
        step = min(ROWS_AT_ONCE[wide], rows)

        def body(i, carry):
            at = pl.ds(pl.multiple_of(i * step, step), step)
            total = terms[0][at, :].astype(jnp.float32)
            for t in terms[1:]:
                total = total + t[at, :].astype(jnp.float32)
            out[at, :] = total.astype(jnp.bfloat16)
            return carry

        lax.fori_loop(0, rows // step, body, 0)

    def first(self, g, t):
        self.send_a(g, t).start()
        self.send_b(g, t).start()

    def direct(self, g, t):
        self.send_xb(g, t).start()
        self.send_ya(g, t).start()

    def second_a(self, g, t):
        self.send_a(g, t).wait_recv()
        mine = self.part(g, self.order[t], self.spot.dp_x, 0)
        self.add(mine, (mine, self.rel_a[g].at[self.slot(g, t)]))
        self.send_xa(g, t).start()

    def second_b(self, g, t):
        self.send_b(g, t).wait_recv()
        mine = self.part(g, self.order[t], self.spot.dp_y, 1)
        self.add(mine, (mine, self.rel_b[g].at[self.slot(g, t)]))
        self.send_yb(g, t).start()

    def onward(self, g, t, above=False):
        s, row = self.spot, self.order[t]
        to = jnp.where(row > s.row, s.row + 1, s.row - 1)
        slot = jnp.where(row == s.row - 1, LINE, row)
        piece = self.part(g, row, None if SCATTERED[g][3] else s.dp)
        recv = self.above_r.at[g] if above else self.z_r.at[g, row]
        return remote(piece, self.line[g].at[slot], self.z_s.at[g, row], recv, s.at_row(to))

    def along(self, g, t, mine, terms, out):
        s, row = self.spot, self.order[t]
        if t < LINE - 1:
            passed = jnp.logical_or(jnp.logical_and(row > s.row, s.row > 0), jnp.logical_and(row < s.row, s.row < LINE - 1))
            last = row == s.row - 1

            @pl.when(passed)
            def _():
                self.onward(g, t).wait_recv()
                self.add(mine, terms + (self.line[g].at[row],))

            if len(terms) > 1:

                @pl.when(jnp.logical_not(passed))
                def _():
                    self.add(mine, terms)

            @pl.when(last)
            def _():
                self.onward(g, t, True).start()

            @pl.when(jnp.logical_not(last))
            def _():
                self.onward(g, t).start()

        else:
            below, over = self.line[g].at[s.row], self.line[g].at[LINE]

            def wait_below():
                remote(below, below, self.z_s.at[g, s.row], self.z_r.at[g, s.row], s.beside_x).wait_recv()

            def wait_over():
                remote(over, over, self.z_s.at[g, s.row], self.above_r.at[g], s.beside_x).wait_recv()

            @pl.when(s.inside)
            def _():
                wait_below()
                wait_over()
                self.add(out, terms + (below, over))

            @pl.when(s.row == 0)
            def _():
                wait_over()
                self.add(out, terms + (over,))

            @pl.when(s.row == LINE - 1)
            def _():
                wait_below()
                self.add(out, terms + (below,))

    def line_step(self, g, t):
        mine = self.part(g, self.order[t])
        self.along(g, t, mine, (mine,), mine)

    def third(self, g, t):
        s, row = self.spot, self.order[t]
        for c in (self.send_xa(g, t), self.send_xb(g, t), self.send_ya(g, t), self.send_yb(g, t)):
            c.wait_recv()
        mine = self.part(g, row, s.dp)
        slot = self.slot(g, t)
        terms = (mine, self.from_x[g].at[slot], self.from_y[g].at[slot])
        if SCATTERED[g][3]:
            self.add(self.stage[g], terms)
        else:
            self.along(g, t, mine, terms, self.stage[g])
        if t == LINE - 1:
            for c in self.spread(g):
                c.start()
            self.settle(g).start()

    def spread(self, g):
        s = self.spot
        p = self.fin(g, s.dp)
        mine = self.stage[g]
        return (
            remote(mine, p, self.fx_s.at[g], self.fx_r.at[g], s.beside_x),
            remote(mine, p, self.fy_s.at[g], self.fy_r.at[g], s.beside_y),
        )

    def settle(self, g):
        return pltpu.make_async_copy(self.stage[g], self.fin(g, self.spot.dp), self.own_s.at[g])

    def relays(self, g):
        s = self.spot
        a, b = self.fin(g, s.dp_y, 0), self.fin(g, s.dp_x, 1)
        return (
            remote(a, a, self.ha_s.at[g], self.ha_r.at[g], s.beside_x),
            remote(b, b, self.hb_s.at[g], self.hb_r.at[g], s.beside_y),
        )

    def fourth_x(self, g):
        s = self.spot
        p = self.fin(g, s.dp_x)
        remote(p, p, self.fx_s.at[g], self.fx_r.at[g], s.beside_x).wait_recv()
        self.relays(g)[1].start()

    def fourth_y(self, g):
        s = self.spot
        p = self.fin(g, s.dp_y)
        remote(p, p, self.fy_s.at[g], self.fy_r.at[g], s.beside_y).wait_recv()
        self.relays(g)[0].start()

    def fifth(self, g):
        s = self.spot
        a, b = self.fin(g, s.dp_d, 0), self.fin(g, s.dp_d, 1)
        remote(a, a, self.ha_s.at[g], self.ha_r.at[g], s.beside_x).wait_recv()
        remote(b, b, self.hb_s.at[g], self.hb_r.at[g], s.beside_y).wait_recv()

    def drain(self):
        for g in range(len(SCATTERED)):
            for t in range(LINE):
                if t == LINE - 1 or not SCATTERED[g][3]:
                    for c in (
                        self.send_a(g, t), self.send_b(g, t), self.send_xa(g, t),
                        self.send_xb(g, t), self.send_ya(g, t), self.send_yb(g, t),
                    ):
                        c.wait_send()
                if t < LINE - 1:
                    self.onward(g, t).wait_send()
            for c in self.spread(g) + self.relays(g):
                c.wait_send()
            self.settle(g).wait()


class Spread:
    SEMS = [pltpu.SemaphoreType.DMA((LINE,)), pltpu.SemaphoreType.DMA((4,))]

    def __init__(self, spot, src, out, sems):
        self.spot, self.src, self.out = spot, src, out
        self.s, self.r = sems
        self.count, wide = src.shape
        self.cut = wide // LINE

    def slot(self, n):
        return self.out.at[pl.ds(pl.multiple_of(n * self.count, self.count), self.count)]

    def copy(self, away, local=False):
        s = self.spot
        row = lax.rem(s.row + away, LINE)
        src = self.src.at[:, pl.ds(pl.multiple_of(row * self.cut, self.cut), self.cut)]
        n = 2 * lax.rem(s.row, 2) + s.col
        if local:
            return pltpu.make_async_copy(src, self.slot(n), self.r.at[n])
        return remote(src, self.slot(n), self.s.at[away], self.r.at[n], (s.dp, row, s.row // 2))

    def start(self):
        s = self.spot
        here = s.row // 2 == s.col

        @pl.when(here)
        def _():
            self.copy(0, True).start()

        @pl.when(jnp.logical_not(here))
        def _():
            self.copy(0).start()

        for away in range(1, LINE):
            self.copy(away).start()

    def wait(self):
        s = self.spot
        for n in range(4):
            pltpu.make_async_copy(self.slot(n), self.slot(n), self.r.at[n]).wait()

        @pl.when(jnp.logical_not(s.row // 2 == s.col))
        def _():
            self.copy(0).wait_send()

        for away in range(1, LINE):
            self.copy(away).wait_send()


(OWN, TOKENS_IN, COTANGENT_IN, ALONG, FROM_X, FROM_Y, TO_CORE, TURN_X, PROJECT, ATTEND, ATTN_OUT, NORM_1, TURN_H, GROW, SHRINK, NORM_2, LAST) = range(17)
(SEND, ADD_A, ADD_B, SUM_UP, LINE_STEP, BACK_X, BACK_Y, OUTER_W, INNER, HIDDEN, INNER_W, NORM_BACK, MIXED, ATTN_W, QKV_W, INPUT, SUMS, SUMS_X, SUMS_Y, SUMS_LINE, INPUT_LAST, PLACE_OUT, PLACE_INPUT) = range(17, 40)
FORWARD_ORDER = (
    (OWN, 0), (OWN, 1), (ALONG, 0, 0), (ALONG, 0, 1), (OWN, 2), (FROM_X, 0, 0), (FROM_Y, 0, 0), (ALONG, 1, 0),
    (FROM_X, 0, 1), (FROM_Y, 0, 1), (ALONG, 1, 1), (ALONG, 0, 2), (FROM_Y, 1, 0), (ALONG, 2, 0), (TOKENS_IN,),
    (ALONG, 2, 1), (ALONG, 1, 2), (FROM_X, 1, 1), (FROM_Y, 1, 1), (FROM_Y, 2, 0), (FROM_X, 1, 0), (OWN, 3),
    (FROM_Y, 1, 2), (FROM_X, 0, 2), (FROM_X, 2, 1), (FROM_X, 1, 2), (TO_CORE,), (ALONG, 3, 0), (ALONG, 3, 1),
    (OWN, 4), (PROJECT, 0), (ALONG, 3, 2), (PROJECT, 1), (PROJECT, 2), (PROJECT, 3), (PROJECT, 4), (ALONG, 2, 2),
    (PROJECT, 5), (OWN, 5), (FROM_X, 3, 1), (ATTEND, 0, 0), (ATTEND, 0, 1), (FROM_X, 3, 0), (ALONG, 4, 0),
    (FROM_Y, 3, 0), (TURN_X,), (ATTEND, 0, 2), (ATTEND, 0, 3), (ALONG, 4, 1), (ATTEND, 1, 0), (ATTEND, 1, 1),
    (ATTEND, 1, 2), (ATTEND, 1, 3), (FROM_Y, 3, 1), (FROM_X, 4, 0), (ATTEND, 2, 0), (FROM_Y, 0, 2), (FROM_X, 2, 0),
    (ATTEND, 2, 1), (FROM_Y, 3, 2), (ATTEND, 2, 2), (ATTEND, 2, 3), (ALONG, 4, 2), (ATTEND, 3, 0), (FROM_Y, 2, 1),
    (ATTEND, 3, 1), (FROM_X, 2, 2), (FROM_Y, 4, 0), (FROM_X, 3, 2), (FROM_Y, 2, 2), (ATTEND, 3, 2), (ATTEND, 3, 3),
    (ATTN_OUT, 0), (ATTN_OUT, 1), (ALONG, 5, 1), (ATTN_OUT, 2), (ATTN_OUT, 3), (ALONG, 5, 0), (NORM_1,),
    (COTANGENT_IN,), (FROM_X, 4, 1), (ALONG, 5, 2), (FROM_Y, 4, 2), (FROM_X, 4, 2), (GROW, 0), (GROW, 1), (GROW, 2),
    (FROM_Y, 4, 1), (GROW, 3), (FROM_X, 5, 1), (FROM_Y, 5, 1), (FROM_Y, 5, 0), (GROW, 4), (FROM_Y, 5, 2),
    (FROM_X, 5, 0), (FROM_X, 5, 2), (GROW, 5), (GROW, 6), (GROW, 7), (SHRINK, 0), (TURN_H,), (SHRINK, 1), (SHRINK, 2),
    (SHRINK, 3), (NORM_2,), (LAST,),
)
BACKWARD_ORDER = (
    (OUTER_W, 0), (OUTER_W, 1), (OUTER_W, 2), (OUTER_W, 3), (SEND, 1, 3), (INNER, 0), (SEND, 1, 0), (INNER, 1),
    (INNER, 2), (INNER, 3), (INNER, 4), (INNER, 5), (INNER, 6), (INNER, 7), (HIDDEN, 0), (HIDDEN, 1), (SEND, 1, 2),
    (HIDDEN, 2), (HIDDEN, 3), (SEND, 1, 1), (INNER_W, 0), (SEND, 2, 0), (INNER_W, 1), (INNER_W, 2), (SEND, 2, 1),
    (NORM_BACK,), (SEND, 2, 2), (LINE_STEP, 0, 0), (ADD_A, 1, 0), (ADD_B, 1, 0), (INNER_W, 3), (MIXED, 0),
    (SEND, 2, 3), (ADD_B, 2, 0), (MIXED, 1), (ATTN_W, 0), (ATTEND, 0, 0), (ATTN_W, 1), (SEND, 5, 0), (ATTEND, 0, 1),
    (SEND, 5, 1), (ATTEND, 0, 2), (ADD_A, 2, 0), (ATTEND, 0, 3), (ATTEND, 0, 4), (ATTEND, 1, 0), (ADD_A, 1, 2),
    (ATTEND, 1, 1), (ATTEND, 1, 2), (ATTEND, 1, 3), (ATTEND, 1, 4), (ADD_A, 2, 1), (LINE_STEP, 0, 1),
    (LINE_STEP, 0, 2), (ATTEND, 2, 0), (ADD_B, 2, 1), (ADD_A, 1, 1), (ATTEND, 2, 1), (ATTEND, 2, 2), (ATTEND, 2, 3),
    (ATTEND, 2, 4), (ADD_B, 2, 2), (ATTEND, 3, 0), (ADD_A, 2, 2), (ADD_B, 5, 0), (ATTEND, 3, 1), (ATTEND, 3, 2),
    (ATTN_W, 2), (ATTEND, 3, 3), (ADD_A, 5, 1), (ADD_B, 1, 1), (ATTEND, 3, 4), (QKV_W, 0), (SEND, 5, 2), (SEND, 4, 0),
    (ATTN_W, 3), (QKV_W, 1), (SEND, 3, 1), (SEND, 3, 0), (QKV_W, 2), (PLACE_OUT,), (QKV_W, 3), (SEND, 4, 3),
    (INPUT, 0), (SEND, 4, 2), (ADD_B, 5, 1), (ADD_B, 2, 3), (ADD_A, 5, 0), (ADD_A, 4, 0), (SUMS,), (SUM_UP, 2, 0),
    (ADD_A, 3, 1), (ADD_B, 1, 2), (INPUT, 1), (INPUT, 2), (ADD_A, 5, 2), (ADD_B, 5, 2), (ADD_B, 4, 0), (SEND, 4, 1),
    (ADD_A, 3, 0), (INPUT, 3), (SEND, 3, 2), (LINE_STEP, 0, 3), (ADD_B, 3, 0), (SEND, 0, 3), (SUM_UP, 2, 1),
    (SEND, 3, 3), (ADD_A, 2, 3), (ADD_A, 4, 3), (SUM_UP, 1, 0), (ADD_B, 4, 1), (SEND, 5, 3), (ADD_B, 3, 1),
    (SUM_UP, 5, 0), (SUM_UP, 2, 2), (ADD_A, 4, 1), (ADD_A, 0, 3), (ADD_B, 1, 3), (SUM_UP, 1, 1), (ADD_B, 0, 3),
    (ADD_A, 1, 3), (ADD_B, 4, 2), (INPUT_LAST,), (SUM_UP, 3, 0), (ADD_B, 3, 3), (ADD_A, 4, 2), (SUM_UP, 5, 1),
    (SUM_UP, 5, 2), (ADD_B, 5, 3), (ADD_B, 3, 2), (SUM_UP, 2, 3), (ADD_A, 5, 3), (SUM_UP, 4, 0), (SUMS_X,),
    (SUM_UP, 1, 2), (ADD_A, 3, 2), (SUM_UP, 0, 3), (SUM_UP, 3, 1), (ADD_A, 3, 3), (SUM_UP, 4, 1), (PLACE_INPUT,),
    (ADD_B, 4, 3), (SUM_UP, 5, 3), (BACK_Y, 2), (BACK_X, 2), (SUM_UP, 3, 2), (BACK_Y, 0), (SUM_UP, 4, 2), (BACK_X, 0),
    (SUM_UP, 1, 3), (SUMS_Y,), (SUM_UP, 3, 3), (SUM_UP, 4, 3), (SUMS_LINE,), (BACK_X, 5), (BACK_Y, 3), (BACK_X, 3),
    (BACK_X, 1), (BACK_Y, 1), (BACK_Y, 4), (BACK_Y, 5), (BACK_X, 4),
)


F32, LOW = jnp.float32, jnp.bfloat16
ANYWHERE = pl.BlockSpec(memory_space=pl.ANY)
IN_VMEM = pl.BlockSpec(memory_space=pltpu.VMEM)
LANES = 128
BLOCK = 32


def at(start, size):
    return pl.ds(pl.multiple_of(start * size, size), size)


def dot(a, b):
    return jnp.dot(a, b, preferred_element_type=F32)


def dot_t(a, b):
    return lax.dot_general(a, b, (((1,), (1,)), ((), ())), preferred_element_type=F32)


def loop(count, body):
    def step(i, carry):
        body(i)
        return carry

    lax.fori_loop(0, count, step, 0)


def head_lanes(half, dtype):
    lane = lax.broadcasted_iota(jnp.int32, (1, LANES), 1)
    return jnp.where((lane < HD) == (half == 0), 1.0, 0.0).astype(dtype)


def fold(values):
    return jnp.sum(values.reshape(values.shape[0] // 8, 8, values.shape[1]), 0)


def forward_kernel(*refs):
    it = iter(refs)

    def take(n):
        return [next(it) for _ in range(n)]

    x, ct, wq, wk, wv, wo_s, wi_s, wout_s = take(8)
    seg, bq, bv, bi = take(4)
    small = take(6)
    out_w = take(GROUPS)
    o_xt, o_qkv, o_probs, o_mixed_t, o_unit, o_inv, o_h_t, o_slope, o_act_t, o_dpre, o_dout, o_pars, o_out, o_sums = take(14)
    bufs = take(GROUPS)
    xs, cts, pars4, pars, qkv, qkv_bias, probs, mask, mixed, part, recv1, recv2 = take(12)
    unit, inv, h1, h_low, inner, slope, act, act_t, h_t, x_t, mixed_t, dpre, dout, out, sums = take(15)
    tok_sems, gat_sems = take(len(Tokens.SEMS)), take(len(Gather.SEMS))
    core_s, core_r, save = take(3)

    spot = Spot()
    gather = Gather(spot, ((wq, wk, wv), (wo_s,), (wi_s,), (wout_s,)), bufs, gat_sems)
    tokens = Tokens(spot, x, ct, xs, cts, pars4, tok_sems)
    wqkv, wo, wi, wout = bufs
    seq, width = xs.shape
    own = seq // 2
    half = qkv.shape[1] // 3
    mine, theirs = spot.col * own, (1 - spot.col) * own

    def rows_of(base, start, size):
        return pl.ds(pl.multiple_of(base + start * size, size), size)

    gather.load()
    pars4[spot.row] = jnp.zeros(pars4.shape[1:], F32)
    for i, p in enumerate(small):
        pars4[spot.row, pl.ds(i, 1), :] = p[...].astype(F32).reshape(1, -1)
    greet(spot)

    saves = []

    def keep(src, dst):
        c = pltpu.make_async_copy(src, dst, save.at[len(saves)])
        c.start()
        saves.append(c)

    def to_other(n, src, dst):
        return remote(src, dst, core_s.at[n], core_r.at[n], spot.other_core)

    def make_mask():
        values = seg[...].astype(F32)
        for i in range(seq // LANES):
            down = jnp.broadcast_to(values[:, i * LANES : (i + 1) * LANES], (LANES, LANES)).T
            for j in range(seq // LANES):
                across = values[:, j * LANES : (j + 1) * LANES]
                mask[pl.ds(i * LANES, LANES), pl.ds(j * LANES, LANES)] = jnp.where(down == across, 0.0, -1e30)
        qkv_bias[:, pl.ds(0, half)] = jnp.broadcast_to(bq[...].astype(F32).reshape(1, half), (8, half))
        qkv_bias[:, pl.ds(half, half)] = jnp.zeros((8, half), F32)
        qkv_bias[:, pl.ds(2 * half, half)] = jnp.broadcast_to(bv[...].astype(F32).reshape(1, half), (8, half))

    def spread_pars():
        for r in range(LINE):
            pars[:, pl.ds(r * (width // LINE), width // LINE)] = pars4[r]

    def project(n):
        def chunk(c):
            cols = at(c, 256)
            w = wqkv[:, :, cols].reshape(width, 256)
            value = (dot(xs[...], w) + qkv_bias[0:1, cols]).astype(LOW).astype(F32)
            qkv[:, cols] = (value * jnp.where(c < half // 256, 0.125, 1.0)).astype(LOW)

        chunk(n)

    def transpose_x():
        loop(width // LANES, lambda c: x_t.__setitem__((at(c, LANES), slice(None)), xs[:, at(c, LANES)].T))

    def attend(pair, i):
        lanes = pl.ds(pair * LANES, LANES)
        keys = qkv[:, pl.ds(half + pair * LANES, LANES)]
        values = qkv[:, pl.ds(2 * half + pair * LANES, LANES)]

        def block(i):
            rows = at(i, LANES)
            queries = qkv[rows, lanes]

            def head(h, total):
                scores = dot_t(queries * head_lanes(h, LOW), keys) + mask[rows, :]
                expo = jnp.exp(scores - jnp.max(scores, 1, keepdims=True))
                p = (expo / jnp.sum(expo, 1, keepdims=True)).astype(LOW)
                probs[2 * pair + h, rows, :] = p
                return total + dot(p, values) * head_lanes(h, F32)

            total = lax.fori_loop(0, 2, head, jnp.zeros((LANES, LANES), F32))
            mixed[rows, lanes] = total.astype(LOW)

        block(i)
        if i == seq // LANES - 1:
            mixed_t[lanes, :] = mixed[:, lanes].T

    def attn_out(r):
        part[:, pl.ds(r * 256, 256)] = dot(mixed[...], wo[r])

    def first_norm():
        def block(i):
            rows, there = at(i, BLOCK), rows_of(mine, i, BLOCK)
            value = xs[there, :].astype(F32) + (part[there, :] + recv1[rows, :] + pars[0:1, :])
            centred = value - jnp.mean(value, 1, keepdims=True)
            scale = lax.rsqrt(jnp.mean(centred * centred, 1, keepdims=True) + norm_eps)
            one = centred * scale
            unit[rows, :] = one
            inv[rows, :] = jnp.broadcast_to(scale, (BLOCK, LANES))
            h = one * pars[1:2, :] + pars[2:3, :]
            h1[rows, :] = h
            h_low[there, :] = h.astype(LOW)

        loop(own // BLOCK, block)

    def transpose_h():
        loop(width // LANES, lambda c: h_t.__setitem__((at(c, LANES), slice(None)), h_low[:, at(c, LANES)].T))

    def grow(c):
        cols = at(c, 256)
        inner[...] = dot(h_low[...], wi[:, :, cols].reshape(width, 256))
        bias = bi[cols].astype(F32).reshape(1, 256)

        def block(i):
            rows = at(i, 64)
            v = inner[rows, :] + bias
            cdf = 0.5 * (1.0 + lax.erf(v * inv_root_two))
            slope[rows, cols] = cdf + v * (jnp.exp(-0.5 * v * v) * inv_root_two_pi)
            act[rows, cols] = (v * cdf).astype(LOW)

        loop(seq // 64, block)
        act_t[cols, :] = act[:, cols].T

    def shrink(r):
        part[:, at(r, 256)] = dot(act[...], wout[r])

    def second_norm():
        sums[...] = jnp.zeros_like(sums)

        def block(i):
            rows, there = at(i, BLOCK), rows_of(mine, i, BLOCK)
            value = h1[rows, :] + (part[there, :] + recv2[rows, :] + pars[3:4, :])
            centred = value - jnp.mean(value, 1, keepdims=True)
            scale = lax.rsqrt(jnp.mean(centred * centred, 1, keepdims=True) + norm_eps)
            one = centred * scale
            out[rows, :] = (one * pars[4:5, :] + pars[5:6, :]).astype(LOW)
            dy = cts[rows, :].astype(F32)
            s = dy * pars[4:5, :]
            d = scale * (s - jnp.mean(s, 1, keepdims=True) - one * jnp.mean(s * one, 1, keepdims=True))
            dpre[rows, :] = d
            d_low = d.astype(LOW)
            dout[there, :] = d_low
            sums[0] += fold(d_low.astype(F32))
            sums[1] += fold(dy * one)
            sums[2] += fold(dy)

        loop(own // BLOCK, block)

    seen = set()

    def once(*what):
        new = what not in seen
        seen.add(what)
        return new

    def arrived(which, turns=range(LINE - 1)):
        for g in range(len(GATHERED)):
            for n in turns:
                if GATHERED[g][0] == which and once("arrived", g, n):
                    gather.arrive(g, n)

    def relayed():
        if once("relayed"):
            tokens.wait_relayed()

    their_half = part.at[pl.ds(pl.multiple_of(theirs, own), own)]
    my_rows = pl.ds(pl.multiple_of(mine, own), own)
    first, second = to_other(0, their_half, recv1), to_other(2, their_half, recv2)
    pass_h, pass_d = to_other(1, *[h_low.at[my_rows]] * 2), to_other(3, *[dout.at[my_rows]] * 2)

    def hidden_there():
        if once("hidden"):
            pass_h.wait_recv()

    def do(what, *n):
        if what == OWN:
            gather.start_own(*n)
        elif what == TOKENS_IN:
            tokens.start_x()
            tokens.start_par()
        elif what == COTANGENT_IN:
            tokens.start_ct()
        elif what == ALONG:
            gather.z_step(*n)
        elif what == FROM_X:
            gather.x_step(*n)
        elif what == FROM_Y:
            gather.y_step(*n)
        elif what == TO_CORE:
            tokens.wait_x()
        elif what == TURN_X:
            relayed()
            transpose_x()
            keep(x_t, o_xt)
        elif what == PROJECT:
            relayed()
            arrived(0)
            project(*n)
            if n[0] == 5:
                keep(wqkv, out_w[0])
                keep(qkv, o_qkv)
        elif what == ATTEND:
            attend(*n)
            if n == (3, 3):
                keep(probs, o_probs)
                keep(mixed_t, o_mixed_t)
        elif what == ATTN_OUT:
            arrived(1)
            attn_out(*n)
            if n[0] == LINE - 1:
                keep(wo, out_w[1])
                first.start()
        elif what == NORM_1:
            tokens.wait_par()
            spread_pars()
            keep(pars, o_pars)
            first.wait_recv()
            first_norm()
            pass_h.start()
            keep(unit, o_unit)
            keep(inv, o_inv)
        elif what == TURN_H:
            hidden_there()
            transpose_h()
            keep(h_t, o_h_t)
        elif what == GROW:
            hidden_there()
            arrived(2)
            grow(*n)
            if n[0] == hidden // 256 - 1:
                keep(wi, out_w[2])
                keep(slope, o_slope)
                keep(act_t, o_act_t)
        elif what == SHRINK:
            if n[0]:
                arrived(3, (n[0] - 1,))
            elif once("sent"):
                first.wait_send()
            row = spot.near[n[0] - 1] if n[0] else spot.row
            shrink(row)
            keep(wout.at[row], out_w[3].at[row])
            if n[0] == LINE - 1:
                second.start()
        elif what == NORM_2:
            tokens.wait_ct()
            second.wait_recv()
            second_norm()
            pass_d.start()
            keep(dpre, o_dpre)
            keep(out, o_out)
            keep(sums, o_sums)
        elif what == LAST:
            pass_d.wait_recv()
            keep(dout, o_dout)

    hidden = act.shape[1]
    make_mask()
    for step in FORWARD_ORDER:
        do(*step)
    for c in (second, pass_h, pass_d):
        c.wait_send()
    gather.drain()
    tokens.drain()
    for c in saves:
        c.wait()


def forward(x, ct, wq, wk, wv, wo, wi, wout, seg, bq, bv, bi, small):
    half, hidden = wq.shape[1], wi.shape[1]
    seq, width = x.shape[0] // 2, MODEL_WIDTH
    own, heads = seq // 2, half // HD
    weights = [((LINE, wq.shape[0], 3 * half), LOW), ((LINE,) + wo.shape, LOW), ((LINE,) + wi.shape, LOW), ((LINE,) + wout.shape, LOW)]
    named = dict(
        xs=((seq, width), LOW), cts=((own, width), LOW), pars4=((LINE, 8, width // LINE), F32), pars=((8, width), F32),
        qkv=((seq, 3 * half), LOW), qkv_bias=((8, 3 * half), F32), probs=((heads, seq, seq), LOW), mask=((seq, seq), F32),
        mixed=((seq, half), LOW), part=((seq, width), F32), recv1=((own, width), F32), recv2=((own, width), F32),
        unit=((own, width), F32), inv=((own, LANES), F32), h1=((own, width), F32), h_low=((seq, width), LOW),
        inner=((seq, 256), F32), slope=((seq, hidden), F32), act=((seq, hidden), LOW), act_t=((hidden, seq), LOW),
        h_t=((width, seq), LOW), x_t=((width, seq), LOW), mixed_t=((half, seq), LOW), dpre=((own, width), F32),
        dout=((seq, width), LOW), out=((own, width), LOW), sums=((3, 8, width), F32),
    )
    saved = ("x_t", "qkv", "probs", "mixed_t", "unit", "inv", "h_t", "slope", "act_t", "dpre", "dout", "pars", "out", "sums")
    outs = weights + [named[n] for n in saved]
    res = pl.pallas_call(
        forward_kernel,
        name="forward",
        out_shape=[jax.ShapeDtypeStruct(*o) for o in outs],
        in_specs=[ANYWHERE] * 8 + [IN_VMEM] * (4 + len(small)),
        out_specs=[ANYWHERE] * len(outs),
        scratch_shapes=[pltpu.VMEM(*w) for w in weights]
        + [pltpu.VMEM(*named[n]) for n in named]
        + Tokens.SEMS
        + Gather.SEMS
        + [pltpu.SemaphoreType.DMA((4,)), pltpu.SemaphoreType.DMA((4,)), pltpu.SemaphoreType.DMA((len(outs) + LINE,))],
        compiler_params=pltpu.CompilerParams(collective_id=0, has_side_effects=True, vmem_limit_bytes=60 * 2**20),
    )(x, ct, wq, wk, wv, wo, wi, wout, seg, bq, bv, bi, *small)
    return res[:GROUPS], dict(zip(saved, res[GROUPS:]))


class Sums:
    SEMS = [pltpu.SemaphoreType.DMA((3,)), pltpu.SemaphoreType.DMA((3,)), pltpu.SemaphoreType.DMA((LINE,)), pltpu.SemaphoreType.DMA((LINE,))]

    def __init__(self, spot, vec, from_core, with_x, from_x, with_y, from_y, from_line, sems):
        self.spot, self.vec, self.from_core, self.with_x = spot, vec, from_core, with_x
        self.from_x, self.with_y, self.from_y, self.from_line = from_x, with_y, from_y, from_line
        self.s, self.r, self.z_s, self.z_r = sems

    def hop(self, n):
        s = self.spot
        src, dst, to = (
            (self.vec.at[pl.ds(0, 8)], self.from_core, s.other_core),
            (self.with_x, self.from_x, s.beside_x),
            (self.with_y, self.from_y, s.beside_y),
        )[n]
        return remote(src, dst, self.s.at[n], self.r.at[n], to)

    def line(self, away):
        s = self.spot
        row = lax.rem(s.row + away, LINE)
        return remote(self.from_line.at[s.row], self.from_line.at[s.row], self.z_s.at[away], self.z_r.at[s.row], s.at_row(row))

    def step(self, n):
        if n == 0:
            self.hop(0).start()
        elif n == 1:
            self.hop(0).wait_recv()
            self.with_x[pl.ds(0, 8), :] = self.vec[pl.ds(0, 8), :] + self.from_core[...]
            self.with_x[pl.ds(8, 8), :] = self.vec[pl.ds(8, 8), :]
            self.hop(1).start()
        elif n == 2:
            self.hop(1).wait_recv()
            self.with_y[...] = self.with_x[...] + self.from_x[...]
            self.hop(2).start()
        elif n == 3:
            self.hop(2).wait_recv()
            self.from_line[self.spot.row] = self.with_y[...] + self.from_y[...]
            for away in range(1, LINE):
                self.line(away).start()

    def total(self):
        s = self.spot
        for row in s.near:
            block = self.from_line.at[row]
            pltpu.make_async_copy(block, block, self.z_r.at[row]).wait()
        return self.from_line[0] + self.from_line[1] + self.from_line[2] + self.from_line[3]

    def drain(self):
        for n in range(3):
            self.hop(n).wait_send()
        for away in range(1, LINE):
            self.line(away).wait_send()


SAVED = ("x_t", "qkv", "probs", "mixed_t", "unit", "inv", "h_t", "slope", "act_t", "dpre", "dout", "pars", "out")


def backward_kernel(*refs):
    it = iter(refs)

    def take(n):
        return [next(it) for _ in range(n)]

    wqkv_h, wo_h, wi_h, wout_h = take(GROUPS)
    saved = dict(zip(SAVED, take(len(SAVED))))
    (sums2,) = take(1)
    final = take(GROUPS)
    placed_out, placed_dx, o_norms, o_bias = take(4)
    wo, wi, wout, wst = take(4)
    parts = take(GROUPS)
    rel_a, rel_b, from_x, from_y, line, stage = (take(len(SCATTERED)) for _ in range(6))
    act_t, dout, h_t, dpre, unit, inv, pars, mixed_t, qkv = take(9)
    slope, probs, ds, dinner, part, recv1, recv2, dattn, dmixed, dqkv, dx = take(11)
    vecs = take(7)
    scat_sems, sum_sems = take(len(Scatter.SEMS)), take(len(Sums.SEMS))
    out_sems, dx_sems = take(2), take(2)
    core_s, core_r, load, st_sem, sl_sem, pr_sem = take(6)

    spot = Spot()
    scatter = Scatter(spot, parts, rel_a, rel_b, from_x, from_y, line, stage, final, scat_sems)
    totals = Sums(spot, *vecs, sum_sems)
    vec = vecs[0]
    place_out, place_dx = Spread(spot, saved["out"], placed_out, out_sems), Spread(spot, dx, placed_dx, dx_sems)
    seq, width = dout.shape
    hidden = dinner.shape[1]
    half = qkv.shape[1] // 3
    own = seq // 2
    cut = width // LINE
    mine, theirs = spot.col * own, (1 - spot.col) * own

    def rows_of(base, start, size):
        return pl.ds(pl.multiple_of(base + start * size, size), size)

    fetches = {}

    def fetch(name, src, dst):
        fetches[name] = pltpu.make_async_copy(src, dst, load.at[len(fetches)])
        fetches[name].start()

    def to_other(n, src, dst):
        return remote(src, dst, core_s.at[n], core_r.at[n], spot.other_core)

    def wout_grad(f):
        rows = at(f, 512)
        for r in range(LINE):
            parts[0][r, rows, :] = dot(act_t[rows, :], dout[:, pl.ds(r * cut, cut)]).astype(LOW)

    def slope_copy(f):
        slot = f % 2
        return pltpu.make_async_copy(saved["slope"].at[:, at(f, 256)], slope.at[slot], sl_sem.at[slot])

    def inner_grad(f):
        rows = at(f, 256)

        if f + 1 < hidden // 256:
            slope_copy(f + 1).start()

        total = dot_t(dout[:, pl.ds(0, cut)], wout[0, rows, :])
        for r in range(1, LINE):
            total += dot_t(dout[:, pl.ds(r * cut, cut)], wout[r, rows, :])
        slope_copy(f).wait()
        part[:, pl.ds(0, 256)] = total
        part[pl.ds(0, 8), pl.ds(256, 256)] = jnp.zeros((8, 256), F32)

        def block(i):
            here = at(i, 64)
            d = (part[here, pl.ds(0, 256)] * slope[f % 2, here, :]).astype(LOW)
            dinner[here, rows] = d
            part[pl.ds(0, 8), pl.ds(256, 256)] += fold(d.astype(F32))

        loop(seq // 64, block)
        row, col = f // 4, f % 4
        vec[pl.ds(9 + row, 1), at(col, 256)] = jnp.sum(part[pl.ds(0, 8), pl.ds(256, 256)], 0, keepdims=True)

    def hidden_grad(r):
        part[:, at(r, cut)] = dot_t(dinner[...], wi[r])

    def wi_grad(t):
        row = scatter.order[t]

        def chunk(n):
            cols = at(n, 512)
            parts[1][row, :, cols] = dot(h_t[at(row, cut), :], dinner[:, cols]).astype(LOW)

        loop(hidden // 512, chunk)

    def first_norm_back():
        part_sums = jnp.zeros((8, width), F32)

        def block(i, carry):
            b_sum, g_sum, s_sum = carry
            rows, there = at(i, BLOCK), rows_of(mine, i, BLOCK)
            dh = dpre[rows, :] + (part[there, :] + recv1[rows, :])
            one = unit[rows, :]
            s = dh * pars[1:2, :]
            scale = inv[rows, :][:, 0:1]
            d = scale * (s - jnp.mean(s, 1, keepdims=True) - one * jnp.mean(s * one, 1, keepdims=True))
            dpre[rows, :] = d
            d_low = d.astype(LOW)
            dattn[there, :] = d_low
            return b_sum + fold(d_low.astype(F32)), g_sum + fold(dh * one), s_sum + fold(dh)

        b_sum, g_sum, s_sum = lax.fori_loop(0, own // BLOCK, block, (part_sums, part_sums, part_sums))
        for i, v in enumerate((b_sum, g_sum, s_sum)):
            vec[pl.ds(i, 1), :] = jnp.sum(v, 0, keepdims=True)

    def mixed_grad(n):
        rows = at(n, 256)
        total = dot_t(dattn[:, pl.ds(0, cut)], wo[0, rows, :])
        for r in range(1, LINE):
            total += dot_t(dattn[:, pl.ds(r * cut, cut)], wo[r, rows, :])
        dmixed[:, rows] = total.astype(LOW)

    def wo_grad(r):
        parts[2][r] = dot(mixed_t[...], dattn[:, at(r, cut)]).astype(LOW)

    def probs_copy(head):
        return pltpu.make_async_copy(saved["probs"].at[head], probs.at[head % 4], pr_sem.at[head % 4])

    def attend_back(pair, i):
        lanes = pl.ds(pair * LANES, LANES)
        keys_at, values_at = pl.ds(half + pair * LANES, LANES), pl.ds(2 * half + pair * LANES, LANES)
        slots = [(2 * pair + h) % 4 for h in range(2)]

        def block(i):
            rows = at(i, LANES)
            grad = dmixed[rows, lanes]

            def head(h, total):
                dp = dot_t(grad * head_lanes(h, LOW), qkv[:, values_at])
                p = probs[slots[0] + h, rows, :].astype(F32)
                d = (p * (dp - jnp.sum(p * dp, 1, keepdims=True))).astype(LOW)
                ds[h, rows, :] = d
                return total + dot(d, qkv[:, keys_at]) * head_lanes(h, F32)

            total = lax.fori_loop(0, 2, head, jnp.zeros((LANES, LANES), F32))
            dqkv[rows, lanes] = (total * 0.125).astype(LOW)

        if i < seq // LANES:
            block(i)
            return
        queries_t, grad_t = qkv[:, lanes].T, dmixed[:, lanes].T
        dk = jnp.concatenate([dot(queries_t[h * HD : (h + 1) * HD], ds[h]) for h in range(2)], 0)
        dqkv[:, keys_at] = dk.astype(LOW).T
        dv = jnp.concatenate([dot(grad_t[h * HD : (h + 1) * HD], probs[slots[h]]) for h in range(2)], 0)
        dqkv[:, values_at] = dv.astype(LOW).T

    def qkv_sums():
        for i, base in enumerate((0, 2 * half)):
            cols = pl.ds(base, half)

            def block(n, carry):
                return carry + fold(dqkv[at(n, 64), cols].astype(F32))

            v = lax.fori_loop(0, seq // 64, block, jnp.zeros((8, half), F32))
            vec[pl.ds(8, 1), pl.ds(i * half, half)] = jnp.sum(v, 0, keepdims=True)

    def wqkv_grad(t):
        row = scatter.order[t]

        def chunk(n):
            cols = at(n, 512)
            parts[3][row, :, cols] = dot(h_t[at(row, cut), :], dqkv[:, cols]).astype(LOW)

        loop(3 * half // 512, chunk)

    def weight_copy(r):
        return pltpu.make_async_copy(wqkv_h.at[r], wst.at[r % 2], st_sem.at[r % 2])

    def input_grad(r):
        weight_copy(r).wait()
        part[:, pl.ds(r * cut, cut)] = dot_t(dqkv[...], wst[r % 2])
        if r + 2 < LINE:
            weight_copy(r + 2).start()

    def finish_input():
        def block(i):
            rows, there = at(i, BLOCK), rows_of(mine, i, BLOCK)
            dx[rows, :] = (dpre[rows, :] + (part[there, :] + recv2[rows, :])).astype(LOW)

        loop(own // BLOCK, block)

    their_half = part.at[pl.ds(pl.multiple_of(theirs, own), own)]
    my_rows = pl.ds(pl.multiple_of(mine, own), own)

    swap1, swap2 = to_other(0, their_half, recv1), to_other(2, their_half, recv2)
    pass_d = to_other(1, dattn.at[my_rows], dattn.at[my_rows])
    seen = set()

    def once(*what):
        new = what not in seen
        seen.add(what)
        return new

    def need(*names):
        for n in names:
            if once("fetched", n):
                fetches[n].wait()

    def do(what, *n):
        if what == SEND:
            scatter.first(*n)
            scatter.direct(*n)
        elif what == ADD_A:
            scatter.second_a(*n)
        elif what == ADD_B:
            scatter.second_b(*n)
        elif what == SUM_UP:
            scatter.third(*n)
        elif what == LINE_STEP:
            scatter.line_step(*n)
        elif what == BACK_X:
            scatter.fourth_x(*n)
        elif what == BACK_Y:
            scatter.fourth_y(*n)
        elif what == OUTER_W:
            wout_grad(*n)
        elif what == INNER:
            need("wout")
            inner_grad(*n)
        elif what == HIDDEN:
            need("wi")
            hidden_grad(*n)
            if n[0] == LINE - 1:
                swap1.start()
        elif what == INNER_W:
            need("h_t")
            wi_grad(*n)
            if n[0] == LINE - 1:
                fetch("x_t", saved["x_t"], h_t)
        elif what == NORM_BACK:
            need("dpre", "unit", "inv", "pars")
            swap1.wait_recv()
            first_norm_back()
            pass_d.start()
        elif what == MIXED:
            need("wo")
            if once("passed"):
                pass_d.wait_recv()
            mixed_grad(*n)
        elif what == ATTN_W:
            need("mixed_t")
            wo_grad(scatter.order[n[0]])
        elif what == ATTEND:
            need("qkv")
            pair, i = n
            if i == 0:
                for h in range(2):
                    probs_copy(2 * pair + h).wait()
            attend_back(pair, i)
            if i == seq // LANES:
                for h in range(2):
                    if 2 * pair + h + 4 < half // HD:
                        probs_copy(2 * pair + h + 4).start()
        elif what == QKV_W:
            need("x_t")
            wqkv_grad(*n)
        elif what == INPUT:
            if n[0] == 0:
                swap1.wait_send()
            input_grad(*n)
            if n[0] == LINE - 1:
                swap2.start()
        elif what == SUMS:
            qkv_sums()
            totals.step(0)
        elif what in (SUMS_X, SUMS_Y, SUMS_LINE):
            totals.step(1 + what - SUMS_X)
        elif what == INPUT_LAST:
            swap2.wait_recv()
            finish_input()
        elif what == PLACE_OUT:
            place_out.start()
        elif what == PLACE_INPUT:
            place_dx.start()

    fetch("dout", saved["dout"], dout)
    fetch("act_t", saved["act_t"], act_t)
    greet(spot)
    need("dout", "act_t")
    fetch("wout", wout_h, wout)
    slope_copy(0).start()
    fetch("wi", wi_h, wi)
    fetch("h_t", saved["h_t"], h_t)
    for name, dst in (("dpre", dpre), ("unit", unit), ("inv", inv), ("pars", pars)):
        fetch(name, saved[name], dst)
    fetch("wo", wo_h, wo)
    fetch("mixed_t", saved["mixed_t"], mixed_t)
    fetch("qkv", saved["qkv"], qkv)
    for head in range(4):
        probs_copy(head).start()
    weight_copy(0).start()
    weight_copy(1).start()
    vec[...] = jnp.zeros_like(vec)
    for i in range(3):
        vec[pl.ds(3 + i, 1), :] = jnp.sum(sums2[i], 0, keepdims=True)
    for step in BACKWARD_ORDER:
        do(*step)
    whole = totals.total()
    totals.drain()
    for i in range(8):
        o_bias[pl.ds(i, 1), :] = whole[8 + i : 9 + i, :]
    vecs[-1][0] = whole
    o_norms[...] = vecs[-1][0, pl.ds(0, 8), at(spot.row, cut)]
    for g in range(len(SCATTERED)):
        scatter.fifth(g)
    scatter.drain()
    for c in (swap2, pass_d):
        c.wait_send()
    place_out.wait()
    place_dx.wait()


def backward(weights, saved):
    wqkv, wo, wi, wout = weights
    shapes = [w.shape for w in (wout, wi, wo, wqkv)]
    seq, width = saved["dout"].shape
    half, hidden, own = wo.shape[1], wi.shape[2], seq // 2
    cut = width // LINE

    groups = Scatter.sizes(shapes)

    def each(f):
        return [pltpu.VMEM(f(*s), LOW) for s in groups]

    def like(name):
        return pltpu.VMEM(saved[name].shape, saved[name].dtype)

    placed = jax.ShapeDtypeStruct((2 * seq, cut), LOW)
    scratch = (
        [pltpu.VMEM(w.shape, LOW) for w in (wo, wi, wout)]
        + [pltpu.VMEM((2,) + wqkv.shape[1:], LOW)]
        + [pltpu.VMEM(s, LOW) for s in shapes]
        + each(lambda r, c, n: (n, r // 8, c)) * 2
        + each(lambda r, c, n: (n, r // 4, c)) * 2
        + each(lambda r, c, n: (LINE + 1, r if n == 1 else r // 4, c))
        + each(lambda r, c, n: (r // 4, c))
        + [like(n) for n in ("act_t", "dout", "h_t", "dpre", "unit", "inv", "pars", "mixed_t", "qkv")]
        + [
            pltpu.VMEM((2, seq, 256), F32), pltpu.VMEM((4, seq, seq), LOW), pltpu.VMEM((2, seq, seq), LOW),
            pltpu.VMEM((seq, hidden), LOW), pltpu.VMEM((seq, width), F32), pltpu.VMEM((own, width), F32),
            pltpu.VMEM((own, width), F32), pltpu.VMEM((seq, width), LOW), pltpu.VMEM((seq, half), LOW),
            pltpu.VMEM((seq, 3 * half), LOW), pltpu.VMEM((own, width), LOW),
        ]
        + [pltpu.VMEM(s, F32) for s in ((16, width), (8, width)) + ((16, width),) * 4 + ((LINE, 16, width),)]
        + Scatter.SEMS
        + Sums.SEMS
        + Spread.SEMS * 2
        + [pltpu.SemaphoreType.DMA((n,)) for n in (3, 3, 16, 2, 2, 4)]
    )
    res = pl.pallas_call(
        backward_kernel,
        name="backward",
        out_shape=[jax.ShapeDtypeStruct(s[1:], LOW) for s in shapes]
        + [placed] * 2
        + [jax.ShapeDtypeStruct((8, cut), F32), jax.ShapeDtypeStruct((8, width), F32)],
        in_specs=[ANYWHERE] * (GROUPS + len(SAVED)) + [IN_VMEM],
        out_specs=[ANYWHERE] * (GROUPS + 2) + [IN_VMEM] * 2,
        scratch_shapes=scratch,
        compiler_params=pltpu.CompilerParams(collective_id=1, has_side_effects=True, vmem_limit_bytes=63 * 2**20),
    )(*weights, *[saved[n] for n in SAVED], saved["sums"])
    return res


def finish_kernel(wqkv, wo, wi, wout, out, dx, norms, biases, *outs):
    wq_o, wk_o, wv_o, wo_o, wi_o, wout_o, out_o, dx_o, bq_o, bv_o, bi_o = outs[:11]
    half = wq_o.shape[1]
    for i, o in enumerate((wq_o, wk_o, wv_o)):
        o[...] = wqkv[:, i * half : (i + 1) * half].astype(F32)
    for src, dst in ((wo, wo_o), (wi, wi_o), (wout, wout_o)):
        dst[...] = src[...].astype(F32)
    out_o[...] = out[...]
    dx_o[...] = dx[...]

    @pl.when(pl.program_id(0) == 0)
    def _():
        bq_o[...] = biases[0, 0:half]
        bv_o[...] = biases[0, half : 2 * half]
        wide = biases.shape[1]
        for i in range(bi_o.shape[0] // wide):
            bi_o[i * wide : (i + 1) * wide] = biases[1 + i, :]
        for i, o in enumerate(outs[11:]):
            o[...] = norms[i, :]


def finish(wqkv, wo, wi, wout, out, dx, norms, biases, steps=4):
    half, cut = wqkv.shape[1] // 3, norms.shape[1]
    big = [(wqkv.shape[0], half)] * 3 + [w.shape for w in (wo, wi, wout)]

    def tiled(shape):
        return pl.BlockSpec((shape[0] // steps, shape[1]), lambda i: (i, 0))

    def whole(shape):
        return pl.BlockSpec(shape, lambda i: (0,) * len(shape))

    vectors = [(half,), (half,), (wi.shape[1],)] + [(cut,)] * 6
    return pl.pallas_call(
        finish_kernel,
        name="finish",
        grid=(steps,),
        out_shape=[jax.ShapeDtypeStruct(s, F32) for s in big]
        + [jax.ShapeDtypeStruct(v.shape, LOW) for v in (out, dx)]
        + [jax.ShapeDtypeStruct(s, F32) for s in vectors],
        in_specs=[tiled(v.shape) for v in (wqkv, wo, wi, wout, out, dx)] + [whole(norms.shape), whole(biases.shape)],
        out_specs=[tiled(s) for s in big] + [tiled(out.shape)] * 2 + [whole(s) for s in vectors],
        compiler_params=pltpu.CompilerParams(vmem_limit_bytes=63 * 2**20),
    )(wqkv, wo, wi, wout, out, dx, norms, biases)


def per_chip(
    hidden_in, segment_ids, query_weight, query_bias, key_weight, value_weight, value_bias, attn_out_weight,
    attn_out_bias, norm1_gain, first_norm_offset, inner_weight, inner_bias, outer_weight, outer_bias, norm2_gain,
    second_norm_offset, cotangent,
):
    half = query_weight.shape[1]
    small = (attn_out_bias, norm1_gain, first_norm_offset, outer_bias, norm2_gain, second_norm_offset)
    weights, saved = forward(
        hidden_in, cotangent, query_weight, key_weight, value_weight, attn_out_weight, inner_weight, outer_weight,
        segment_ids, query_bias, value_bias, inner_bias, small,
    )
    wout, wi, wo, wqkv, layer_out, input_grad, norms, biases = backward(weights, saved)
    wq, wk, wv, wo, wi, wout, layer_out, input_grad, bq, bv, bi, bo, g1, b1, bout, g2, b2 = finish(
        wqkv, wo, wi, wout, layer_out, input_grad, norms, biases
    )
    return layer_out, input_grad, wq, bq, wk, wv, bv, wo, bo, g1, b1, wi, bi, wout, bout, g2, b2


def solution(mesh):
    def whole(*args):
        segments, wq = args[1], args[2]
        sizes = tuple(mesh.shape[a] for a in ("dp", "row", "col"))
        fits = sizes == (4, LINE, 2) and segments.shape == (16, SEQ) and wq.shape[0] == MODEL_WIDTH
        body = per_chip if fits else shards
        return jax.shard_map(body, mesh=mesh, in_specs=IN_SPECS, out_specs=OUT_SPECS, check_vma=False)(*args)

    return whole
```

```python
import functools

import jax
import jax.numpy as jnp
from jax import lax
from jax.experimental import pallas as pl
from jax.experimental.pallas import tpu as pltpu
from jax.sharding import PartitionSpec as P

MODEL_WIDTH = 1024
HD = 64
SEQ = 512


norm_eps = 1e-12
inv_root_two = 0.7071067811865476
inv_root_two_pi = 0.3989422804014327


def product(left, right):
    return jnp.dot(left, right, preferred_element_type=jnp.float32)


def over_tokens(left, right):
    return lax.dot_general(
        left, right, (((0,), (0,)), ((), ())), preferred_element_type=jnp.float32
    )


def against(left, right):
    return lax.dot_general(
        left, right, (((1,), (1,)), ((), ())), preferred_element_type=jnp.float32
    )


def col_gather(values):
    return lax.all_gather(values, "col", axis=0, tiled=True)


def row_gather(values):
    return lax.all_gather(values, "row", axis=0, tiled=True)


def row_reduce(values):
    return lax.psum_scatter(values, "row", scatter_dimension=0, tiled=True)


def col_reduce(values):
    return lax.psum_scatter(values, "col", scatter_dimension=0, tiled=True)


def row_sum_values(first_branch, second_branch):
    return lax.psum((first_branch, second_branch), "row")


def apply_norm(preact_input, norm_gain, norm_offset):
    total, squares = row_sum_values(
        jnp.sum(preact_input, 1), jnp.sum(preact_input * preact_input, 1)
    )
    row_mean = total / MODEL_WIDTH
    inverse_deviation = lax.rsqrt(squares / MODEL_WIDTH - row_mean * row_mean + norm_eps)
    centred_rows = (preact_input - row_mean[:, None]) * inverse_deviation[:, None]
    return (centred_rows * norm_gain + norm_offset, centred_rows, inverse_deviation)


def norm_backward_pass(incoming_gradient, centred_rows, inverse_deviation, norm_gain):
    scaled_rows = incoming_gradient * norm_gain
    first_branch, second_branch = row_sum_values(
        jnp.sum(scaled_rows, 1), jnp.sum(scaled_rows * centred_rows, 1)
    )
    return inverse_deviation[:, None] * (
        scaled_rows
        - first_branch[:, None] / MODEL_WIDTH
        - centred_rows * second_branch[:, None] / MODEL_WIDTH
    )


def seg_mask(segments):
    return (segments[:, None] == segments[None, :])[None]


def attend_forward(items):
    queries, keys, values, segments = items
    scores = jnp.einsum("qhd,khd->hqk", queries, keys, preferred_element_type=jnp.float32) * 0.125
    scores = jnp.where(seg_mask(segments), scores, -1e30)
    peak = jnp.max(scores, -1, keepdims=True)
    expo = jnp.exp(scores - peak)
    total = jnp.sum(expo, -1, keepdims=True)
    probs = (expo / total).astype(jnp.bfloat16)
    mixed = jnp.einsum("hqk,khd->qhd", probs, values, preferred_element_type=jnp.float32)
    return (mixed.astype(jnp.bfloat16), (peak + jnp.log(total))[..., 0])


def attend_backward(items):
    queries, keys, values, segments, dmixed, lse = items
    scores = jnp.einsum("qhd,khd->hqk", queries, keys, preferred_element_type=jnp.float32) * 0.125
    probs = jnp.where(seg_mask(segments), jnp.exp(scores - lse[..., None]), 0.0)
    dvalues = jnp.einsum(
        "hqk,qhd->khd", probs.astype(jnp.bfloat16), dmixed, preferred_element_type=jnp.float32
    )
    dprobs = jnp.einsum("qhd,khd->hqk", dmixed, values, preferred_element_type=jnp.float32)
    middle = jnp.sum(probs * dprobs, -1, keepdims=True)
    dscores = (probs * (dprobs - middle)).astype(jnp.bfloat16)
    dqueries = jnp.einsum("hqk,khd->qhd", dscores, keys, preferred_element_type=jnp.float32) * 0.125
    dkeys = jnp.einsum("hqk,qhd->khd", dscores, queries, preferred_element_type=jnp.float32) * 0.125
    return (dqueries.astype(jnp.bfloat16), dkeys.astype(jnp.bfloat16), dvalues.astype(jnp.bfloat16))


def shards(
    hidden_in,
    segment_ids,
    query_weight,
    query_bias,
    key_weight,
    value_weight,
    value_bias,
    attn_out_weight,
    attn_out_bias,
    norm1_gain,
    first_norm_offset,
    inner_weight,
    inner_bias,
    outer_weight,
    outer_bias,
    norm2_gain,
    second_norm_offset,
    cotangent,
):
    local_seqs = segment_ids.shape[0]
    col_width = query_weight.shape[1]
    head_local = col_width // HD
    first_norm_gain = norm1_gain.astype(jnp.float32)
    second_norm_gain = norm2_gain.astype(jnp.float32)
    x_full = col_gather(hidden_in)
    part_q, part_k, part_v = (
        lax.psum_scatter(product(x_full, query_weight), "row", scatter_dimension=0, tiled=True),
        lax.psum_scatter(product(x_full, key_weight), "row", scatter_dimension=0, tiled=True),
        lax.psum_scatter(product(x_full, value_weight), "row", scatter_dimension=0, tiled=True),
    )
    queries = (part_q + query_bias).astype(jnp.bfloat16)
    keys = part_k.astype(jnp.bfloat16)
    values = (part_v + value_bias).astype(jnp.bfloat16)
    q_heads = queries.reshape(local_seqs, SEQ, head_local, HD)
    k_heads = keys.reshape(local_seqs, SEQ, head_local, HD)
    v_heads = values.reshape(local_seqs, SEQ, head_local, HD)
    mixed, lse = lax.map(attend_forward, (q_heads, k_heads, v_heads, segment_ids))
    mixed = mixed.reshape(local_seqs * SEQ, col_width)
    mixed_full = row_gather(mixed)
    attn = col_reduce(product(mixed_full, attn_out_weight)) + attn_out_bias
    first_preact = hidden_in.astype(jnp.float32) + attn
    hidden_state, first_centred_rows, first_inverse_deviation = apply_norm(
        first_preact, first_norm_gain, first_norm_offset
    )
    hidden_full = col_gather(hidden_state.astype(jnp.bfloat16))
    inner = row_reduce(product(hidden_full, inner_weight)) + inner_bias
    active = jax.nn.gelu(inner, approximate=False).astype(jnp.bfloat16)
    active_full = row_gather(active)
    outer_product = col_reduce(product(active_full, outer_weight)) + outer_bias
    closing_result, second_centred_rows, second_inverse_deviation = apply_norm(
        hidden_state + outer_product, second_norm_gain, second_norm_offset
    )
    layer_out = closing_result.astype(jnp.bfloat16)
    output_gradient = cotangent.astype(jnp.float32)
    second_gain_gradient = jnp.sum(output_gradient * second_centred_rows, 0)
    shift_two_grad = jnp.sum(output_gradient, 0)
    second_preact_grad = norm_backward_pass(
        output_gradient, second_centred_rows, second_inverse_deviation, second_norm_gain
    )
    dout_full = col_gather(second_preact_grad.astype(jnp.bfloat16))
    outer_bias_grad = jnp.sum(dout_full, 0, dtype=jnp.float32)
    outer_weight_grad = over_tokens(active_full, dout_full)
    dactive = row_reduce(against(dout_full, outer_weight))
    cdf = 0.5 * (1.0 + lax.erf(inner * inv_root_two))
    density = jnp.exp(-0.5 * inner * inner) * inv_root_two_pi
    dinner = (dactive * (cdf + inner * density)).astype(jnp.bfloat16)
    dinner_full = row_gather(dinner)
    inner_bias_grad = jnp.sum(dinner_full, 0, dtype=jnp.float32)
    inner_weight_grad = over_tokens(hidden_full, dinner_full)
    hidden_state_grad = second_preact_grad + col_reduce(against(dinner_full, inner_weight))
    first_gain_gradient = jnp.sum(hidden_state_grad * first_centred_rows, 0)
    shift_one_grad = jnp.sum(hidden_state_grad, 0)
    first_preact_grad = norm_backward_pass(
        hidden_state_grad, first_centred_rows, first_inverse_deviation, first_norm_gain
    )
    dattn_full = col_gather(first_preact_grad.astype(jnp.bfloat16))
    attn_out_bias_grad = jnp.sum(dattn_full, 0, dtype=jnp.float32)
    attn_out_weight_grad = over_tokens(mixed_full, dattn_full)
    dmixed = row_reduce(against(dattn_full, attn_out_weight)).astype(jnp.bfloat16)
    dq_heads, dk_heads, dv_heads = lax.map(
        attend_backward,
        (
            q_heads,
            k_heads,
            v_heads,
            segment_ids,
            dmixed.reshape(local_seqs, SEQ, head_local, HD),
            lse,
        ),
    )
    dq_rows = dq_heads.reshape(local_seqs * SEQ, col_width)
    dk_rows = dk_heads.reshape(local_seqs * SEQ, col_width)
    dv_rows = dv_heads.reshape(local_seqs * SEQ, col_width)
    dq_full, dk_full, dv_full = (
        lax.all_gather(dq_rows, "row", axis=0, tiled=True),
        lax.all_gather(dk_rows, "row", axis=0, tiled=True),
        lax.all_gather(dv_rows, "row", axis=0, tiled=True),
    )
    query_bias_grad = jnp.sum(dq_full, 0, dtype=jnp.float32)
    value_bias_grad = jnp.sum(dv_full, 0, dtype=jnp.float32)
    query_weight_grad = over_tokens(x_full, dq_full)
    key_weight_grad = over_tokens(x_full, dk_full)
    value_weight_grad = over_tokens(x_full, dv_full)
    dx_part = (
        against(dq_full, query_weight)
        + against(dk_full, key_weight)
        + against(dv_full, value_weight)
    )
    input_grad = (first_preact_grad + col_reduce(dx_part)).astype(jnp.bfloat16)
    summed = (
        lax.psum(query_weight_grad.astype(jnp.bfloat16), "dp").astype(jnp.float32),
        lax.psum(query_bias_grad.astype(jnp.bfloat16), "dp").astype(jnp.float32),
        lax.psum(key_weight_grad.astype(jnp.bfloat16), "dp").astype(jnp.float32),
        lax.psum(value_weight_grad.astype(jnp.bfloat16), "dp").astype(jnp.float32),
        lax.psum(value_bias_grad.astype(jnp.bfloat16), "dp").astype(jnp.float32),
        lax.psum(attn_out_weight_grad.astype(jnp.bfloat16), "dp").astype(jnp.float32),
        lax.psum(attn_out_bias_grad.astype(jnp.bfloat16), "dp").astype(jnp.float32),
        lax.psum(inner_weight_grad.astype(jnp.bfloat16), "dp").astype(jnp.float32),
        lax.psum(inner_bias_grad.astype(jnp.bfloat16), "dp").astype(jnp.float32),
        lax.psum(outer_weight_grad.astype(jnp.bfloat16), "dp").astype(jnp.float32),
        lax.psum(outer_bias_grad.astype(jnp.bfloat16), "dp").astype(jnp.float32),
    )
    norms = lax.psum(
        (first_gain_gradient, shift_one_grad, second_gain_gradient, shift_two_grad), ("dp", "col")
    )
    return (
        layer_out,
        input_grad,
        summed[0],
        summed[1],
        summed[2],
        summed[3],
        summed[4],
        summed[5],
        summed[6],
        norms[0],
        norms[1],
        summed[7],
        summed[8],
        summed[9],
        summed[10],
        norms[2],
        norms[3],
    )


IN_SPECS = (
    P(("dp", "col"), "row"),
    P(("dp", "row"), None),
    P("row", "col"),
    P("col"),
    P("row", "col"),
    P("row", "col"),
    P("col"),
    P("col", "row"),
    P("row"),
    P("row"),
    P("row"),
    P("row", "col"),
    P("col"),
    P("col", "row"),
    P("row"),
    P("row"),
    P("row"),
    P(("dp", "col"), "row"),
)
OUT_SPECS = (
    P(("dp", "col"), "row"),
    P(("dp", "col"), "row"),
    P("row", "col"),
    P("col"),
    P("row", "col"),
    P("row", "col"),
    P("col"),
    P("col", "row"),
    P("row"),
    P("row"),
    P("row"),
    P("row", "col"),
    P("col"),
    P("col", "row"),
    P("row"),
    P("row"),
    P("row"),
)


MESH = pl.DeviceIdType.MESH
LINE = 4
GROUPS = 4
GATHERED = ((1, 0, 8), (0, 0, 8), (2, 0, 8), (3, 0, 4), (3, 4, 4))
SCATTERED = (
    (0, 0, 2, True), (0, 2, 2, True), (0, 4, 2, True), (0, 6, 2, False), (1, 0, 8, False), (3, 0, 8, False),
    (2, 0, 8, False),
)


class Spot:
    def __init__(self):
        self.dp = lax.axis_index("dp")
        self.row = lax.axis_index("row")
        self.col = lax.axis_index("col")
        k, r = self.dp, self.row
        self.dp_x = k + 1 - 2 * lax.rem(k, 2)
        self.dp_y = lax.rem(k + 2, 4)
        self.dp_d = 3 - k
        self.beside_x = (self.dp_x, r, self.col)
        self.beside_y = (self.dp_y, r, self.col)
        self.other_core = (k, r, 1 - self.col)
        self.inside = jnp.logical_and(r > 0, r < LINE - 1)
        first = jnp.where(r > 0, r - 1, 1)
        second = jnp.where(r == 0, 2, jnp.where(r == LINE - 1, 1, r + 1))
        third = jnp.where(r < 2, LINE - 1, 0)
        self.near = (first, second, third)

    def at_row(self, row):
        return (self.dp, row, self.col)


def remote(src, dst, send, recv, device):
    return pltpu.make_async_remote_copy(
        src_ref=src, dst_ref=dst, send_sem=send, recv_sem=recv, device_id=device, device_id_type=MESH
    )


def greet(spot, far=False):
    barrier = pltpu.get_barrier_semaphore()

    def tell(device):
        pl.semaphore_signal(barrier, inc=1, device_id=device, device_id_type=MESH)

    if far:
        for away in range(LINE):
            row = lax.rem(spot.row + away, LINE)
            for core in (1, 2):
                if away or core == 1:
                    tell((spot.dp, row, lax.rem(spot.col + core, 2)))
        tell(spot.beside_x)
        tell(spot.beside_y)
        pl.semaphore_wait(barrier, 2 * LINE + 1)
        return
    for device in (spot.beside_x, spot.beside_y, spot.other_core):
        tell(device)

    @pl.when(spot.row > 0)
    def _():
        tell(spot.at_row(spot.row - 1))

    @pl.when(spot.row < LINE - 1)
    def _():
        tell(spot.at_row(spot.row + 1))

    pl.semaphore_wait(barrier, 3 + jnp.where(spot.inside, 2, 1))


class Gather:
    SEMS = (
        [pltpu.SemaphoreType.DMA((len(GATHERED), 2))]
        + [pltpu.SemaphoreType.DMA((GROUPS, 3))]
        + [pltpu.SemaphoreType.DMA((len(GATHERED), LINE))] * 10
    )

    def __init__(self, spot, shards, bufs, sems):
        self.spot, self.shards, self.bufs = spot, shards, bufs
        (self.own_s, self.own_l, self.zs, self.zr, self.xs, self.xr, self.ys, self.yr, self.fas, self.far, self.fbs, self.fbr) = sems
        self.loaded = set()

    def piece(self, g, row, j, half=None):
        which, first, count = GATHERED[g]
        eighth = self.bufs[which].shape[1] // 8
        q = eighth * count // 4
        size = q if half is None else q // 2
        start = first * eighth + j * q + (0 if half is None else half * size)
        return self.bufs[which].at[row, pl.ds(pl.multiple_of(start, size), size)]

    def own_copy(self, g, up):
        s = self.spot
        piece = self.piece(g, s.row, s.dp)
        row = s.row + 1 if up else s.row - 1
        return remote(piece, piece, self.own_s.at[g, int(up)], self.zr.at[g, s.row], s.at_row(row))

    def local(self, g):
        mine = self.bufs[g].at[self.spot.row]
        wide = self.shards[g][0].shape[1]
        return [
            pltpu.make_async_copy(part, mine.at[:, pl.ds(i * wide, wide)], self.own_l.at[g, i])
            for i, part in enumerate(self.shards[g])
        ]

    def load(self):
        for g in (1, 0, 2, 3):
            for c in self.local(g):
                c.start()

    def start_own(self, g):
        s = self.spot
        which = GATHERED[g][0]
        if which not in self.loaded:
            self.loaded.add(which)
            for c in self.local(which):
                c.wait()

        @pl.when(s.row < LINE - 1)
        def _():
            self.own_copy(g, True).start()

        @pl.when(s.row > 0)
        def _():
            self.own_copy(g, False).start()

    def onward(self, g, n):
        s = self.spot
        row = s.near[n]
        p = self.piece(g, row, s.dp)
        to = jnp.where(row < s.row, s.row + 1, s.row - 1)
        return remote(p, p, self.zs.at[g, row], self.zr.at[g, row], s.at_row(to))

    def across(self, g, n):
        s = self.spot
        row = s.near[n]
        p = self.piece(g, row, s.dp)
        return (
            remote(p, p, self.xs.at[g, row], self.xr.at[g, row], s.beside_x),
            remote(p, p, self.ys.at[g, row], self.yr.at[g, row], s.beside_y),
        )

    def relays(self, g, n):
        s = self.spot
        row = s.near[n]
        a = self.piece(g, row, s.dp_y, 0)
        b = self.piece(g, row, s.dp_x, 1)
        return (
            remote(a, a, self.fas.at[g, row], self.far.at[g, row], s.beside_x),
            remote(b, b, self.fbs.at[g, row], self.fbr.at[g, row], s.beside_y),
        )

    def z_step(self, g, n):
        self.onward(g, n).wait_recv()

        @pl.when(self.spot.inside)
        def _():
            self.onward(g, n).start()

        for c in self.across(g, n):
            c.start()

    def x_step(self, g, n):
        s = self.spot
        row = s.near[n]
        p = self.piece(g, row, s.dp_x)
        remote(p, p, self.xs.at[g, row], self.xr.at[g, row], s.beside_x).wait_recv()
        self.relays(g, n)[1].start()

    def y_step(self, g, n):
        s = self.spot
        row = s.near[n]
        p = self.piece(g, row, s.dp_y)
        remote(p, p, self.ys.at[g, row], self.yr.at[g, row], s.beside_y).wait_recv()
        self.relays(g, n)[0].start()

    def arrive(self, g, n):
        s = self.spot
        row = s.near[n]
        a, b = self.piece(g, row, s.dp_d, 0), self.piece(g, row, s.dp_d, 1)
        remote(a, a, self.fas.at[g, row], self.far.at[g, row], s.beside_x).wait_recv()
        remote(b, b, self.fbs.at[g, row], self.fbr.at[g, row], s.beside_y).wait_recv()

    def drain(self):
        s = self.spot
        for g in range(len(GATHERED)):

            @pl.when(s.row < LINE - 1)
            def _():
                self.own_copy(g, True).wait_send()

            @pl.when(s.row > 0)
            def _():
                self.own_copy(g, False).wait_send()

            for n in range(LINE - 1):

                @pl.when(s.inside)
                def _():
                    self.onward(g, n).wait_send()

                for c in self.across(g, n) + self.relays(g, n):
                    c.wait_send()


class Tokens:
    SEMS = [pltpu.SemaphoreType.DMA((2,)), pltpu.SemaphoreType.DMA((LINE,))] + [pltpu.SemaphoreType.DMA((LINE,))] * 2 + [
        pltpu.SemaphoreType.DMA((2, 2)),
        pltpu.SemaphoreType.DMA((LINE,)),
        pltpu.SemaphoreType.DMA((LINE,)),
        pltpu.SemaphoreType.DMA((LINE,)),
    ]

    def __init__(self, spot, x, ct, xs, cts, pars, sems):
        self.spot = spot
        self.x, self.ct, self.xs, self.cts, self.pars = x, ct, xs, cts, pars
        (self.x_s, self.x_r, self.x_fs, self.x_fr, self.c_s, self.c_r, self.p_s, self.p_r) = sems
        self.seq = x.shape[0] // 2
        self.wide = x.shape[1]

    def cols(self, ref, row):
        return ref.at[:, pl.ds(pl.multiple_of(row * self.wide, self.wide), self.wide)]

    def x_copy(self, i, local):
        s = self.spot
        row = 2 * s.col + i
        src = self.x.at[pl.ds(i * self.seq, self.seq)]
        dst = self.cols(self.xs, s.row)
        if local:
            return pltpu.make_async_copy(src, dst, self.x_r.at[s.row])
        return remote(src, dst, self.x_s.at[i], self.x_r.at[s.row], s.at_row(row))

    def ct_copy(self, i, core, local):
        s = self.spot
        half = self.seq // 2
        row = 2 * s.col + i
        src = self.ct.at[pl.ds(i * self.seq + core * half, half)]
        dst = self.cols(self.cts, s.row)
        if local:
            return pltpu.make_async_copy(src, dst, self.c_r.at[s.row])
        return remote(src, dst, self.c_s.at[i, core], self.c_r.at[s.row], (s.dp, row, jnp.int32(core)))

    def par_copy(self, away):
        s = self.spot
        row = lax.rem(s.row + away, LINE)
        mine = self.pars.at[s.row]
        return remote(mine, mine, self.p_s.at[away], self.p_r.at[s.row], s.at_row(row))

    def start_x(self):
        s = self.spot
        for i in range(2):
            here = 2 * s.col + i == s.row

            @pl.when(here)
            def _():
                self.x_copy(i, True).start()

            @pl.when(jnp.logical_not(here))
            def _():
                self.x_copy(i, False).start()

    def start_par(self):
        for away in range(1, LINE):
            self.par_copy(away).start()

    def start_ct(self):
        s = self.spot
        for i in range(2):
            for core in range(2):
                here = jnp.logical_and(2 * s.col + i == s.row, s.col == core)

                @pl.when(here)
                def _():
                    self.ct_copy(i, core, True).start()

                @pl.when(jnp.logical_not(here))
                def _():
                    self.ct_copy(i, core, False).start()

    def rows(self):
        return (self.spot.row,) + self.spot.near

    def relay(self, row):
        block = self.cols(self.xs, row)
        return remote(block, block, self.x_fs.at[row], self.x_fr.at[row], self.spot.other_core)

    def wait_x(self):
        s = self.spot
        first = s.row // 2 == s.col
        for row in self.rows():

            @pl.when(first)
            def _():
                block = self.cols(self.xs, row)
                pltpu.make_async_copy(block, block, self.x_r.at[row]).wait()
                self.relay(row).start()

    def wait_relayed(self):
        s = self.spot
        first = s.row // 2 == s.col
        for row in self.rows():

            @pl.when(jnp.logical_not(first))
            def _():
                self.relay(row).wait_recv()

    def wait_ct(self):
        for row in self.rows():
            block = self.cols(self.cts, row)
            pltpu.make_async_copy(block, block, self.c_r.at[row]).wait()

    def wait_par(self):
        for row in self.spot.near:
            block = self.pars.at[row]
            pltpu.make_async_copy(block, block, self.p_r.at[row]).wait()

    def drain(self):
        s = self.spot
        for i in range(2):

            @pl.when(jnp.logical_not(2 * s.col + i == s.row))
            def _():
                self.x_copy(i, False).wait_send()

            for core in range(2):

                @pl.when(jnp.logical_not(jnp.logical_and(2 * s.col + i == s.row, s.col == core)))
                def _():
                    self.ct_copy(i, core, False).wait_send()

        for away in range(1, LINE):
            self.par_copy(away).wait_send()

        @pl.when(s.row // 2 == s.col)
        def _():
            for row in self.rows():
                self.relay(row).wait_send()


ROWS_AT_ONCE = {1536: 16, 2048: 16, 256: 64}


class Scatter:
    SEMS = [pltpu.SemaphoreType.DMA((len(SCATTERED), LINE))] * 14 + [pltpu.SemaphoreType.DMA((len(SCATTERED),))] * 10

    @staticmethod
    def sizes(shapes):
        return [(shapes[b][1] // 8 * n, shapes[b][2], 1 if line else LINE) for b, _, n, line in SCATTERED]

    def __init__(self, spot, parts, rel_a, rel_b, from_x, from_y, line, stage, final, sems):
        self.spot, self.parts, self.rel_a, self.rel_b = spot, parts, rel_a, rel_b
        self.from_x, self.from_y, self.line, self.stage, self.final = from_x, from_y, line, stage, final
        (
            self.ra_s, self.ra_r, self.rb_s, self.rb_r,
            self.xa_s, self.xa_r, self.xb_s, self.xb_r,
            self.ya_s, self.ya_r, self.yb_s, self.yb_r,
            self.z_s, self.z_r,
            self.above_r, self.fx_s, self.fx_r, self.fy_s, self.fy_r,
            self.ha_s, self.ha_r, self.hb_s, self.hb_r, self.own_s,
        ) = sems
        self.order = (spot.near[2], spot.near[1], spot.near[0], spot.row)

    def rows(self, g, j, half):
        which, first, count, _ = SCATTERED[g]
        eighth = self.parts[which].shape[1] // 8
        if j is None:
            return pl.ds(first * eighth, count * eighth)
        q = eighth * count // 4
        size = q if half is None else q // 2
        start = first * eighth + j * q + (0 if half is None else half * size)
        return pl.ds(pl.multiple_of(start, size), size)

    def part(self, g, row, j=None, half=None):
        return self.parts[SCATTERED[g][0]].at[row, self.rows(g, j, half)]

    def fin(self, g, j, half=None):
        return self.final[SCATTERED[g][0]].at[self.rows(g, j, half)]

    def slot(self, g, t):
        return 0 if SCATTERED[g][3] else self.order[t]

    def half(self, ref, g, t, half):
        h = ref[g].shape[1] // 2
        return ref[g].at[self.slot(g, t), pl.ds(half * h, h)]

    def send_a(self, g, t):
        s, row = self.spot, self.order[t]
        return remote(self.part(g, row, s.dp_d, 0), self.rel_a[g].at[self.slot(g, t)], self.ra_s.at[g, row], self.ra_r.at[g, row], s.beside_y)

    def send_b(self, g, t):
        s, row = self.spot, self.order[t]
        return remote(self.part(g, row, s.dp_d, 1), self.rel_b[g].at[self.slot(g, t)], self.rb_s.at[g, row], self.rb_r.at[g, row], s.beside_x)

    def send_xa(self, g, t):
        s, row = self.spot, self.order[t]
        return remote(self.part(g, row, s.dp_x, 0), self.half(self.from_x, g, t, 0), self.xa_s.at[g, row], self.xa_r.at[g, row], s.beside_x)

    def send_xb(self, g, t):
        s, row = self.spot, self.order[t]
        return remote(self.part(g, row, s.dp_x, 1), self.half(self.from_x, g, t, 1), self.xb_s.at[g, row], self.xb_r.at[g, row], s.beside_x)

    def send_ya(self, g, t):
        s, row = self.spot, self.order[t]
        return remote(self.part(g, row, s.dp_y, 0), self.half(self.from_y, g, t, 0), self.ya_s.at[g, row], self.ya_r.at[g, row], s.beside_y)

    def send_yb(self, g, t):
        s, row = self.spot, self.order[t]
        return remote(self.part(g, row, s.dp_y, 1), self.half(self.from_y, g, t, 1), self.yb_s.at[g, row], self.yb_r.at[g, row], s.beside_y)

    def add(self, out, terms):
        rows, wide = out.shape
        step = min(ROWS_AT_ONCE[wide], rows)

        def body(i, carry):
            at = pl.ds(pl.multiple_of(i * step, step), step)
            total = terms[0][at, :].astype(jnp.float32)
            for t in terms[1:]:
                total = total + t[at, :].astype(jnp.float32)
            out[at, :] = total.astype(jnp.bfloat16)
            return carry

        lax.fori_loop(0, rows // step, body, 0)

    def first(self, g, t):
        self.send_a(g, t).start()
        self.send_b(g, t).start()

    def direct(self, g, t):
        self.send_xb(g, t).start()
        self.send_ya(g, t).start()

    def second_a(self, g, t):
        self.send_a(g, t).wait_recv()
        mine = self.part(g, self.order[t], self.spot.dp_x, 0)
        self.add(mine, (mine, self.rel_a[g].at[self.slot(g, t)]))
        self.send_xa(g, t).start()

    def second_b(self, g, t):
        self.send_b(g, t).wait_recv()
        mine = self.part(g, self.order[t], self.spot.dp_y, 1)
        self.add(mine, (mine, self.rel_b[g].at[self.slot(g, t)]))
        self.send_yb(g, t).start()

    def onward(self, g, t, above=False):
        s, row = self.spot, self.order[t]
        to = jnp.where(row > s.row, s.row + 1, s.row - 1)
        slot = jnp.where(row == s.row - 1, LINE, row)
        piece = self.part(g, row, None if SCATTERED[g][3] else s.dp)
        recv = self.above_r.at[g] if above else self.z_r.at[g, row]
        return remote(piece, self.line[g].at[slot], self.z_s.at[g, row], recv, s.at_row(to))

    def along(self, g, t, mine, terms, out):
        s, row = self.spot, self.order[t]
        if t < LINE - 1:
            passed = jnp.logical_or(jnp.logical_and(row > s.row, s.row > 0), jnp.logical_and(row < s.row, s.row < LINE - 1))
            last = row == s.row - 1

            @pl.when(passed)
            def _():
                self.onward(g, t).wait_recv()
                self.add(mine, terms + (self.line[g].at[row],))

            if len(terms) > 1:

                @pl.when(jnp.logical_not(passed))
                def _():
                    self.add(mine, terms)

            @pl.when(last)
            def _():
                self.onward(g, t, True).start()

            @pl.when(jnp.logical_not(last))
            def _():
                self.onward(g, t).start()

        else:
            below, over = self.line[g].at[s.row], self.line[g].at[LINE]

            def wait_below():
                remote(below, below, self.z_s.at[g, s.row], self.z_r.at[g, s.row], s.beside_x).wait_recv()

            def wait_over():
                remote(over, over, self.z_s.at[g, s.row], self.above_r.at[g], s.beside_x).wait_recv()

            @pl.when(s.inside)
            def _():
                wait_below()
                wait_over()
                self.add(out, terms + (below, over))

            @pl.when(s.row == 0)
            def _():
                wait_over()
                self.add(out, terms + (over,))

            @pl.when(s.row == LINE - 1)
            def _():
                wait_below()
                self.add(out, terms + (below,))

    def line_step(self, g, t):
        mine = self.part(g, self.order[t])
        self.along(g, t, mine, (mine,), mine)

    def third(self, g, t):
        s, row = self.spot, self.order[t]
        for c in (self.send_xa(g, t), self.send_xb(g, t), self.send_ya(g, t), self.send_yb(g, t)):
            c.wait_recv()
        mine = self.part(g, row, s.dp)
        slot = self.slot(g, t)
        terms = (mine, self.from_x[g].at[slot], self.from_y[g].at[slot])
        if SCATTERED[g][3]:
            self.add(self.stage[g], terms)
        else:
            self.along(g, t, mine, terms, self.stage[g])
        if t == LINE - 1:
            for c in self.spread(g):
                c.start()
            self.settle(g).start()

    def spread(self, g):
        s = self.spot
        p = self.fin(g, s.dp)
        mine = self.stage[g]
        return (
            remote(mine, p, self.fx_s.at[g], self.fx_r.at[g], s.beside_x),
            remote(mine, p, self.fy_s.at[g], self.fy_r.at[g], s.beside_y),
        )

    def settle(self, g):
        return pltpu.make_async_copy(self.stage[g], self.fin(g, self.spot.dp), self.own_s.at[g])

    def relays(self, g):
        s = self.spot
        a, b = self.fin(g, s.dp_y, 0), self.fin(g, s.dp_x, 1)
        return (
            remote(a, a, self.ha_s.at[g], self.ha_r.at[g], s.beside_x),
            remote(b, b, self.hb_s.at[g], self.hb_r.at[g], s.beside_y),
        )

    def fourth_x(self, g):
        s = self.spot
        p = self.fin(g, s.dp_x)
        remote(p, p, self.fx_s.at[g], self.fx_r.at[g], s.beside_x).wait_recv()
        self.relays(g)[1].start()

    def fourth_y(self, g):
        s = self.spot
        p = self.fin(g, s.dp_y)
        remote(p, p, self.fy_s.at[g], self.fy_r.at[g], s.beside_y).wait_recv()
        self.relays(g)[0].start()

    def fifth(self, g):
        s = self.spot
        a, b = self.fin(g, s.dp_d, 0), self.fin(g, s.dp_d, 1)
        remote(a, a, self.ha_s.at[g], self.ha_r.at[g], s.beside_x).wait_recv()
        remote(b, b, self.hb_s.at[g], self.hb_r.at[g], s.beside_y).wait_recv()

    def drain(self):
        for g in range(len(SCATTERED)):
            for t in range(LINE):
                if t == LINE - 1 or not SCATTERED[g][3]:
                    for c in (
                        self.send_a(g, t), self.send_b(g, t), self.send_xa(g, t),
                        self.send_xb(g, t), self.send_ya(g, t), self.send_yb(g, t),
                    ):
                        c.wait_send()
                if t < LINE - 1:
                    self.onward(g, t).wait_send()
            for c in self.spread(g) + self.relays(g):
                c.wait_send()
            self.settle(g).wait()


class Spread:
    SEMS = [pltpu.SemaphoreType.DMA((LINE,)), pltpu.SemaphoreType.DMA((4,))]

    def __init__(self, spot, src, out, sems):
        self.spot, self.src, self.out = spot, src, out
        self.s, self.r = sems
        self.count, wide = src.shape
        self.cut = wide // LINE

    def slot(self, n):
        return self.out.at[pl.ds(pl.multiple_of(n * self.count, self.count), self.count)]

    def copy(self, away, local=False):
        s = self.spot
        row = lax.rem(s.row + away, LINE)
        src = self.src.at[:, pl.ds(pl.multiple_of(row * self.cut, self.cut), self.cut)]
        n = 2 * lax.rem(s.row, 2) + s.col
        if local:
            return pltpu.make_async_copy(src, self.slot(n), self.r.at[n])
        return remote(src, self.slot(n), self.s.at[away], self.r.at[n], (s.dp, row, s.row // 2))

    def start(self):
        s = self.spot
        here = s.row // 2 == s.col

        @pl.when(here)
        def _():
            self.copy(0, True).start()

        @pl.when(jnp.logical_not(here))
        def _():
            self.copy(0).start()

        for away in range(1, LINE):
            self.copy(away).start()

    def wait(self):
        s = self.spot
        for n in range(4):
            pltpu.make_async_copy(self.slot(n), self.slot(n), self.r.at[n]).wait()

        @pl.when(jnp.logical_not(s.row // 2 == s.col))
        def _():
            self.copy(0).wait_send()

        for away in range(1, LINE):
            self.copy(away).wait_send()


(OWN, TOKENS_IN, COTANGENT_IN, ALONG, FROM_X, FROM_Y, TO_CORE, TURN_X, PROJECT, ATTEND, ATTN_OUT, NORM_1, TURN_H, GROW, SHRINK, NORM_2, LAST) = range(17)
(SEND, ADD_A, ADD_B, SUM_UP, LINE_STEP, BACK_X, BACK_Y, OUTER_W, INNER, HIDDEN, INNER_W, NORM_BACK, MIXED, ATTN_W, QKV_W, INPUT, SUMS, SUMS_X, SUMS_Y, SUMS_LINE, INPUT_LAST, PLACE_OUT, PLACE_INPUT) = range(17, 40)
FORWARD_ORDER = (
    (OWN, 0), (OWN, 1), (ALONG, 0, 0), (ALONG, 0, 1), (FROM_Y, 0, 0), (FROM_X, 0, 0), (ALONG, 1, 0), (ALONG, 1, 1),
    (ALONG, 0, 2), (TOKENS_IN,), (FROM_Y, 0, 1), (FROM_X, 0, 1), (ALONG, 1, 2), (OWN, 2), (FROM_X, 0, 2),
    (FROM_Y, 1, 0), (FROM_X, 1, 0), (FROM_X, 1, 2), (FROM_Y, 0, 2), (FROM_Y, 1, 2), (FROM_X, 1, 1), (FROM_Y, 1, 1),
    (ALONG, 2, 0), (ALONG, 2, 1), (TO_CORE,), (PROJECT, 0), (ALONG, 2, 2), (OWN, 3), (PROJECT, 1), (PROJECT, 2),
    (OWN, 4), (PROJECT, 3), (PROJECT, 4), (PROJECT, 5), (ATTEND, 0, 0), (ATTEND, 0, 1), (FROM_X, 2, 1),
    (ATTEND, 0, 2), (FROM_Y, 2, 1), (ATTEND, 0, 3), (ATTEND, 1, 0), (ATTEND, 1, 1), (ALONG, 3, 0), (ALONG, 3, 1),
    (ATTEND, 1, 2), (ATTEND, 1, 3), (ATTEND, 2, 0), (FROM_Y, 2, 2), (ATTEND, 2, 1), (ALONG, 4, 0), (ATTEND, 2, 2),
    (ATTEND, 2, 3), (ATTEND, 3, 0), (ALONG, 4, 1), (ATTEND, 3, 1), (FROM_Y, 3, 1), (ATTEND, 3, 2), (ATTEND, 3, 3),
    (ATTN_OUT, 0), (ATTN_OUT, 1), (FROM_X, 2, 2), (FROM_X, 2, 0), (ATTN_OUT, 2), (FROM_Y, 2, 0), (FROM_Y, 3, 0),
    (ATTN_OUT, 3), (ALONG, 3, 2), (FROM_X, 4, 0), (ALONG, 4, 2), (FROM_Y, 4, 1), (NORM_1,), (FROM_X, 3, 1),
    (COTANGENT_IN,), (GROW, 0), (TURN_X,), (FROM_Y, 3, 2), (FROM_Y, 4, 0), (GROW, 1), (GROW, 2), (FROM_X, 3, 2),
    (FROM_X, 3, 0), (GROW, 3), (FROM_X, 4, 1), (GROW, 4), (FROM_Y, 4, 2), (FROM_X, 4, 2), (GROW, 5), (GROW, 6),
    (GROW, 7), (TURN_H,), (SHRINK, 0), (SHRINK, 1), (SHRINK, 2), (SHRINK, 3), (NORM_2,), (LAST,),
)
BACKWARD_ORDER = (
    (PLACE_OUT,), (OUTER_W, 0), (OUTER_W, 1), (OUTER_W, 2), (OUTER_W, 3), (SEND, 3, 1), (INNER, 0), (INNER, 1),
    (SEND, 3, 0), (INNER, 2), (INNER, 3), (INNER, 4), (SEND, 3, 2), (SEND, 3, 3), (INNER, 5), (INNER, 6), (INNER, 7),
    (INNER_W, 0), (HIDDEN, 0), (INNER_W, 1), (SEND, 4, 1), (LINE_STEP, 0, 0), (SEND, 4, 0), (HIDDEN, 1), (INNER_W, 2),
    (HIDDEN, 2), (HIDDEN, 3), (SEND, 4, 2), (ADD_B, 3, 3), (ADD_A, 3, 1), (ADD_B, 4, 1), (LINE_STEP, 0, 1),
    (INNER_W, 3), (ADD_B, 3, 0), (NORM_BACK,), (LINE_STEP, 0, 2), (ADD_A, 4, 1), (SEND, 4, 3), (MIXED, 0),
    (ATTN_W, 0), (ADD_B, 4, 0), (ADD_A, 3, 0), (ADD_A, 3, 2), (MIXED, 1), (SEND, 6, 0), (ATTEND, 0, 0),
    (ATTEND, 0, 1), (ATTEND, 0, 2), (LINE_STEP, 1, 0), (ATTEND, 0, 3), (ATTEND, 0, 4), (ATTN_W, 1), (ATTEND, 1, 0),
    (ADD_A, 4, 0), (ATTEND, 1, 1), (ATTEND, 1, 2), (ATTEND, 1, 3), (ATTEND, 1, 4), (ATTEND, 2, 0), (ADD_A, 4, 2),
    (LINE_STEP, 1, 1), (ATTN_W, 2), (ATTEND, 2, 1), (ATTEND, 2, 2), (SEND, 6, 2), (LINE_STEP, 1, 2), (SEND, 6, 1),
    (ATTEND, 2, 3), (ADD_A, 3, 3), (ADD_B, 4, 3), (ATTEND, 2, 4), (ATTEND, 3, 0), (ATTEND, 3, 1), (ATTEND, 3, 2),
    (ATTEND, 3, 3), (ATTEND, 3, 4), (ADD_B, 3, 1), (QKV_W, 0), (SEND, 5, 0), (LINE_STEP, 0, 3), (ATTN_W, 3),
    (ADD_B, 4, 2), (SUM_UP, 3, 0), (INPUT, 0), (ADD_B, 6, 0), (ADD_A, 6, 2), (INPUT, 1), (ADD_A, 4, 3),
    (LINE_STEP, 2, 0), (QKV_W, 1), (LINE_STEP, 1, 3), (ADD_B, 6, 1), (INPUT, 2), (SEND, 6, 3), (SUM_UP, 4, 0),
    (SEND, 0, 3), (ADD_A, 6, 1), (SUM_UP, 3, 1), (INPUT, 3), (SEND, 5, 1), (ADD_A, 5, 0), (QKV_W, 2), (SEND, 5, 2),
    (ADD_B, 6, 3), (LINE_STEP, 2, 1), (ADD_B, 5, 0), (LINE_STEP, 2, 2), (SEND, 1, 3), (QKV_W, 3), (SEND, 5, 3),
    (ADD_B, 3, 2), (SUM_UP, 4, 1), (LINE_STEP, 2, 3), (SEND, 2, 3), (SUM_UP, 4, 2), (ADD_B, 1, 3), (ADD_A, 6, 0),
    (SUMS,), (ADD_A, 5, 3), (SUMS_X,), (ADD_A, 5, 1), (ADD_B, 5, 3), (ADD_B, 5, 1), (ADD_A, 0, 3), (ADD_B, 5, 2),
    (ADD_B, 0, 3), (ADD_B, 6, 2), (ADD_A, 2, 3), (INPUT_LAST,), (ADD_A, 6, 3), (ADD_A, 5, 2), (SUM_UP, 5, 0),
    (SUM_UP, 6, 0), (ADD_B, 2, 3), (SUMS_Y,), (SUM_UP, 4, 3), (SUM_UP, 5, 1), (SUM_UP, 3, 2), (ADD_A, 1, 3),
    (SUM_UP, 6, 1), (SUM_UP, 5, 2), (SUM_UP, 3, 3), (SUM_UP, 2, 3), (SUM_UP, 6, 2), (SUM_UP, 0, 3), (PLACE_INPUT,),
    (SUM_UP, 1, 3), (SUM_UP, 5, 3), (BACK_Y, 0), (SUM_UP, 6, 3), (BACK_Y, 2), (BACK_X, 4), (SUMS_LINE,), (BACK_Y, 4),
    (BACK_X, 3), (BACK_X, 2), (BACK_Y, 6), (BACK_X, 5), (BACK_X, 0), (BACK_X, 1), (BACK_Y, 3), (BACK_X, 6),
    (BACK_Y, 1), (BACK_Y, 5),
)


F32, LOW = jnp.float32, jnp.bfloat16
ANYWHERE = pl.BlockSpec(memory_space=pl.ANY)
IN_VMEM = pl.BlockSpec(memory_space=pltpu.VMEM)
LANES = 128
BLOCK = 32


def at(start, size):
    return pl.ds(pl.multiple_of(start * size, size), size)


def dot(a, b):
    return jnp.dot(a, b, preferred_element_type=F32)


def dot_t(a, b):
    return lax.dot_general(a, b, (((1,), (1,)), ((), ())), preferred_element_type=F32)


def loop(count, body):
    def step(i, carry):
        body(i)
        return carry

    lax.fori_loop(0, count, step, 0)


def head_lanes(half, dtype):
    lane = lax.broadcasted_iota(jnp.int32, (1, LANES), 1)
    return jnp.where((lane < HD) == (half == 0), 1.0, 0.0).astype(dtype)


def fold(values):
    return jnp.sum(values.reshape(values.shape[0] // 8, 8, values.shape[1]), 0)


def forward_kernel(*refs):
    it = iter(refs)

    def take(n):
        return [next(it) for _ in range(n)]

    x, ct, wq, wk, wv, wo_s, wi_s, wout_s = take(8)
    seg, bq, bv, bi = take(4)
    small = take(6)
    out_w = take(GROUPS)
    o_xt, o_qkv, o_probs, o_mixed_t, o_unit, o_inv, o_h_t, o_slope, o_act_t, o_dpre, o_dout, o_pars, o_out, o_sums = take(14)
    bufs = take(GROUPS)
    xs, cts, pars4, pars, qkv, qkv_bias, probs, mask, mixed, part, recv1, recv2 = take(12)
    unit, inv, h1, h_low, inner, slope, act, act_t, h_t, x_t, mixed_t, dpre, dout, out, sums = take(15)
    tok_sems, gat_sems = take(len(Tokens.SEMS)), take(len(Gather.SEMS))
    core_s, core_r, save = take(3)

    spot = Spot()
    gather = Gather(spot, ((wq, wk, wv), (wo_s,), (wi_s,), (wout_s,)), bufs, gat_sems)
    tokens = Tokens(spot, x, ct, xs, cts, pars4, tok_sems)
    wqkv, wo, wi, wout = bufs
    seq, width = xs.shape
    own = seq // 2
    half = qkv.shape[1] // 3
    mine, theirs = spot.col * own, (1 - spot.col) * own

    def rows_of(base, start, size):
        return pl.ds(pl.multiple_of(base + start * size, size), size)

    gather.load()
    pars4[spot.row] = jnp.zeros(pars4.shape[1:], F32)
    for i, p in enumerate(small):
        pars4[spot.row, pl.ds(i, 1), :] = p[...].astype(F32).reshape(1, -1)
    greet(spot)

    saves = []

    def keep(src, dst):
        c = pltpu.make_async_copy(src, dst, save.at[len(saves)])
        c.start()
        saves.append(c)

    def to_other(n, src, dst):
        return remote(src, dst, core_s.at[n], core_r.at[n], spot.other_core)

    def make_mask():
        values = seg[...].astype(F32)
        for i in range(seq // LANES):
            down = jnp.broadcast_to(values[:, i * LANES : (i + 1) * LANES], (LANES, LANES)).T
            for j in range(seq // LANES):
                across = values[:, j * LANES : (j + 1) * LANES]
                mask[pl.ds(i * LANES, LANES), pl.ds(j * LANES, LANES)] = jnp.where(down == across, 0.0, -1e30)
        qkv_bias[:, pl.ds(0, half)] = jnp.broadcast_to(bq[...].astype(F32).reshape(1, half), (8, half))
        qkv_bias[:, pl.ds(half, half)] = jnp.zeros((8, half), F32)
        qkv_bias[:, pl.ds(2 * half, half)] = jnp.broadcast_to(bv[...].astype(F32).reshape(1, half), (8, half))

    def spread_pars():
        for r in range(LINE):
            pars[:, pl.ds(r * (width // LINE), width // LINE)] = pars4[r]

    def project(n):
        def chunk(c):
            cols = at(c, 256)
            w = wqkv[:, :, cols].reshape(width, 256)
            value = (dot(xs[...], w) + qkv_bias[0:1, cols]).astype(LOW).astype(F32)
            qkv[:, cols] = (value * jnp.where(c < half // 256, 0.125, 1.0)).astype(LOW)

        chunk(n)

    def transpose_x():
        loop(width // LANES, lambda c: x_t.__setitem__((at(c, LANES), slice(None)), xs[:, at(c, LANES)].T))

    def attend(pair, i):
        lanes = pl.ds(pair * LANES, LANES)
        keys = qkv[:, pl.ds(half + pair * LANES, LANES)]
        values = qkv[:, pl.ds(2 * half + pair * LANES, LANES)]

        def block(i):
            rows = at(i, LANES)
            queries = qkv[rows, lanes]

            def head(h, total):
                scores = dot_t(queries * head_lanes(h, LOW), keys) + mask[rows, :]
                expo = jnp.exp(scores - jnp.max(scores, 1, keepdims=True))
                p = (expo / jnp.sum(expo, 1, keepdims=True)).astype(LOW)
                probs[2 * pair + h, rows, :] = p
                return total + dot(p, values) * head_lanes(h, F32)

            total = lax.fori_loop(0, 2, head, jnp.zeros((LANES, LANES), F32))
            mixed[rows, lanes] = total.astype(LOW)

        block(i)
        if i == seq // LANES - 1:
            mixed_t[lanes, :] = mixed[:, lanes].T

    def attn_out(r):
        part[:, pl.ds(r * 256, 256)] = dot(mixed[...], wo[r])

    def first_norm():
        def block(i):
            rows, there = at(i, BLOCK), rows_of(mine, i, BLOCK)
            value = xs[there, :].astype(F32) + (part[there, :] + recv1[rows, :] + pars[0:1, :])
            centred = value - jnp.mean(value, 1, keepdims=True)
            scale = lax.rsqrt(jnp.mean(centred * centred, 1, keepdims=True) + norm_eps)
            one = centred * scale
            unit[rows, :] = one
            inv[rows, :] = jnp.broadcast_to(scale, (BLOCK, LANES))
            h = one * pars[1:2, :] + pars[2:3, :]
            h1[rows, :] = h
            h_low[there, :] = h.astype(LOW)

        loop(own // BLOCK, block)

    def transpose_h():
        loop(width // LANES, lambda c: h_t.__setitem__((at(c, LANES), slice(None)), h_low[:, at(c, LANES)].T))

    def grow(c):
        cols = at(c, 256)
        inner[...] = dot(h_low[...], wi[:, :, cols].reshape(width, 256))
        bias = bi[cols].astype(F32).reshape(1, 256)

        def block(i):
            rows = at(i, 64)
            v = inner[rows, :] + bias
            cdf = 0.5 * (1.0 + lax.erf(v * inv_root_two))
            slope[rows, cols] = cdf + v * (jnp.exp(-0.5 * v * v) * inv_root_two_pi)
            act[rows, cols] = (v * cdf).astype(LOW)

        loop(seq // 64, block)
        act_t[cols, :] = act[:, cols].T

    def shrink(r):
        part[:, at(r, 256)] = dot(act[...], wout[r])

    def second_norm():
        sums[...] = jnp.zeros_like(sums)

        def block(i):
            rows, there = at(i, BLOCK), rows_of(mine, i, BLOCK)
            value = h1[rows, :] + (part[there, :] + recv2[rows, :] + pars[3:4, :])
            centred = value - jnp.mean(value, 1, keepdims=True)
            scale = lax.rsqrt(jnp.mean(centred * centred, 1, keepdims=True) + norm_eps)
            one = centred * scale
            out[rows, :] = (one * pars[4:5, :] + pars[5:6, :]).astype(LOW)
            dy = cts[rows, :].astype(F32)
            s = dy * pars[4:5, :]
            d = scale * (s - jnp.mean(s, 1, keepdims=True) - one * jnp.mean(s * one, 1, keepdims=True))
            dpre[rows, :] = d
            d_low = d.astype(LOW)
            dout[there, :] = d_low
            sums[0] += fold(d_low.astype(F32))
            sums[1] += fold(dy * one)
            sums[2] += fold(dy)

        loop(own // BLOCK, block)

    seen = set()

    def once(*what):
        new = what not in seen
        seen.add(what)
        return new

    def arrived(which, turns=range(LINE - 1)):
        for g in range(len(GATHERED)):
            for n in turns:
                if GATHERED[g][0] == which and once("arrived", g, n):
                    gather.arrive(g, n)

    def relayed():
        if once("relayed"):
            tokens.wait_relayed()

    their_half = part.at[pl.ds(pl.multiple_of(theirs, own), own)]
    my_rows = pl.ds(pl.multiple_of(mine, own), own)
    first = to_other(0, their_half, recv1)

    def second(row):
        cols = at(row, 256)
        return to_other(
            4 + row, part.at[pl.ds(pl.multiple_of(theirs, own), own), cols], recv2.at[:, cols]
        )

    pass_h, pass_d = to_other(1, *[h_low.at[my_rows]] * 2), to_other(3, *[dout.at[my_rows]] * 2)

    def hidden_there():
        if once("hidden"):
            pass_h.wait_recv()

    def do(what, *n):
        if what == OWN:
            gather.start_own(*n)
        elif what == TOKENS_IN:
            tokens.start_x()
            tokens.start_par()
        elif what == COTANGENT_IN:
            tokens.start_ct()
        elif what == ALONG:
            gather.z_step(*n)
        elif what == FROM_X:
            gather.x_step(*n)
        elif what == FROM_Y:
            gather.y_step(*n)
        elif what == TO_CORE:
            tokens.wait_x()
        elif what == TURN_X:
            relayed()
            transpose_x()
            keep(x_t, o_xt)
        elif what == PROJECT:
            relayed()
            arrived(0)
            project(*n)
            if n[0] == 5:
                keep(wqkv, out_w[0])
                keep(qkv, o_qkv)
        elif what == ATTEND:
            attend(*n)
            if n == (3, 3):
                keep(probs, o_probs)
                keep(mixed_t, o_mixed_t)
        elif what == ATTN_OUT:
            arrived(1)
            attn_out(*n)
            if n[0] == LINE - 1:
                keep(wo, out_w[1])
                first.start()
        elif what == NORM_1:
            tokens.wait_par()
            spread_pars()
            keep(pars, o_pars)
            first.wait_recv()
            first_norm()
            pass_h.start()
            keep(unit, o_unit)
            keep(inv, o_inv)
        elif what == TURN_H:
            hidden_there()
            transpose_h()
            keep(h_t, o_h_t)
        elif what == GROW:
            hidden_there()
            arrived(2)
            grow(*n)
            if n[0] == hidden // 256 - 1:
                keep(wi, out_w[2])
                keep(slope, o_slope)
                keep(act_t, o_act_t)
        elif what == SHRINK:
            if n[0]:
                arrived(3, (n[0] - 1,))
            elif once("sent"):
                first.wait_send()
            row = spot.near[n[0] - 1] if n[0] else spot.row
            shrink(row)
            keep(wout.at[row], out_w[3].at[row])
            second(row).start()
        elif what == NORM_2:
            tokens.wait_ct()
            for row in range(LINE):
                second(row).wait_recv()
            second_norm()
            pass_d.start()
            keep(dpre, o_dpre)
            keep(out, o_out)
            keep(sums, o_sums)
        elif what == LAST:
            pass_d.wait_recv()
            keep(dout, o_dout)

    hidden = act.shape[1]
    make_mask()
    for step in FORWARD_ORDER:
        do(*step)
    for c in (pass_h, pass_d, *(second(row) for row in range(LINE))):
        c.wait_send()
    gather.drain()
    tokens.drain()
    for c in saves:
        c.wait()


def forward(x, ct, wq, wk, wv, wo, wi, wout, seg, bq, bv, bi, small):
    half, hidden = wq.shape[1], wi.shape[1]
    seq, width = x.shape[0] // 2, MODEL_WIDTH
    own, heads = seq // 2, half // HD
    weights = [((LINE, wq.shape[0], 3 * half), LOW), ((LINE,) + wo.shape, LOW), ((LINE,) + wi.shape, LOW), ((LINE,) + wout.shape, LOW)]
    named = dict(
        xs=((seq, width), LOW), cts=((own, width), LOW), pars4=((LINE, 8, width // LINE), F32), pars=((8, width), F32),
        qkv=((seq, 3 * half), LOW), qkv_bias=((8, 3 * half), F32), probs=((heads, seq, seq), LOW), mask=((seq, seq), F32),
        mixed=((seq, half), LOW), part=((seq, width), F32), recv1=((own, width), F32), recv2=((own, width), F32),
        unit=((own, width), F32), inv=((own, LANES), F32), h1=((own, width), F32), h_low=((seq, width), LOW),
        inner=((seq, 256), F32), slope=((seq, hidden), F32), act=((seq, hidden), LOW), act_t=((hidden, seq), LOW),
        h_t=((width, seq), LOW), x_t=((width, seq), LOW), mixed_t=((half, seq), LOW), dpre=((own, width), F32),
        dout=((seq, width), LOW), out=((own, width), LOW), sums=((3, 8, width), F32),
    )
    saved = ("x_t", "qkv", "probs", "mixed_t", "unit", "inv", "h_t", "slope", "act_t", "dpre", "dout", "pars", "out", "sums")
    outs = weights + [named[n] for n in saved]
    res = pl.pallas_call(
        forward_kernel,
        name="forward",
        out_shape=[jax.ShapeDtypeStruct(*o) for o in outs],
        in_specs=[ANYWHERE] * 8 + [IN_VMEM] * (4 + len(small)),
        out_specs=[ANYWHERE] * len(outs),
        scratch_shapes=[pltpu.VMEM(*w) for w in weights]
        + [pltpu.VMEM(*named[n]) for n in named]
        + Tokens.SEMS
        + Gather.SEMS
        + [pltpu.SemaphoreType.DMA((4 + LINE,)), pltpu.SemaphoreType.DMA((4 + LINE,)), pltpu.SemaphoreType.DMA((len(outs) + LINE,))],
        compiler_params=pltpu.CompilerParams(collective_id=0, has_side_effects=True, vmem_limit_bytes=60 * 2**20),
    )(x, ct, wq, wk, wv, wo, wi, wout, seg, bq, bv, bi, *small)
    return res[:GROUPS], dict(zip(saved, res[GROUPS:]))


class Sums:
    SEMS = [pltpu.SemaphoreType.DMA((3,)), pltpu.SemaphoreType.DMA((3,)), pltpu.SemaphoreType.DMA((LINE,)), pltpu.SemaphoreType.DMA((LINE,))]

    def __init__(self, spot, vec, from_core, with_x, from_x, with_y, from_y, from_line, sems):
        self.spot, self.vec, self.from_core, self.with_x = spot, vec, from_core, with_x
        self.from_x, self.with_y, self.from_y, self.from_line = from_x, with_y, from_y, from_line
        self.s, self.r, self.z_s, self.z_r = sems

    def hop(self, n):
        s = self.spot
        src, dst, to = (
            (self.vec.at[pl.ds(0, 8)], self.from_core, s.other_core),
            (self.with_x, self.from_x, s.beside_x),
            (self.with_y, self.from_y, s.beside_y),
        )[n]
        return remote(src, dst, self.s.at[n], self.r.at[n], to)

    def line(self, away):
        s = self.spot
        row = lax.rem(s.row + away, LINE)
        return remote(self.from_line.at[s.row], self.from_line.at[s.row], self.z_s.at[away], self.z_r.at[s.row], s.at_row(row))

    def step(self, n):
        if n == 0:
            self.hop(0).start()
        elif n == 1:
            self.hop(0).wait_recv()
            self.with_x[pl.ds(0, 8), :] = self.vec[pl.ds(0, 8), :] + self.from_core[...]
            self.with_x[pl.ds(8, 8), :] = self.vec[pl.ds(8, 8), :]
            self.hop(1).start()
        elif n == 2:
            self.hop(1).wait_recv()
            self.with_y[...] = self.with_x[...] + self.from_x[...]
            self.hop(2).start()
        elif n == 3:
            self.hop(2).wait_recv()
            self.from_line[self.spot.row] = self.with_y[...] + self.from_y[...]
            for away in range(1, LINE):
                self.line(away).start()

    def total(self):
        s = self.spot
        for row in s.near:
            block = self.from_line.at[row]
            pltpu.make_async_copy(block, block, self.z_r.at[row]).wait()
        return self.from_line[0] + self.from_line[1] + self.from_line[2] + self.from_line[3]

    def drain(self):
        for n in range(3):
            self.hop(n).wait_send()
        for away in range(1, LINE):
            self.line(away).wait_send()


SAVED = ("x_t", "qkv", "probs", "mixed_t", "unit", "inv", "h_t", "slope", "act_t", "dpre", "dout", "pars", "out")


def backward_kernel(*refs):
    it = iter(refs)

    def take(n):
        return [next(it) for _ in range(n)]

    wqkv_h, wo_h, wi_h, wout_h = take(GROUPS)
    saved = dict(zip(SAVED, take(len(SAVED))))
    (sums2,) = take(1)
    final = take(GROUPS)
    placed_out, placed_dx, o_norms, o_bias = take(4)
    wo, wi, wout, wst = take(4)
    parts = take(GROUPS)
    rel_a, rel_b, from_x, from_y, line, stage = (take(len(SCATTERED)) for _ in range(6))
    act_t, dout, h_t, dpre, unit, inv, pars, mixed_t, qkv = take(9)
    slope, probs, ds, dinner, part, recv1, recv2, dattn, dmixed, dqkv, dx = take(11)
    vecs = take(7)
    scat_sems, sum_sems = take(len(Scatter.SEMS)), take(len(Sums.SEMS))
    out_sems, dx_sems = take(2), take(2)
    core_s, core_r, load, st_sem, sl_sem, pr_sem = take(6)

    spot = Spot()
    scatter = Scatter(spot, parts, rel_a, rel_b, from_x, from_y, line, stage, final, scat_sems)
    totals = Sums(spot, *vecs, sum_sems)
    vec = vecs[0]
    place_out, place_dx = Spread(spot, saved["out"], placed_out, out_sems), Spread(spot, dx, placed_dx, dx_sems)
    seq, width = dout.shape
    hidden = dinner.shape[1]
    half = qkv.shape[1] // 3
    own = seq // 2
    cut = width // LINE
    mine, theirs = spot.col * own, (1 - spot.col) * own

    def rows_of(base, start, size):
        return pl.ds(pl.multiple_of(base + start * size, size), size)

    fetches = {}

    def fetch(name, src, dst):
        fetches[name] = pltpu.make_async_copy(src, dst, load.at[len(fetches)])
        fetches[name].start()

    def to_other(n, src, dst):
        return remote(src, dst, core_s.at[n], core_r.at[n], spot.other_core)

    def wout_grad(f):
        rows = at(f, 512)
        for r in range(LINE):
            parts[0][r, rows, :] = dot(act_t[rows, :], dout[:, pl.ds(r * cut, cut)]).astype(LOW)

    def slope_copy(f):
        slot = f % 2
        return pltpu.make_async_copy(saved["slope"].at[:, at(f, 256)], slope.at[slot], sl_sem.at[slot])

    def inner_grad(f):
        rows = at(f, 256)

        if f + 1 < hidden // 256:
            slope_copy(f + 1).start()

        total = dot_t(dout[:, pl.ds(0, cut)], wout[0, rows, :])
        for r in range(1, LINE):
            total += dot_t(dout[:, pl.ds(r * cut, cut)], wout[r, rows, :])
        slope_copy(f).wait()
        part[:, pl.ds(0, 256)] = total
        part[pl.ds(0, 8), pl.ds(256, 256)] = jnp.zeros((8, 256), F32)

        def block(i):
            here = at(i, 64)
            d = (part[here, pl.ds(0, 256)] * slope[f % 2, here, :]).astype(LOW)
            dinner[here, rows] = d
            part[pl.ds(0, 8), pl.ds(256, 256)] += fold(d.astype(F32))

        loop(seq // 64, block)
        row, col = f // 4, f % 4
        vec[pl.ds(9 + row, 1), at(col, 256)] = jnp.sum(part[pl.ds(0, 8), pl.ds(256, 256)], 0, keepdims=True)

    def hidden_grad(r):
        part[:, at(r, cut)] = dot_t(dinner[...], wi[r])

    def wi_grad(t):
        row = scatter.order[t]

        def chunk(n):
            cols = at(n, 512)
            parts[1][row, :, cols] = dot(h_t[at(row, cut), :], dinner[:, cols]).astype(LOW)

        loop(hidden // 512, chunk)

    def first_norm_back():
        part_sums = jnp.zeros((8, width), F32)

        def block(i, carry):
            b_sum, g_sum, s_sum = carry
            rows, there = at(i, BLOCK), rows_of(mine, i, BLOCK)
            dh = dpre[rows, :] + (part[there, :] + recv1[rows, :])
            one = unit[rows, :]
            s = dh * pars[1:2, :]
            scale = inv[rows, :][:, 0:1]
            d = scale * (s - jnp.mean(s, 1, keepdims=True) - one * jnp.mean(s * one, 1, keepdims=True))
            dpre[rows, :] = d
            d_low = d.astype(LOW)
            dattn[there, :] = d_low
            return b_sum + fold(d_low.astype(F32)), g_sum + fold(dh * one), s_sum + fold(dh)

        b_sum, g_sum, s_sum = lax.fori_loop(0, own // BLOCK, block, (part_sums, part_sums, part_sums))
        for i, v in enumerate((b_sum, g_sum, s_sum)):
            vec[pl.ds(i, 1), :] = jnp.sum(v, 0, keepdims=True)

    def mixed_grad(n):
        rows = at(n, 256)
        total = dot_t(dattn[:, pl.ds(0, cut)], wo[0, rows, :])
        for r in range(1, LINE):
            total += dot_t(dattn[:, pl.ds(r * cut, cut)], wo[r, rows, :])
        dmixed[:, rows] = total.astype(LOW)

    def wo_grad(r):
        parts[2][r] = dot(mixed_t[...], dattn[:, at(r, cut)]).astype(LOW)

    def probs_copy(head):
        return pltpu.make_async_copy(saved["probs"].at[head], probs.at[head % 4], pr_sem.at[head % 4])

    def attend_back(pair, i):
        lanes = pl.ds(pair * LANES, LANES)
        keys_at, values_at = pl.ds(half + pair * LANES, LANES), pl.ds(2 * half + pair * LANES, LANES)
        slots = [(2 * pair + h) % 4 for h in range(2)]

        def block(i):
            rows = at(i, LANES)
            grad = dmixed[rows, lanes]

            def head(h, total):
                dp = dot_t(grad * head_lanes(h, LOW), qkv[:, values_at])
                p = probs[slots[0] + h, rows, :].astype(F32)
                d = (p * (dp - jnp.sum(p * dp, 1, keepdims=True))).astype(LOW)
                ds[h, rows, :] = d
                return total + dot(d, qkv[:, keys_at]) * head_lanes(h, F32)

            total = lax.fori_loop(0, 2, head, jnp.zeros((LANES, LANES), F32))
            dqkv[rows, lanes] = (total * 0.125).astype(LOW)

        if i < seq // LANES:
            block(i)
            return
        queries_t, grad_t = qkv[:, lanes].T, dmixed[:, lanes].T
        dk = jnp.concatenate([dot(queries_t[h * HD : (h + 1) * HD], ds[h]) for h in range(2)], 0)
        dqkv[:, keys_at] = dk.astype(LOW).T
        dv = jnp.concatenate([dot(grad_t[h * HD : (h + 1) * HD], probs[slots[h]]) for h in range(2)], 0)
        dqkv[:, values_at] = dv.astype(LOW).T

    def qkv_sums():
        for i, base in enumerate((0, 2 * half)):
            cols = pl.ds(base, half)

            def block(n, carry):
                return carry + fold(dqkv[at(n, 64), cols].astype(F32))

            v = lax.fori_loop(0, seq // 64, block, jnp.zeros((8, half), F32))
            vec[pl.ds(8, 1), pl.ds(i * half, half)] = jnp.sum(v, 0, keepdims=True)

    def wqkv_grad(t):
        row = scatter.order[t]

        def chunk(n):
            cols = at(n, 512)
            parts[3][row, :, cols] = dot(h_t[at(row, cut), :], dqkv[:, cols]).astype(LOW)

        loop(3 * half // 512, chunk)

    def weight_copy(r):
        return pltpu.make_async_copy(wqkv_h.at[r], wst.at[r % 2], st_sem.at[r % 2])

    def input_grad(r):
        weight_copy(r).wait()
        part[:, pl.ds(r * cut, cut)] = dot_t(dqkv[...], wst[r % 2])
        if r + 2 < LINE:
            weight_copy(r + 2).start()

    def finish_input():
        def block(i):
            rows, there = at(i, BLOCK), rows_of(mine, i, BLOCK)
            dx[rows, :] = (dpre[rows, :] + (part[there, :] + recv2[rows, :])).astype(LOW)

        loop(own // BLOCK, block)

    their_half = part.at[pl.ds(pl.multiple_of(theirs, own), own)]
    my_rows = pl.ds(pl.multiple_of(mine, own), own)

    swap1, swap2 = to_other(0, their_half, recv1), to_other(2, their_half, recv2)
    pass_d = to_other(1, dattn.at[my_rows], dattn.at[my_rows])
    seen = set()

    def once(*what):
        new = what not in seen
        seen.add(what)
        return new

    def need(*names):
        for n in names:
            if once("fetched", n):
                fetches[n].wait()

    def do(what, *n):
        if what == SEND:
            scatter.first(*n)
            scatter.direct(*n)
        elif what == ADD_A:
            scatter.second_a(*n)
        elif what == ADD_B:
            scatter.second_b(*n)
        elif what == SUM_UP:
            scatter.third(*n)
        elif what == LINE_STEP:
            scatter.line_step(*n)
        elif what == BACK_X:
            scatter.fourth_x(*n)
        elif what == BACK_Y:
            scatter.fourth_y(*n)
        elif what == OUTER_W:
            wout_grad(*n)
        elif what == INNER:
            need("wout")
            inner_grad(*n)
        elif what == HIDDEN:
            need("wi")
            hidden_grad(*n)
            if n[0] == LINE - 1:
                swap1.start()
        elif what == INNER_W:
            need("h_t")
            wi_grad(*n)
            if n[0] == LINE - 1:
                fetch("x_t", saved["x_t"], h_t)
        elif what == NORM_BACK:
            need("dpre", "unit", "inv", "pars")
            swap1.wait_recv()
            first_norm_back()
            pass_d.start()
        elif what == MIXED:
            need("wo")
            if once("passed"):
                pass_d.wait_recv()
            mixed_grad(*n)
        elif what == ATTN_W:
            need("mixed_t")
            wo_grad(scatter.order[n[0]])
        elif what == ATTEND:
            need("qkv")
            pair, i = n
            if i == 0:
                for h in range(2):
                    probs_copy(2 * pair + h).wait()
            attend_back(pair, i)
            if i == seq // LANES:
                for h in range(2):
                    if 2 * pair + h + 4 < half // HD:
                        probs_copy(2 * pair + h + 4).start()
        elif what == QKV_W:
            need("x_t")
            wqkv_grad(*n)
        elif what == INPUT:
            if n[0] == 0:
                swap1.wait_send()
            input_grad(*n)
            if n[0] == LINE - 1:
                swap2.start()
        elif what == SUMS:
            qkv_sums()
            totals.step(0)
        elif what in (SUMS_X, SUMS_Y, SUMS_LINE):
            totals.step(1 + what - SUMS_X)
        elif what == INPUT_LAST:
            swap2.wait_recv()
            finish_input()
        elif what == PLACE_OUT:
            place_out.start()
        elif what == PLACE_INPUT:
            place_dx.start()

    fetch("dout", saved["dout"], dout)
    fetch("act_t", saved["act_t"], act_t)
    greet(spot, far=True)
    need("dout", "act_t")
    fetch("wout", wout_h, wout)
    slope_copy(0).start()
    fetch("wi", wi_h, wi)
    fetch("h_t", saved["h_t"], h_t)
    for name, dst in (("dpre", dpre), ("unit", unit), ("inv", inv), ("pars", pars)):
        fetch(name, saved[name], dst)
    fetch("wo", wo_h, wo)
    fetch("mixed_t", saved["mixed_t"], mixed_t)
    fetch("qkv", saved["qkv"], qkv)
    for head in range(4):
        probs_copy(head).start()
    weight_copy(0).start()
    weight_copy(1).start()
    vec[...] = jnp.zeros_like(vec)
    for i in range(3):
        vec[pl.ds(3 + i, 1), :] = jnp.sum(sums2[i], 0, keepdims=True)
    for step in BACKWARD_ORDER:
        do(*step)
    whole = totals.total()
    totals.drain()
    for i in range(8):
        o_bias[pl.ds(i, 1), :] = whole[8 + i : 9 + i, :]
    vecs[-1][0] = whole
    o_norms[...] = vecs[-1][0, pl.ds(0, 8), at(spot.row, cut)]
    for g in range(len(SCATTERED)):
        scatter.fifth(g)
    scatter.drain()
    for c in (swap2, pass_d):
        c.wait_send()
    place_out.wait()
    place_dx.wait()


def backward(weights, saved):
    wqkv, wo, wi, wout = weights
    shapes = [w.shape for w in (wout, wi, wo, wqkv)]
    seq, width = saved["dout"].shape
    half, hidden, own = wo.shape[1], wi.shape[2], seq // 2
    cut = width // LINE

    groups = Scatter.sizes(shapes)

    def each(f):
        return [pltpu.VMEM(f(*s), LOW) for s in groups]

    def like(name):
        return pltpu.VMEM(saved[name].shape, saved[name].dtype)

    placed = jax.ShapeDtypeStruct((2 * seq, cut), LOW)
    scratch = (
        [pltpu.VMEM(w.shape, LOW) for w in (wo, wi, wout)]
        + [pltpu.VMEM((2,) + wqkv.shape[1:], LOW)]
        + [pltpu.VMEM(s, LOW) for s in shapes]
        + each(lambda r, c, n: (n, r // 8, c)) * 2
        + each(lambda r, c, n: (n, r // 4, c)) * 2
        + each(lambda r, c, n: (LINE + 1, r if n == 1 else r // 4, c))
        + each(lambda r, c, n: (r // 4, c))
        + [like(n) for n in ("act_t", "dout", "h_t", "dpre", "unit", "inv", "pars", "mixed_t", "qkv")]
        + [
            pltpu.VMEM((2, seq, 256), F32), pltpu.VMEM((4, seq, seq), LOW), pltpu.VMEM((2, seq, seq), LOW),
            pltpu.VMEM((seq, hidden), LOW), pltpu.VMEM((seq, width), F32), pltpu.VMEM((own, width), F32),
            pltpu.VMEM((own, width), F32), pltpu.VMEM((seq, width), LOW), pltpu.VMEM((seq, half), LOW),
            pltpu.VMEM((seq, 3 * half), LOW), pltpu.VMEM((own, width), LOW),
        ]
        + [pltpu.VMEM(s, F32) for s in ((16, width), (8, width)) + ((16, width),) * 4 + ((LINE, 16, width),)]
        + Scatter.SEMS
        + Sums.SEMS
        + Spread.SEMS * 2
        + [pltpu.SemaphoreType.DMA((n,)) for n in (3, 3, 16, 2, 2, 4)]
    )
    res = pl.pallas_call(
        backward_kernel,
        name="backward",
        out_shape=[jax.ShapeDtypeStruct(s[1:], LOW) for s in shapes]
        + [placed] * 2
        + [jax.ShapeDtypeStruct((8, cut), F32), jax.ShapeDtypeStruct((8, width), F32)],
        in_specs=[ANYWHERE] * (GROUPS + len(SAVED)) + [IN_VMEM],
        out_specs=[ANYWHERE] * (GROUPS + 2) + [IN_VMEM] * 2,
        scratch_shapes=scratch,
        compiler_params=pltpu.CompilerParams(collective_id=1, has_side_effects=True, vmem_limit_bytes=63 * 2**20),
    )(*weights, *[saved[n] for n in SAVED], saved["sums"])
    return res


def finish_kernel(wqkv, wo, wi, wout, out, dx, norms, biases, *outs):
    wq_o, wk_o, wv_o, wo_o, wi_o, wout_o, out_o, dx_o, bq_o, bv_o, bi_o = outs[:11]
    half = wq_o.shape[1]
    for i, o in enumerate((wq_o, wk_o, wv_o)):
        o[...] = wqkv[:, i * half : (i + 1) * half].astype(F32)
    for src, dst in ((wo, wo_o), (wi, wi_o), (wout, wout_o)):
        dst[...] = src[...].astype(F32)
    out_o[...] = out[...]
    dx_o[...] = dx[...]

    @pl.when(pl.program_id(0) == 0)
    def _():
        bq_o[...] = biases[0, 0:half]
        bv_o[...] = biases[0, half : 2 * half]
        wide = biases.shape[1]
        for i in range(bi_o.shape[0] // wide):
            bi_o[i * wide : (i + 1) * wide] = biases[1 + i, :]
        for i, o in enumerate(outs[11:]):
            o[...] = norms[i, :]


def finish(wqkv, wo, wi, wout, out, dx, norms, biases, steps=2):
    half, cut = wqkv.shape[1] // 3, norms.shape[1]
    big = [(wqkv.shape[0], half)] * 3 + [w.shape for w in (wo, wi, wout)]

    def tiled(shape):
        return pl.BlockSpec((shape[0] // steps, shape[1]), lambda i: (i, 0))

    def whole(shape):
        return pl.BlockSpec(shape, lambda i: (0,) * len(shape))

    vectors = [(half,), (half,), (wi.shape[1],)] + [(cut,)] * 6
    return pl.pallas_call(
        finish_kernel,
        name="finish",
        grid=(steps,),
        out_shape=[jax.ShapeDtypeStruct(s, F32) for s in big]
        + [jax.ShapeDtypeStruct(v.shape, LOW) for v in (out, dx)]
        + [jax.ShapeDtypeStruct(s, F32) for s in vectors],
        in_specs=[tiled(v.shape) for v in (wqkv, wo, wi, wout, out, dx)] + [whole(norms.shape), whole(biases.shape)],
        out_specs=[tiled(s) for s in big] + [tiled(out.shape)] * 2 + [whole(s) for s in vectors],
        compiler_params=pltpu.CompilerParams(vmem_limit_bytes=63 * 2**20),
    )(wqkv, wo, wi, wout, out, dx, norms, biases)


def per_chip(
    hidden_in, segment_ids, query_weight, query_bias, key_weight, value_weight, value_bias, attn_out_weight,
    attn_out_bias, norm1_gain, first_norm_offset, inner_weight, inner_bias, outer_weight, outer_bias, norm2_gain,
    second_norm_offset, cotangent,
):
    half = query_weight.shape[1]
    small = (attn_out_bias, norm1_gain, first_norm_offset, outer_bias, norm2_gain, second_norm_offset)
    weights, saved = forward(
        hidden_in, cotangent, query_weight, key_weight, value_weight, attn_out_weight, inner_weight, outer_weight,
        segment_ids, query_bias, value_bias, inner_bias, small,
    )
    wout, wi, wo, wqkv, layer_out, input_grad, norms, biases = backward(weights, saved)
    wq, wk, wv, wo, wi, wout, layer_out, input_grad, bq, bv, bi, bo, g1, b1, bout, g2, b2 = finish(
        wqkv, wo, wi, wout, layer_out, input_grad, norms, biases
    )
    return layer_out, input_grad, wq, bq, wk, wv, bv, wo, bo, g1, b1, wi, bi, wout, bout, g2, b2


def solution(mesh):
    def whole(*args):
        segments, wq = args[1], args[2]
        sizes = tuple(mesh.shape[a] for a in ("dp", "row", "col"))
        fits = sizes == (4, LINE, 2) and segments.shape == (16, SEQ) and wq.shape[0] == MODEL_WIDTH
        body = per_chip if fits else shards
        return jax.shard_map(body, mesh=mesh, in_specs=IN_SPECS, out_specs=OUT_SPECS, check_vma=False)(*args)

    return whole
```

```python
import functools

import jax
import jax.numpy as jnp
from jax import lax
from jax.experimental import pallas as pl
from jax.experimental.pallas import tpu as pltpu
from jax.sharding import PartitionSpec as P

MODEL_WIDTH = 1024
HD = 64
SEQ = 512


norm_eps = 1e-12
inv_root_two = 0.7071067811865476
inv_root_two_pi = 0.3989422804014327


def product(left, right):
    return jnp.dot(left, right, preferred_element_type=jnp.float32)


def over_tokens(left, right):
    return lax.dot_general(
        left, right, (((0,), (0,)), ((), ())), preferred_element_type=jnp.float32
    )


def against(left, right):
    return lax.dot_general(
        left, right, (((1,), (1,)), ((), ())), preferred_element_type=jnp.float32
    )


def col_gather(values):
    return lax.all_gather(values, "col", axis=0, tiled=True)


def row_gather(values):
    return lax.all_gather(values, "row", axis=0, tiled=True)


def row_reduce(values):
    return lax.psum_scatter(values, "row", scatter_dimension=0, tiled=True)


def col_reduce(values):
    return lax.psum_scatter(values, "col", scatter_dimension=0, tiled=True)


def row_sum_values(first_branch, second_branch):
    return lax.psum((first_branch, second_branch), "row")


def apply_norm(preact_input, norm_gain, norm_offset):
    total, squares = row_sum_values(
        jnp.sum(preact_input, 1), jnp.sum(preact_input * preact_input, 1)
    )
    row_mean = total / MODEL_WIDTH
    inverse_deviation = lax.rsqrt(squares / MODEL_WIDTH - row_mean * row_mean + norm_eps)
    centred_rows = (preact_input - row_mean[:, None]) * inverse_deviation[:, None]
    return (centred_rows * norm_gain + norm_offset, centred_rows, inverse_deviation)


def norm_backward_pass(incoming_gradient, centred_rows, inverse_deviation, norm_gain):
    scaled_rows = incoming_gradient * norm_gain
    first_branch, second_branch = row_sum_values(
        jnp.sum(scaled_rows, 1), jnp.sum(scaled_rows * centred_rows, 1)
    )
    return inverse_deviation[:, None] * (
        scaled_rows
        - first_branch[:, None] / MODEL_WIDTH
        - centred_rows * second_branch[:, None] / MODEL_WIDTH
    )


def seg_mask(segments):
    return (segments[:, None] == segments[None, :])[None]


def attend_forward(items):
    queries, keys, values, segments = items
    scores = jnp.einsum("qhd,khd->hqk", queries, keys, preferred_element_type=jnp.float32) * 0.125
    scores = jnp.where(seg_mask(segments), scores, -1e30)
    peak = jnp.max(scores, -1, keepdims=True)
    expo = jnp.exp(scores - peak)
    total = jnp.sum(expo, -1, keepdims=True)
    probs = (expo / total).astype(jnp.bfloat16)
    mixed = jnp.einsum("hqk,khd->qhd", probs, values, preferred_element_type=jnp.float32)
    return (mixed.astype(jnp.bfloat16), (peak + jnp.log(total))[..., 0])


def attend_backward(items):
    queries, keys, values, segments, dmixed, lse = items
    scores = jnp.einsum("qhd,khd->hqk", queries, keys, preferred_element_type=jnp.float32) * 0.125
    probs = jnp.where(seg_mask(segments), jnp.exp(scores - lse[..., None]), 0.0)
    dvalues = jnp.einsum(
        "hqk,qhd->khd", probs.astype(jnp.bfloat16), dmixed, preferred_element_type=jnp.float32
    )
    dprobs = jnp.einsum("qhd,khd->hqk", dmixed, values, preferred_element_type=jnp.float32)
    middle = jnp.sum(probs * dprobs, -1, keepdims=True)
    dscores = (probs * (dprobs - middle)).astype(jnp.bfloat16)
    dqueries = jnp.einsum("hqk,khd->qhd", dscores, keys, preferred_element_type=jnp.float32) * 0.125
    dkeys = jnp.einsum("hqk,qhd->khd", dscores, queries, preferred_element_type=jnp.float32) * 0.125
    return (dqueries.astype(jnp.bfloat16), dkeys.astype(jnp.bfloat16), dvalues.astype(jnp.bfloat16))


def shards(
    hidden_in,
    segment_ids,
    query_weight,
    query_bias,
    key_weight,
    value_weight,
    value_bias,
    attn_out_weight,
    attn_out_bias,
    norm1_gain,
    first_norm_offset,
    inner_weight,
    inner_bias,
    outer_weight,
    outer_bias,
    norm2_gain,
    second_norm_offset,
    cotangent,
):
    local_seqs = segment_ids.shape[0]
    col_width = query_weight.shape[1]
    head_local = col_width // HD
    first_norm_gain = norm1_gain.astype(jnp.float32)
    second_norm_gain = norm2_gain.astype(jnp.float32)
    x_full = col_gather(hidden_in)
    part_q, part_k, part_v = (
        lax.psum_scatter(product(x_full, query_weight), "row", scatter_dimension=0, tiled=True),
        lax.psum_scatter(product(x_full, key_weight), "row", scatter_dimension=0, tiled=True),
        lax.psum_scatter(product(x_full, value_weight), "row", scatter_dimension=0, tiled=True),
    )
    queries = (part_q + query_bias).astype(jnp.bfloat16)
    keys = part_k.astype(jnp.bfloat16)
    values = (part_v + value_bias).astype(jnp.bfloat16)
    q_heads = queries.reshape(local_seqs, SEQ, head_local, HD)
    k_heads = keys.reshape(local_seqs, SEQ, head_local, HD)
    v_heads = values.reshape(local_seqs, SEQ, head_local, HD)
    mixed, lse = lax.map(attend_forward, (q_heads, k_heads, v_heads, segment_ids))
    mixed = mixed.reshape(local_seqs * SEQ, col_width)
    mixed_full = row_gather(mixed)
    attn = col_reduce(product(mixed_full, attn_out_weight)) + attn_out_bias
    first_preact = hidden_in.astype(jnp.float32) + attn
    hidden_state, first_centred_rows, first_inverse_deviation = apply_norm(
        first_preact, first_norm_gain, first_norm_offset
    )
    hidden_full = col_gather(hidden_state.astype(jnp.bfloat16))
    inner = row_reduce(product(hidden_full, inner_weight)) + inner_bias
    active = jax.nn.gelu(inner, approximate=False).astype(jnp.bfloat16)
    active_full = row_gather(active)
    outer_product = col_reduce(product(active_full, outer_weight)) + outer_bias
    closing_result, second_centred_rows, second_inverse_deviation = apply_norm(
        hidden_state + outer_product, second_norm_gain, second_norm_offset
    )
    layer_out = closing_result.astype(jnp.bfloat16)
    output_gradient = cotangent.astype(jnp.float32)
    second_gain_gradient = jnp.sum(output_gradient * second_centred_rows, 0)
    shift_two_grad = jnp.sum(output_gradient, 0)
    second_preact_grad = norm_backward_pass(
        output_gradient, second_centred_rows, second_inverse_deviation, second_norm_gain
    )
    dout_full = col_gather(second_preact_grad.astype(jnp.bfloat16))
    outer_bias_grad = jnp.sum(dout_full, 0, dtype=jnp.float32)
    outer_weight_grad = over_tokens(active_full, dout_full)
    dactive = row_reduce(against(dout_full, outer_weight))
    cdf = 0.5 * (1.0 + lax.erf(inner * inv_root_two))
    density = jnp.exp(-0.5 * inner * inner) * inv_root_two_pi
    dinner = (dactive * (cdf + inner * density)).astype(jnp.bfloat16)
    dinner_full = row_gather(dinner)
    inner_bias_grad = jnp.sum(dinner_full, 0, dtype=jnp.float32)
    inner_weight_grad = over_tokens(hidden_full, dinner_full)
    hidden_state_grad = second_preact_grad + col_reduce(against(dinner_full, inner_weight))
    first_gain_gradient = jnp.sum(hidden_state_grad * first_centred_rows, 0)
    shift_one_grad = jnp.sum(hidden_state_grad, 0)
    first_preact_grad = norm_backward_pass(
        hidden_state_grad, first_centred_rows, first_inverse_deviation, first_norm_gain
    )
    dattn_full = col_gather(first_preact_grad.astype(jnp.bfloat16))
    attn_out_bias_grad = jnp.sum(dattn_full, 0, dtype=jnp.float32)
    attn_out_weight_grad = over_tokens(mixed_full, dattn_full)
    dmixed = row_reduce(against(dattn_full, attn_out_weight)).astype(jnp.bfloat16)
    dq_heads, dk_heads, dv_heads = lax.map(
        attend_backward,
        (
            q_heads,
            k_heads,
            v_heads,
            segment_ids,
            dmixed.reshape(local_seqs, SEQ, head_local, HD),
            lse,
        ),
    )
    dq_rows = dq_heads.reshape(local_seqs * SEQ, col_width)
    dk_rows = dk_heads.reshape(local_seqs * SEQ, col_width)
    dv_rows = dv_heads.reshape(local_seqs * SEQ, col_width)
    dq_full, dk_full, dv_full = (
        lax.all_gather(dq_rows, "row", axis=0, tiled=True),
        lax.all_gather(dk_rows, "row", axis=0, tiled=True),
        lax.all_gather(dv_rows, "row", axis=0, tiled=True),
    )
    query_bias_grad = jnp.sum(dq_full, 0, dtype=jnp.float32)
    value_bias_grad = jnp.sum(dv_full, 0, dtype=jnp.float32)
    query_weight_grad = over_tokens(x_full, dq_full)
    key_weight_grad = over_tokens(x_full, dk_full)
    value_weight_grad = over_tokens(x_full, dv_full)
    dx_part = (
        against(dq_full, query_weight)
        + against(dk_full, key_weight)
        + against(dv_full, value_weight)
    )
    input_grad = (first_preact_grad + col_reduce(dx_part)).astype(jnp.bfloat16)
    summed = (
        lax.psum(query_weight_grad.astype(jnp.bfloat16), "dp").astype(jnp.float32),
        lax.psum(query_bias_grad.astype(jnp.bfloat16), "dp").astype(jnp.float32),
        lax.psum(key_weight_grad.astype(jnp.bfloat16), "dp").astype(jnp.float32),
        lax.psum(value_weight_grad.astype(jnp.bfloat16), "dp").astype(jnp.float32),
        lax.psum(value_bias_grad.astype(jnp.bfloat16), "dp").astype(jnp.float32),
        lax.psum(attn_out_weight_grad.astype(jnp.bfloat16), "dp").astype(jnp.float32),
        lax.psum(attn_out_bias_grad.astype(jnp.bfloat16), "dp").astype(jnp.float32),
        lax.psum(inner_weight_grad.astype(jnp.bfloat16), "dp").astype(jnp.float32),
        lax.psum(inner_bias_grad.astype(jnp.bfloat16), "dp").astype(jnp.float32),
        lax.psum(outer_weight_grad.astype(jnp.bfloat16), "dp").astype(jnp.float32),
        lax.psum(outer_bias_grad.astype(jnp.bfloat16), "dp").astype(jnp.float32),
    )
    norms = lax.psum(
        (first_gain_gradient, shift_one_grad, second_gain_gradient, shift_two_grad), ("dp", "col")
    )
    return (
        layer_out,
        input_grad,
        summed[0],
        summed[1],
        summed[2],
        summed[3],
        summed[4],
        summed[5],
        summed[6],
        norms[0],
        norms[1],
        summed[7],
        summed[8],
        summed[9],
        summed[10],
        norms[2],
        norms[3],
    )


IN_SPECS = (
    P(("dp", "col"), "row"),
    P(("dp", "row"), None),
    P("row", "col"),
    P("col"),
    P("row", "col"),
    P("row", "col"),
    P("col"),
    P("col", "row"),
    P("row"),
    P("row"),
    P("row"),
    P("row", "col"),
    P("col"),
    P("col", "row"),
    P("row"),
    P("row"),
    P("row"),
    P(("dp", "col"), "row"),
)
OUT_SPECS = (
    P(("dp", "col"), "row"),
    P(("dp", "col"), "row"),
    P("row", "col"),
    P("col"),
    P("row", "col"),
    P("row", "col"),
    P("col"),
    P("col", "row"),
    P("row"),
    P("row"),
    P("row"),
    P("row", "col"),
    P("col"),
    P("col", "row"),
    P("row"),
    P("row"),
    P("row"),
)


MESH = pl.DeviceIdType.MESH
LINE = 4
GROUPS = 4
GATHERED = ((1, 0, 8), (0, 0, 8), (2, 0, 8), (3, 0, 4), (3, 4, 4))
SCATTERED = (
    (0, 0, 2, True), (0, 2, 2, True), (0, 4, 2, True), (0, 6, 2, False), (1, 0, 8, False), (3, 0, 8, False),
    (2, 0, 8, False),
)


class Spot:
    def __init__(self):
        self.dp = lax.axis_index("dp")
        self.row = lax.axis_index("row")
        self.col = lax.axis_index("col")
        k, r = self.dp, self.row
        self.dp_x = k + 1 - 2 * lax.rem(k, 2)
        self.dp_y = lax.rem(k + 2, 4)
        self.dp_d = 3 - k
        self.beside_x = (self.dp_x, r, self.col)
        self.beside_y = (self.dp_y, r, self.col)
        self.other_core = (k, r, 1 - self.col)
        self.inside = jnp.logical_and(r > 0, r < LINE - 1)
        first = jnp.where(r > 0, r - 1, 1)
        second = jnp.where(r == 0, 2, jnp.where(r == LINE - 1, 1, r + 1))
        third = jnp.where(r < 2, LINE - 1, 0)
        self.near = (first, second, third)

    def at_row(self, row):
        return (self.dp, row, self.col)


def remote(src, dst, send, recv, device):
    return pltpu.make_async_remote_copy(
        src_ref=src, dst_ref=dst, send_sem=send, recv_sem=recv, device_id=device, device_id_type=MESH
    )


def greet(spot, far=False):
    barrier = pltpu.get_barrier_semaphore()

    def tell(device):
        pl.semaphore_signal(barrier, inc=1, device_id=device, device_id_type=MESH)

    if far:
        for away in range(LINE):
            row = lax.rem(spot.row + away, LINE)
            for core in (1, 2):
                if away or core == 1:
                    tell((spot.dp, row, lax.rem(spot.col + core, 2)))
        tell(spot.beside_x)
        tell(spot.beside_y)
        pl.semaphore_wait(barrier, 2 * LINE + 1)
        return
    for device in (spot.beside_x, spot.beside_y, spot.other_core):
        tell(device)

    @pl.when(spot.row > 0)
    def _():
        tell(spot.at_row(spot.row - 1))

    @pl.when(spot.row < LINE - 1)
    def _():
        tell(spot.at_row(spot.row + 1))

    pl.semaphore_wait(barrier, 3 + jnp.where(spot.inside, 2, 1))


class Gather:
    SEMS = (
        [pltpu.SemaphoreType.DMA((len(GATHERED), 2))]
        + [pltpu.SemaphoreType.DMA((GROUPS, 3))]
        + [pltpu.SemaphoreType.DMA((len(GATHERED), LINE))] * 10
    )

    def __init__(self, spot, shards, bufs, sems):
        self.spot, self.shards, self.bufs = spot, shards, bufs
        (self.own_s, self.own_l, self.zs, self.zr, self.xs, self.xr, self.ys, self.yr, self.fas, self.far, self.fbs, self.fbr) = sems
        self.loaded = set()

    def piece(self, g, row, j, half=None):
        which, first, count = GATHERED[g]
        eighth = self.bufs[which].shape[1] // 8
        q = eighth * count // 4
        size = q if half is None else q // 2
        start = first * eighth + j * q + (0 if half is None else half * size)
        return self.bufs[which].at[row, pl.ds(pl.multiple_of(start, size), size)]

    def own_copy(self, g, up):
        s = self.spot
        piece = self.piece(g, s.row, s.dp)
        row = s.row + 1 if up else s.row - 1
        return remote(piece, piece, self.own_s.at[g, int(up)], self.zr.at[g, s.row], s.at_row(row))

    def local(self, g):
        mine = self.bufs[g].at[self.spot.row]
        wide = self.shards[g][0].shape[1]
        return [
            pltpu.make_async_copy(part, mine.at[:, pl.ds(i * wide, wide)], self.own_l.at[g, i])
            for i, part in enumerate(self.shards[g])
        ]

    def load(self):
        for g in (1, 0, 2, 3):
            for c in self.local(g):
                c.start()

    def start_own(self, g):
        s = self.spot
        which = GATHERED[g][0]
        if which not in self.loaded:
            self.loaded.add(which)
            for c in self.local(which):
                c.wait()

        @pl.when(s.row < LINE - 1)
        def _():
            self.own_copy(g, True).start()

        @pl.when(s.row > 0)
        def _():
            self.own_copy(g, False).start()

    def onward(self, g, n):
        s = self.spot
        row = s.near[n]
        p = self.piece(g, row, s.dp)
        to = jnp.where(row < s.row, s.row + 1, s.row - 1)
        return remote(p, p, self.zs.at[g, row], self.zr.at[g, row], s.at_row(to))

    def across(self, g, n):
        s = self.spot
        row = s.near[n]
        p = self.piece(g, row, s.dp)
        return (
            remote(p, p, self.xs.at[g, row], self.xr.at[g, row], s.beside_x),
            remote(p, p, self.ys.at[g, row], self.yr.at[g, row], s.beside_y),
        )

    def relays(self, g, n):
        s = self.spot
        row = s.near[n]
        a = self.piece(g, row, s.dp_y, 0)
        b = self.piece(g, row, s.dp_x, 1)
        return (
            remote(a, a, self.fas.at[g, row], self.far.at[g, row], s.beside_x),
            remote(b, b, self.fbs.at[g, row], self.fbr.at[g, row], s.beside_y),
        )

    def z_step(self, g, n):
        self.onward(g, n).wait_recv()

        @pl.when(self.spot.inside)
        def _():
            self.onward(g, n).start()

        for c in self.across(g, n):
            c.start()

    def x_step(self, g, n):
        s = self.spot
        row = s.near[n]
        p = self.piece(g, row, s.dp_x)
        remote(p, p, self.xs.at[g, row], self.xr.at[g, row], s.beside_x).wait_recv()
        self.relays(g, n)[1].start()

    def y_step(self, g, n):
        s = self.spot
        row = s.near[n]
        p = self.piece(g, row, s.dp_y)
        remote(p, p, self.ys.at[g, row], self.yr.at[g, row], s.beside_y).wait_recv()
        self.relays(g, n)[0].start()

    def arrive(self, g, n):
        s = self.spot
        row = s.near[n]
        a, b = self.piece(g, row, s.dp_d, 0), self.piece(g, row, s.dp_d, 1)
        remote(a, a, self.fas.at[g, row], self.far.at[g, row], s.beside_x).wait_recv()
        remote(b, b, self.fbs.at[g, row], self.fbr.at[g, row], s.beside_y).wait_recv()

    def drain(self):
        s = self.spot
        for g in range(len(GATHERED)):

            @pl.when(s.row < LINE - 1)
            def _():
                self.own_copy(g, True).wait_send()

            @pl.when(s.row > 0)
            def _():
                self.own_copy(g, False).wait_send()

            for n in range(LINE - 1):

                @pl.when(s.inside)
                def _():
                    self.onward(g, n).wait_send()

                for c in self.across(g, n) + self.relays(g, n):
                    c.wait_send()


class Tokens:
    SEMS = [pltpu.SemaphoreType.DMA((2,)), pltpu.SemaphoreType.DMA((LINE,))] + [pltpu.SemaphoreType.DMA((LINE,))] * 2 + [
        pltpu.SemaphoreType.DMA((2, 2)),
        pltpu.SemaphoreType.DMA((LINE,)),
        pltpu.SemaphoreType.DMA((LINE,)),
        pltpu.SemaphoreType.DMA((LINE,)),
    ]

    def __init__(self, spot, x, ct, xs, cts, pars, sems):
        self.spot = spot
        self.x, self.ct, self.xs, self.cts, self.pars = x, ct, xs, cts, pars
        (self.x_s, self.x_r, self.x_fs, self.x_fr, self.c_s, self.c_r, self.p_s, self.p_r) = sems
        self.seq = x.shape[0] // 2
        self.wide = x.shape[1]

    def cols(self, ref, row):
        return ref.at[:, pl.ds(pl.multiple_of(row * self.wide, self.wide), self.wide)]

    def x_copy(self, i, local):
        s = self.spot
        row = 2 * s.col + i
        src = self.x.at[pl.ds(i * self.seq, self.seq)]
        dst = self.cols(self.xs, s.row)
        if local:
            return pltpu.make_async_copy(src, dst, self.x_r.at[s.row])
        return remote(src, dst, self.x_s.at[i], self.x_r.at[s.row], s.at_row(row))

    def ct_copy(self, i, core, local):
        s = self.spot
        half = self.seq // 2
        row = 2 * s.col + i
        src = self.ct.at[pl.ds(i * self.seq + core * half, half)]
        dst = self.cols(self.cts, s.row)
        if local:
            return pltpu.make_async_copy(src, dst, self.c_r.at[s.row])
        return remote(src, dst, self.c_s.at[i, core], self.c_r.at[s.row], (s.dp, row, jnp.int32(core)))

    def par_copy(self, away):
        s = self.spot
        row = lax.rem(s.row + away, LINE)
        mine = self.pars.at[s.row]
        return remote(mine, mine, self.p_s.at[away], self.p_r.at[s.row], s.at_row(row))

    def start_x(self):
        s = self.spot
        for i in range(2):
            here = 2 * s.col + i == s.row

            @pl.when(here)
            def _():
                self.x_copy(i, True).start()

            @pl.when(jnp.logical_not(here))
            def _():
                self.x_copy(i, False).start()

    def start_par(self):
        for away in range(1, LINE):
            self.par_copy(away).start()

    def start_ct(self):
        s = self.spot
        for i in range(2):
            for core in range(2):
                here = jnp.logical_and(2 * s.col + i == s.row, s.col == core)

                @pl.when(here)
                def _():
                    self.ct_copy(i, core, True).start()

                @pl.when(jnp.logical_not(here))
                def _():
                    self.ct_copy(i, core, False).start()

    def rows(self):
        return (self.spot.row,) + self.spot.near

    def relay(self, row):
        block = self.cols(self.xs, row)
        return remote(block, block, self.x_fs.at[row], self.x_fr.at[row], self.spot.other_core)

    def wait_x(self):
        s = self.spot
        first = s.row // 2 == s.col
        for row in self.rows():

            @pl.when(first)
            def _():
                block = self.cols(self.xs, row)
                pltpu.make_async_copy(block, block, self.x_r.at[row]).wait()
                self.relay(row).start()

    def wait_relayed(self):
        s = self.spot
        first = s.row // 2 == s.col
        for row in self.rows():

            @pl.when(jnp.logical_not(first))
            def _():
                self.relay(row).wait_recv()

    def wait_ct(self):
        for row in self.rows():
            block = self.cols(self.cts, row)
            pltpu.make_async_copy(block, block, self.c_r.at[row]).wait()

    def wait_par(self):
        for row in self.spot.near:
            block = self.pars.at[row]
            pltpu.make_async_copy(block, block, self.p_r.at[row]).wait()

    def drain(self):
        s = self.spot
        for i in range(2):

            @pl.when(jnp.logical_not(2 * s.col + i == s.row))
            def _():
                self.x_copy(i, False).wait_send()

            for core in range(2):

                @pl.when(jnp.logical_not(jnp.logical_and(2 * s.col + i == s.row, s.col == core)))
                def _():
                    self.ct_copy(i, core, False).wait_send()

        for away in range(1, LINE):
            self.par_copy(away).wait_send()

        @pl.when(s.row // 2 == s.col)
        def _():
            for row in self.rows():
                self.relay(row).wait_send()


ROWS_AT_ONCE = {1536: 16, 2048: 16, 256: 64}


class Scatter:
    SEMS = [pltpu.SemaphoreType.DMA((len(SCATTERED), LINE))] * 14 + [pltpu.SemaphoreType.DMA((len(SCATTERED),))] * 10

    @staticmethod
    def sizes(shapes):
        return [(shapes[b][1] // 8 * n, shapes[b][2], 1 if line else LINE) for b, _, n, line in SCATTERED]

    def __init__(self, spot, parts, rel_a, rel_b, from_x, from_y, line, stage, final, sems):
        self.spot, self.parts, self.rel_a, self.rel_b = spot, parts, rel_a, rel_b
        self.from_x, self.from_y, self.line, self.stage, self.final = from_x, from_y, line, stage, final
        (
            self.ra_s, self.ra_r, self.rb_s, self.rb_r,
            self.xa_s, self.xa_r, self.xb_s, self.xb_r,
            self.ya_s, self.ya_r, self.yb_s, self.yb_r,
            self.z_s, self.z_r,
            self.above_r, self.fx_s, self.fx_r, self.fy_s, self.fy_r,
            self.ha_s, self.ha_r, self.hb_s, self.hb_r, self.own_s,
        ) = sems
        self.order = (spot.near[2], spot.near[1], spot.near[0], spot.row)

    def rows(self, g, j, half):
        which, first, count, _ = SCATTERED[g]
        eighth = self.parts[which].shape[1] // 8
        if j is None:
            return pl.ds(first * eighth, count * eighth)
        q = eighth * count // 4
        size = q if half is None else q // 2
        start = first * eighth + j * q + (0 if half is None else half * size)
        return pl.ds(pl.multiple_of(start, size), size)

    def part(self, g, row, j=None, half=None):
        return self.parts[SCATTERED[g][0]].at[row, self.rows(g, j, half)]

    def fin(self, g, j, half=None):
        return self.final[SCATTERED[g][0]].at[self.rows(g, j, half)]

    def slot(self, g, t):
        return 0 if SCATTERED[g][3] else self.order[t]

    def half(self, ref, g, t, half):
        h = ref[g].shape[1] // 2
        return ref[g].at[self.slot(g, t), pl.ds(half * h, h)]

    def send_a(self, g, t):
        s, row = self.spot, self.order[t]
        return remote(self.part(g, row, s.dp_d, 0), self.rel_a[g].at[self.slot(g, t)], self.ra_s.at[g, row], self.ra_r.at[g, row], s.beside_y)

    def send_b(self, g, t):
        s, row = self.spot, self.order[t]
        return remote(self.part(g, row, s.dp_d, 1), self.rel_b[g].at[self.slot(g, t)], self.rb_s.at[g, row], self.rb_r.at[g, row], s.beside_x)

    def send_xa(self, g, t):
        s, row = self.spot, self.order[t]
        return remote(self.part(g, row, s.dp_x, 0), self.half(self.from_x, g, t, 0), self.xa_s.at[g, row], self.xa_r.at[g, row], s.beside_x)

    def send_xb(self, g, t):
        s, row = self.spot, self.order[t]
        return remote(self.part(g, row, s.dp_x, 1), self.half(self.from_x, g, t, 1), self.xb_s.at[g, row], self.xb_r.at[g, row], s.beside_x)

    def send_ya(self, g, t):
        s, row = self.spot, self.order[t]
        return remote(self.part(g, row, s.dp_y, 0), self.half(self.from_y, g, t, 0), self.ya_s.at[g, row], self.ya_r.at[g, row], s.beside_y)

    def send_yb(self, g, t):
        s, row = self.spot, self.order[t]
        return remote(self.part(g, row, s.dp_y, 1), self.half(self.from_y, g, t, 1), self.yb_s.at[g, row], self.yb_r.at[g, row], s.beside_y)

    def add(self, out, terms):
        rows, wide = out.shape
        step = min(ROWS_AT_ONCE[wide], rows)

        def body(i, carry):
            at = pl.ds(pl.multiple_of(i * step, step), step)
            total = terms[0][at, :].astype(jnp.float32)
            for t in terms[1:]:
                total = total + t[at, :].astype(jnp.float32)
            out[at, :] = total.astype(jnp.bfloat16)
            return carry

        lax.fori_loop(0, rows // step, body, 0)

    def first(self, g, t):
        self.send_a(g, t).start()
        self.send_b(g, t).start()

    def direct(self, g, t):
        self.send_xb(g, t).start()
        self.send_ya(g, t).start()

    def second_a(self, g, t):
        self.send_a(g, t).wait_recv()
        mine = self.part(g, self.order[t], self.spot.dp_x, 0)
        self.add(mine, (mine, self.rel_a[g].at[self.slot(g, t)]))
        self.send_xa(g, t).start()

    def second_b(self, g, t):
        self.send_b(g, t).wait_recv()
        mine = self.part(g, self.order[t], self.spot.dp_y, 1)
        self.add(mine, (mine, self.rel_b[g].at[self.slot(g, t)]))
        self.send_yb(g, t).start()

    def onward(self, g, t, above=False):
        s, row = self.spot, self.order[t]
        to = jnp.where(row > s.row, s.row + 1, s.row - 1)
        slot = jnp.where(row == s.row - 1, LINE, row)
        piece = self.part(g, row, None if SCATTERED[g][3] else s.dp)
        recv = self.above_r.at[g] if above else self.z_r.at[g, row]
        return remote(piece, self.line[g].at[slot], self.z_s.at[g, row], recv, s.at_row(to))

    def along(self, g, t, mine, terms, out):
        s, row = self.spot, self.order[t]
        if t < LINE - 1:
            passed = jnp.logical_or(jnp.logical_and(row > s.row, s.row > 0), jnp.logical_and(row < s.row, s.row < LINE - 1))
            last = row == s.row - 1

            @pl.when(passed)
            def _():
                self.onward(g, t).wait_recv()
                self.add(mine, terms + (self.line[g].at[row],))

            if len(terms) > 1:

                @pl.when(jnp.logical_not(passed))
                def _():
                    self.add(mine, terms)

            @pl.when(last)
            def _():
                self.onward(g, t, True).start()

            @pl.when(jnp.logical_not(last))
            def _():
                self.onward(g, t).start()

        else:
            below, over = self.line[g].at[s.row], self.line[g].at[LINE]

            def wait_below():
                remote(below, below, self.z_s.at[g, s.row], self.z_r.at[g, s.row], s.beside_x).wait_recv()

            def wait_over():
                remote(over, over, self.z_s.at[g, s.row], self.above_r.at[g], s.beside_x).wait_recv()

            @pl.when(s.inside)
            def _():
                wait_below()
                wait_over()
                self.add(out, terms + (below, over))

            @pl.when(s.row == 0)
            def _():
                wait_over()
                self.add(out, terms + (over,))

            @pl.when(s.row == LINE - 1)
            def _():
                wait_below()
                self.add(out, terms + (below,))

    def line_step(self, g, t):
        mine = self.part(g, self.order[t])
        self.along(g, t, mine, (mine,), mine)

    def third(self, g, t):
        s, row = self.spot, self.order[t]
        for c in (self.send_xa(g, t), self.send_xb(g, t), self.send_ya(g, t), self.send_yb(g, t)):
            c.wait_recv()
        mine = self.part(g, row, s.dp)
        slot = self.slot(g, t)
        terms = (mine, self.from_x[g].at[slot], self.from_y[g].at[slot])
        if SCATTERED[g][3]:
            self.add(self.stage[g], terms)
        else:
            self.along(g, t, mine, terms, self.stage[g])
        if t == LINE - 1:
            for c in self.spread(g):
                c.start()
            self.settle(g).start()

    def spread(self, g):
        s = self.spot
        p = self.fin(g, s.dp)
        mine = self.stage[g]
        return (
            remote(mine, p, self.fx_s.at[g], self.fx_r.at[g], s.beside_x),
            remote(mine, p, self.fy_s.at[g], self.fy_r.at[g], s.beside_y),
        )

    def settle(self, g):
        return pltpu.make_async_copy(self.stage[g], self.fin(g, self.spot.dp), self.own_s.at[g])

    def relays(self, g):
        s = self.spot
        a, b = self.fin(g, s.dp_y, 0), self.fin(g, s.dp_x, 1)
        return (
            remote(a, a, self.ha_s.at[g], self.ha_r.at[g], s.beside_x),
            remote(b, b, self.hb_s.at[g], self.hb_r.at[g], s.beside_y),
        )

    def fourth_x(self, g):
        s = self.spot
        p = self.fin(g, s.dp_x)
        remote(p, p, self.fx_s.at[g], self.fx_r.at[g], s.beside_x).wait_recv()
        self.relays(g)[1].start()

    def fourth_y(self, g):
        s = self.spot
        p = self.fin(g, s.dp_y)
        remote(p, p, self.fy_s.at[g], self.fy_r.at[g], s.beside_y).wait_recv()
        self.relays(g)[0].start()

    def fifth(self, g):
        s = self.spot
        a, b = self.fin(g, s.dp_d, 0), self.fin(g, s.dp_d, 1)
        remote(a, a, self.ha_s.at[g], self.ha_r.at[g], s.beside_x).wait_recv()
        remote(b, b, self.hb_s.at[g], self.hb_r.at[g], s.beside_y).wait_recv()

    def drain(self):
        for g in range(len(SCATTERED)):
            for t in range(LINE):
                if t == LINE - 1 or not SCATTERED[g][3]:
                    for c in (
                        self.send_a(g, t), self.send_b(g, t), self.send_xa(g, t),
                        self.send_xb(g, t), self.send_ya(g, t), self.send_yb(g, t),
                    ):
                        c.wait_send()
                if t < LINE - 1:
                    self.onward(g, t).wait_send()
            for c in self.spread(g) + self.relays(g):
                c.wait_send()
            self.settle(g).wait()


class Spread:
    SEMS = [pltpu.SemaphoreType.DMA((LINE,)), pltpu.SemaphoreType.DMA((4,))]

    def __init__(self, spot, src, out, sems):
        self.spot, self.src, self.out = spot, src, out
        self.s, self.r = sems
        self.count, wide = src.shape
        self.cut = wide // LINE

    def slot(self, n):
        return self.out.at[pl.ds(pl.multiple_of(n * self.count, self.count), self.count)]

    def copy(self, away, local=False):
        s = self.spot
        row = lax.rem(s.row + away, LINE)
        src = self.src.at[:, pl.ds(pl.multiple_of(row * self.cut, self.cut), self.cut)]
        n = 2 * lax.rem(s.row, 2) + s.col
        if local:
            return pltpu.make_async_copy(src, self.slot(n), self.r.at[n])
        return remote(src, self.slot(n), self.s.at[away], self.r.at[n], (s.dp, row, s.row // 2))

    def start(self):
        s = self.spot
        here = s.row // 2 == s.col

        @pl.when(here)
        def _():
            self.copy(0, True).start()

        @pl.when(jnp.logical_not(here))
        def _():
            self.copy(0).start()

        for away in range(1, LINE):
            self.copy(away).start()

    def wait(self):
        s = self.spot
        for n in range(4):
            pltpu.make_async_copy(self.slot(n), self.slot(n), self.r.at[n]).wait()

        @pl.when(jnp.logical_not(s.row // 2 == s.col))
        def _():
            self.copy(0).wait_send()

        for away in range(1, LINE):
            self.copy(away).wait_send()


(OWN, TOKENS_IN, COTANGENT_IN, ALONG, FROM_X, FROM_Y, TO_CORE, TURN_X, PROJECT, ATTEND, ATTN_OUT, NORM_1, TURN_H, GROW, SHRINK, NORM_2, LAST) = range(17)
(SEND, ADD_A, ADD_B, SUM_UP, LINE_STEP, BACK_X, BACK_Y, OUTER_W, INNER, HIDDEN, INNER_W, NORM_BACK, MIXED, ATTN_W, QKV_W, INPUT, SUMS, SUMS_X, SUMS_Y, SUMS_LINE, INPUT_LAST, PLACE_OUT, PLACE_INPUT) = range(17, 40)
FORWARD_ORDER = (
    (OWN, 0), (OWN, 1), (ALONG, 0, 0), (ALONG, 0, 1), (ALONG, 1, 0), (ALONG, 1, 1), (ALONG, 0, 2), (TOKENS_IN,),
    (FROM_Y, 0, 0), (FROM_X, 0, 0), (FROM_X, 1, 0), (FROM_X, 0, 1), (FROM_Y, 1, 0), (ALONG, 1, 2), (OWN, 2),
    (FROM_Y, 1, 1), (FROM_X, 1, 1), (FROM_Y, 1, 2), (FROM_X, 0, 2), (FROM_Y, 0, 2), (FROM_X, 1, 2), (FROM_Y, 0, 1),
    (TO_CORE,), (ALONG, 2, 0), (ALONG, 2, 1), (OWN, 3), (PROJECT, 0), (PROJECT, 1), (PROJECT, 2), (PROJECT, 3),
    (PROJECT, 4), (PROJECT, 5), (FROM_Y, 2, 0), (ATTEND, 0, 0), (FROM_X, 2, 0), (ALONG, 2, 2), (ATTEND, 0, 1),
    (OWN, 4), (ATTEND, 0, 2), (ATTEND, 0, 3), (ATTEND, 1, 0), (FROM_X, 2, 1), (ALONG, 3, 0), (ATTEND, 1, 1),
    (ALONG, 3, 1), (ATTEND, 1, 2), (ATTEND, 1, 3), (ATTEND, 2, 0), (ATTEND, 2, 1), (ATTEND, 2, 2), (ALONG, 4, 0),
    (ALONG, 4, 1), (ATTEND, 2, 3), (ATTEND, 3, 0), (ATTEND, 3, 1), (ATTEND, 3, 2), (FROM_Y, 2, 2), (ATTEND, 3, 3),
    (ATTN_OUT, 0), (ATTN_OUT, 1), (ATTN_OUT, 2), (ATTN_OUT, 3), (ALONG, 3, 2), (FROM_X, 2, 2), (FROM_Y, 2, 1),
    (TURN_X,), (FROM_Y, 4, 0), (FROM_X, 3, 1), (ALONG, 4, 2), (NORM_1,), (COTANGENT_IN,), (FROM_X, 4, 1),
    (FROM_Y, 3, 0), (FROM_X, 3, 0), (FROM_Y, 4, 1), (FROM_Y, 3, 1), (FROM_Y, 3, 2), (FROM_X, 4, 0), (FROM_X, 3, 2),
    (GROW, 0), (GROW, 1), (GROW, 2), (GROW, 3), (GROW, 4), (GROW, 5), (GROW, 6), (FROM_X, 4, 2), (GROW, 7),
    (FROM_Y, 4, 2), (SHRINK, 0), (SHRINK, 1), (SHRINK, 2), (SHRINK, 3), (TURN_H,), (NORM_2,), (LAST,),
)
BACKWARD_ORDER = (
    (PLACE_OUT,), (OUTER_W, 0), (OUTER_W, 1), (OUTER_W, 2), (OUTER_W, 3), (SEND, 3, 2), (INNER, 0), (INNER, 1),
    (SEND, 3, 1), (SEND, 3, 3), (SEND, 3, 0), (INNER, 2), (INNER, 3), (INNER, 4), (INNER, 5), (INNER, 6), (INNER, 7),
    (INNER_W, 0), (SEND, 4, 0), (LINE_STEP, 0, 0), (INNER_W, 1), (SEND, 4, 1), (HIDDEN, 0), (HIDDEN, 1),
    (ADD_B, 4, 0), (HIDDEN, 2), (HIDDEN, 3), (ADD_A, 3, 1), (ADD_A, 3, 2), (ADD_A, 3, 0), (LINE_STEP, 0, 1),
    (INNER_W, 2), (SEND, 4, 2), (ADD_A, 3, 3), (ADD_B, 3, 3), (NORM_BACK,), (LINE_STEP, 1, 0), (INNER_W, 3),
    (LINE_STEP, 0, 2), (ADD_A, 4, 1), (MIXED, 0), (SEND, 4, 3), (ATTN_W, 0), (MIXED, 1), (ATTEND, 0, 0),
    (ADD_B, 4, 2), (ADD_B, 4, 1), (ATTEND, 0, 1), (ATTEND, 0, 2), (ATTN_W, 1), (ATTEND, 0, 3), (ATTEND, 0, 4),
    (ADD_A, 4, 2), (ATTEND, 1, 0), (ATTEND, 1, 1), (ATTEND, 1, 2), (LINE_STEP, 1, 1), (ADD_A, 4, 0), (ATTN_W, 2),
    (ATTEND, 1, 3), (ATTN_W, 3), (LINE_STEP, 1, 2), (SEND, 6, 2), (ADD_B, 3, 1), (ADD_A, 4, 3), (ATTEND, 1, 4),
    (ADD_B, 4, 3), (SEND, 6, 0), (ATTEND, 2, 0), (ATTEND, 2, 1), (SEND, 6, 1), (SEND, 6, 3), (ATTEND, 2, 2),
    (ATTEND, 2, 3), (ATTEND, 2, 4), (ADD_B, 3, 0), (LINE_STEP, 0, 3), (ATTEND, 3, 0), (ATTEND, 3, 1), (SEND, 0, 3),
    (LINE_STEP, 2, 0), (ATTEND, 3, 2), (ATTEND, 3, 3), (ATTEND, 3, 4), (QKV_W, 0), (SEND, 5, 0), (QKV_W, 1),
    (SUM_UP, 4, 0), (QKV_W, 2), (ADD_B, 0, 3), (ADD_A, 0, 3), (ADD_A, 6, 0), (SEND, 5, 1), (LINE_STEP, 2, 1),
    (ADD_B, 6, 1), (ADD_B, 6, 3), (SUMS,), (SEND, 5, 2), (LINE_STEP, 2, 2), (INPUT, 0), (SUM_UP, 0, 3), (ADD_A, 6, 2),
    (INPUT, 1), (LINE_STEP, 1, 3), (SUMS_X,), (ADD_B, 5, 1), (SEND, 1, 3), (ADD_A, 6, 1), (ADD_B, 6, 0), (QKV_W, 3),
    (SUM_UP, 3, 0), (ADD_A, 6, 3), (ADD_B, 6, 2), (ADD_A, 5, 0), (SUM_UP, 4, 1), (SUM_UP, 4, 2), (ADD_B, 5, 0),
    (SEND, 5, 3), (ADD_A, 1, 3), (INPUT, 2), (ADD_B, 3, 2), (ADD_B, 1, 3), (BACK_X, 0), (LINE_STEP, 2, 3),
    (ADD_A, 5, 1), (SUM_UP, 6, 0), (SEND, 2, 3), (ADD_A, 5, 2), (ADD_B, 5, 2), (BACK_Y, 0), (INPUT, 3),
    (SUM_UP, 5, 0), (SUMS_Y,), (SUM_UP, 6, 1), (ADD_A, 2, 3), (SUM_UP, 4, 3), (SUM_UP, 3, 1), (ADD_A, 5, 3),
    (ADD_B, 5, 3), (SUM_UP, 5, 1), (SUM_UP, 3, 2), (SUM_UP, 5, 2), (ADD_B, 2, 3), (INPUT_LAST,), (SUM_UP, 6, 2),
    (PLACE_INPUT,), (SUM_UP, 1, 3), (SUM_UP, 3, 3), (SUM_UP, 2, 3), (SUM_UP, 5, 3), (BACK_Y, 3), (SUMS_LINE,),
    (SUM_UP, 6, 3), (BACK_X, 4), (BACK_Y, 2), (BACK_X, 3), (BACK_X, 1), (BACK_Y, 5), (BACK_X, 2), (BACK_Y, 1),
    (BACK_Y, 4), (BACK_X, 5), (BACK_Y, 6), (BACK_X, 6),
)


F32, LOW = jnp.float32, jnp.bfloat16
ANYWHERE = pl.BlockSpec(memory_space=pl.ANY)
IN_VMEM = pl.BlockSpec(memory_space=pltpu.VMEM)
LANES = 128
BLOCK = 32


def at(start, size):
    return pl.ds(pl.multiple_of(start * size, size), size)


def dot(a, b):
    return jnp.dot(a, b, preferred_element_type=F32)


def dot_t(a, b):
    return lax.dot_general(a, b, (((1,), (1,)), ((), ())), preferred_element_type=F32)


def loop(count, body):
    def step(i, carry):
        body(i)
        return carry

    lax.fori_loop(0, count, step, 0)


def head_lanes(half, dtype):
    lane = lax.broadcasted_iota(jnp.int32, (1, LANES), 1)
    return jnp.where((lane < HD) == (half == 0), 1.0, 0.0).astype(dtype)


def fold(values):
    return jnp.sum(values.reshape(values.shape[0] // 8, 8, values.shape[1]), 0)


def forward_kernel(*refs):
    it = iter(refs)

    def take(n):
        return [next(it) for _ in range(n)]

    x, ct, wq, wk, wv, wo_s, wi_s, wout_s = take(8)
    seg, bq, bv, bi = take(4)
    small = take(6)
    out_w = take(GROUPS)
    o_xt, o_qkv, o_probs, o_mixed_t, o_unit, o_inv, o_h_t, o_slope, o_act_t, o_dpre, o_dout, o_pars, o_out, o_sums = take(14)
    bufs = take(GROUPS)
    xs, cts, pars4, pars, qkv, qkv_bias, probs, mask, mixed, part, recv1, recv2 = take(12)
    unit, inv, h1, h_low, inner, slope, act, act_t, h_t, x_t, mixed_t, dpre, dout, out, sums = take(15)
    tok_sems, gat_sems = take(len(Tokens.SEMS)), take(len(Gather.SEMS))
    core_s, core_r, save = take(3)

    spot = Spot()
    gather = Gather(spot, ((wq, wk, wv), (wo_s,), (wi_s,), (wout_s,)), bufs, gat_sems)
    tokens = Tokens(spot, x, ct, xs, cts, pars4, tok_sems)
    wqkv, wo, wi, wout = bufs
    seq, width = xs.shape
    own = seq // 2
    half = qkv.shape[1] // 3
    mine, theirs = spot.col * own, (1 - spot.col) * own

    def rows_of(base, start, size):
        return pl.ds(pl.multiple_of(base + start * size, size), size)

    gather.load()
    pars4[spot.row] = jnp.zeros(pars4.shape[1:], F32)
    for i, p in enumerate(small):
        pars4[spot.row, pl.ds(i, 1), :] = p[...].astype(F32).reshape(1, -1)
    greet(spot)

    saves = []

    def keep(src, dst):
        c = pltpu.make_async_copy(src, dst, save.at[len(saves)])
        c.start()
        saves.append(c)

    def to_other(n, src, dst):
        return remote(src, dst, core_s.at[n], core_r.at[n], spot.other_core)

    def make_mask():
        values = seg[...].astype(F32)
        for i in range(seq // LANES):
            down = jnp.broadcast_to(values[:, i * LANES : (i + 1) * LANES], (LANES, LANES)).T
            for j in range(seq // LANES):
                across = values[:, j * LANES : (j + 1) * LANES]
                mask[pl.ds(i * LANES, LANES), pl.ds(j * LANES, LANES)] = jnp.where(down == across, 0.0, -1e30)
        qkv_bias[:, pl.ds(0, half)] = jnp.broadcast_to(bq[...].astype(F32).reshape(1, half), (8, half))
        qkv_bias[:, pl.ds(half, half)] = jnp.zeros((8, half), F32)
        qkv_bias[:, pl.ds(2 * half, half)] = jnp.broadcast_to(bv[...].astype(F32).reshape(1, half), (8, half))

    def spread_pars():
        for r in range(LINE):
            pars[:, pl.ds(r * (width // LINE), width // LINE)] = pars4[r]

    def project(n):
        def chunk(c):
            cols = at(c, 256)
            w = wqkv[:, :, cols].reshape(width, 256)
            value = (dot(xs[...], w) + qkv_bias[0:1, cols]).astype(LOW).astype(F32)
            qkv[:, cols] = (value * jnp.where(c < half // 256, 0.125, 1.0)).astype(LOW)

        chunk(n)

    def transpose_x():
        loop(width // LANES, lambda c: x_t.__setitem__((at(c, LANES), slice(None)), xs[:, at(c, LANES)].T))

    def attend(pair, i):
        lanes = pl.ds(pair * LANES, LANES)
        keys = qkv[:, pl.ds(half + pair * LANES, LANES)]
        values = qkv[:, pl.ds(2 * half + pair * LANES, LANES)]

        def block(i):
            rows = at(i, LANES)
            queries = qkv[rows, lanes]

            def head(h, total):
                scores = dot_t(queries * head_lanes(h, LOW), keys) + mask[rows, :]
                expo = jnp.exp(scores - jnp.max(scores, 1, keepdims=True))
                p = (expo / jnp.sum(expo, 1, keepdims=True)).astype(LOW)
                probs[2 * pair + h, rows, :] = p
                return total + dot(p, values) * head_lanes(h, F32)

            total = lax.fori_loop(0, 2, head, jnp.zeros((LANES, LANES), F32))
            mixed[rows, lanes] = total.astype(LOW)

        block(i)
        if i == seq // LANES - 1:
            mixed_t[lanes, :] = mixed[:, lanes].T

    def attn_out(r):
        part[:, pl.ds(r * 256, 256)] = dot(mixed[...], wo[r])

    def first_norm():
        def block(i):
            rows, there = at(i, BLOCK), rows_of(mine, i, BLOCK)
            value = xs[there, :].astype(F32) + (part[there, :] + recv1[rows, :] + pars[0:1, :])
            centred = value - jnp.mean(value, 1, keepdims=True)
            scale = lax.rsqrt(jnp.mean(centred * centred, 1, keepdims=True) + norm_eps)
            one = centred * scale
            unit[rows, :] = one
            inv[rows, :] = jnp.broadcast_to(scale, (BLOCK, LANES))
            h = one * pars[1:2, :] + pars[2:3, :]
            h1[rows, :] = h
            h_low[there, :] = h.astype(LOW)

        loop(own // BLOCK, block)

    def transpose_h():
        loop(width // LANES, lambda c: h_t.__setitem__((at(c, LANES), slice(None)), h_low[:, at(c, LANES)].T))

    def grow(c):
        cols = at(c, 256)
        inner[...] = dot(h_low[...], wi[:, :, cols].reshape(width, 256))
        bias = bi[cols].astype(F32).reshape(1, 256)

        def block(i):
            rows = at(i, 64)
            v = inner[rows, :] + bias
            cdf = 0.5 * (1.0 + lax.erf(v * inv_root_two))
            slope[rows, cols] = cdf + v * (jnp.exp(-0.5 * v * v) * inv_root_two_pi)
            act[rows, cols] = (v * cdf).astype(LOW)

        loop(seq // 64, block)
        act_t[cols, :] = act[:, cols].T

    def shrink(r):
        part[:, at(r, 256)] = dot(act[...], wout[r])

    def second_norm():
        sums[...] = jnp.zeros_like(sums)

        def block(i):
            rows, there = at(i, BLOCK), rows_of(mine, i, BLOCK)
            value = h1[rows, :] + (part[there, :] + recv2[rows, :] + pars[3:4, :])
            centred = value - jnp.mean(value, 1, keepdims=True)
            scale = lax.rsqrt(jnp.mean(centred * centred, 1, keepdims=True) + norm_eps)
            one = centred * scale
            out[rows, :] = (one * pars[4:5, :] + pars[5:6, :]).astype(LOW)
            dy = cts[rows, :].astype(F32)
            s = dy * pars[4:5, :]
            d = scale * (s - jnp.mean(s, 1, keepdims=True) - one * jnp.mean(s * one, 1, keepdims=True))
            dpre[rows, :] = d
            d_low = d.astype(LOW)
            dout[there, :] = d_low
            sums[0] += fold(d_low.astype(F32))
            sums[1] += fold(dy * one)
            sums[2] += fold(dy)

        loop(own // BLOCK, block)

    seen = set()

    def once(*what):
        new = what not in seen
        seen.add(what)
        return new

    def arrived(which, turns=range(LINE - 1)):
        for g in range(len(GATHERED)):
            for n in turns:
                if GATHERED[g][0] == which and once("arrived", g, n):
                    gather.arrive(g, n)

    def relayed():
        if once("relayed"):
            tokens.wait_relayed()

    their_half = part.at[pl.ds(pl.multiple_of(theirs, own), own)]
    my_rows = pl.ds(pl.multiple_of(mine, own), own)
    first = to_other(0, their_half, recv1)

    def second(row):
        cols = at(row, 256)
        return to_other(
            4 + row, part.at[pl.ds(pl.multiple_of(theirs, own), own), cols], recv2.at[:, cols]
        )

    pass_h, pass_d = to_other(1, *[h_low.at[my_rows]] * 2), to_other(3, *[dout.at[my_rows]] * 2)

    def hidden_there():
        if once("hidden"):
            pass_h.wait_recv()

    def do(what, *n):
        if what == OWN:
            gather.start_own(*n)
        elif what == TOKENS_IN:
            tokens.start_x()
            tokens.start_par()
        elif what == COTANGENT_IN:
            tokens.start_ct()
        elif what == ALONG:
            gather.z_step(*n)
        elif what == FROM_X:
            gather.x_step(*n)
        elif what == FROM_Y:
            gather.y_step(*n)
        elif what == TO_CORE:
            tokens.wait_x()
        elif what == TURN_X:
            relayed()
            transpose_x()
            keep(x_t, o_xt)
        elif what == PROJECT:
            relayed()
            arrived(0)
            project(*n)
            if n[0] == 5:
                keep(wqkv, out_w[0])
                keep(qkv, o_qkv)
        elif what == ATTEND:
            attend(*n)
            if n == (3, 3):
                keep(probs, o_probs)
                keep(mixed_t, o_mixed_t)
        elif what == ATTN_OUT:
            arrived(1)
            attn_out(*n)
            if n[0] == LINE - 1:
                keep(wo, out_w[1])
                first.start()
        elif what == NORM_1:
            tokens.wait_par()
            spread_pars()
            keep(pars, o_pars)
            first.wait_recv()
            first_norm()
            pass_h.start()
            keep(unit, o_unit)
            keep(inv, o_inv)
        elif what == TURN_H:
            hidden_there()
            transpose_h()
            keep(h_t, o_h_t)
        elif what == GROW:
            hidden_there()
            arrived(2)
            grow(*n)
            if n[0] == hidden // 256 - 1:
                keep(wi, out_w[2])
                keep(slope, o_slope)
                keep(act_t, o_act_t)
        elif what == SHRINK:
            if n[0]:
                arrived(3, (n[0] - 1,))
            elif once("sent"):
                first.wait_send()
            row = spot.near[n[0] - 1] if n[0] else spot.row
            shrink(row)
            keep(wout.at[row], out_w[3].at[row])
            second(row).start()
        elif what == NORM_2:
            tokens.wait_ct()
            for row in range(LINE):
                second(row).wait_recv()
            second_norm()
            pass_d.start()
            keep(dpre, o_dpre)
            keep(out, o_out)
            keep(sums, o_sums)
        elif what == LAST:
            pass_d.wait_recv()
            keep(dout, o_dout)

    hidden = act.shape[1]
    make_mask()
    for step in FORWARD_ORDER:
        do(*step)
    for c in (pass_h, pass_d, *(second(row) for row in range(LINE))):
        c.wait_send()
    gather.drain()
    tokens.drain()
    for c in saves:
        c.wait()


def forward(x, ct, wq, wk, wv, wo, wi, wout, seg, bq, bv, bi, small):
    half, hidden = wq.shape[1], wi.shape[1]
    seq, width = x.shape[0] // 2, MODEL_WIDTH
    own, heads = seq // 2, half // HD
    weights = [((LINE, wq.shape[0], 3 * half), LOW), ((LINE,) + wo.shape, LOW), ((LINE,) + wi.shape, LOW), ((LINE,) + wout.shape, LOW)]
    named = dict(
        xs=((seq, width), LOW), cts=((own, width), LOW), pars4=((LINE, 8, width // LINE), F32), pars=((8, width), F32),
        qkv=((seq, 3 * half), LOW), qkv_bias=((8, 3 * half), F32), probs=((heads, seq, seq), LOW), mask=((seq, seq), F32),
        mixed=((seq, half), LOW), part=((seq, width), F32), recv1=((own, width), F32), recv2=((own, width), F32),
        unit=((own, width), F32), inv=((own, LANES), F32), h1=((own, width), F32), h_low=((seq, width), LOW),
        inner=((seq, 256), F32), slope=((seq, hidden), F32), act=((seq, hidden), LOW), act_t=((hidden, seq), LOW),
        h_t=((width, seq), LOW), x_t=((width, seq), LOW), mixed_t=((half, seq), LOW), dpre=((own, width), F32),
        dout=((seq, width), LOW), out=((own, width), LOW), sums=((3, 8, width), F32),
    )
    saved = ("x_t", "qkv", "probs", "mixed_t", "unit", "inv", "h_t", "slope", "act_t", "dpre", "dout", "pars", "out", "sums")
    outs = weights + [named[n] for n in saved]
    res = pl.pallas_call(
        forward_kernel,
        name="forward",
        out_shape=[jax.ShapeDtypeStruct(*o) for o in outs],
        in_specs=[ANYWHERE] * 8 + [IN_VMEM] * (4 + len(small)),
        out_specs=[ANYWHERE] * len(outs),
        scratch_shapes=[pltpu.VMEM(*w) for w in weights]
        + [pltpu.VMEM(*named[n]) for n in named]
        + Tokens.SEMS
        + Gather.SEMS
        + [pltpu.SemaphoreType.DMA((4 + LINE,)), pltpu.SemaphoreType.DMA((4 + LINE,)), pltpu.SemaphoreType.DMA((len(outs) + LINE,))],
        compiler_params=pltpu.CompilerParams(collective_id=0, has_side_effects=True, vmem_limit_bytes=60 * 2**20),
    )(x, ct, wq, wk, wv, wo, wi, wout, seg, bq, bv, bi, *small)
    return res[:GROUPS], dict(zip(saved, res[GROUPS:]))


class Sums:
    SEMS = [pltpu.SemaphoreType.DMA((3,)), pltpu.SemaphoreType.DMA((3,)), pltpu.SemaphoreType.DMA((LINE,)), pltpu.SemaphoreType.DMA((LINE,))]

    def __init__(self, spot, vec, from_core, with_x, from_x, with_y, from_y, from_line, sems):
        self.spot, self.vec, self.from_core, self.with_x = spot, vec, from_core, with_x
        self.from_x, self.with_y, self.from_y, self.from_line = from_x, with_y, from_y, from_line
        self.s, self.r, self.z_s, self.z_r = sems

    def hop(self, n):
        s = self.spot
        src, dst, to = (
            (self.vec.at[pl.ds(0, 8)], self.from_core, s.other_core),
            (self.with_x, self.from_x, s.beside_x),
            (self.with_y, self.from_y, s.beside_y),
        )[n]
        return remote(src, dst, self.s.at[n], self.r.at[n], to)

    def line(self, away):
        s = self.spot
        row = lax.rem(s.row + away, LINE)
        return remote(self.from_line.at[s.row], self.from_line.at[s.row], self.z_s.at[away], self.z_r.at[s.row], s.at_row(row))

    def step(self, n):
        if n == 0:
            self.hop(0).start()
        elif n == 1:
            self.hop(0).wait_recv()
            self.with_x[pl.ds(0, 8), :] = self.vec[pl.ds(0, 8), :] + self.from_core[...]
            self.with_x[pl.ds(8, 8), :] = self.vec[pl.ds(8, 8), :]
            self.hop(1).start()
        elif n == 2:
            self.hop(1).wait_recv()
            self.with_y[...] = self.with_x[...] + self.from_x[...]
            self.hop(2).start()
        elif n == 3:
            self.hop(2).wait_recv()
            self.from_line[self.spot.row] = self.with_y[...] + self.from_y[...]
            for away in range(1, LINE):
                self.line(away).start()

    def total(self):
        s = self.spot
        for row in s.near:
            block = self.from_line.at[row]
            pltpu.make_async_copy(block, block, self.z_r.at[row]).wait()
        return self.from_line[0] + self.from_line[1] + self.from_line[2] + self.from_line[3]

    def drain(self):
        for n in range(3):
            self.hop(n).wait_send()
        for away in range(1, LINE):
            self.line(away).wait_send()


SAVED = ("x_t", "qkv", "probs", "mixed_t", "unit", "inv", "h_t", "slope", "act_t", "dpre", "dout", "pars", "out")


def backward_kernel(*refs):
    it = iter(refs)

    def take(n):
        return [next(it) for _ in range(n)]

    wqkv_h, wo_h, wi_h, wout_h = take(GROUPS)
    saved = dict(zip(SAVED, take(len(SAVED))))
    (sums2,) = take(1)
    final = take(GROUPS)
    placed_out, placed_dx, o_norms, o_bias = take(4)
    wo, wi, wout, wst = take(4)
    parts = take(GROUPS)
    rel_a, rel_b, from_x, from_y, line, stage = (take(len(SCATTERED)) for _ in range(6))
    act_t, dout, h_t, dpre, unit, inv, pars, mixed_t, qkv = take(9)
    slope, probs, ds, dinner, part, recv1, recv2, dattn, dmixed, dqkv, dx = take(11)
    vecs = take(7)
    scat_sems, sum_sems = take(len(Scatter.SEMS)), take(len(Sums.SEMS))
    out_sems, dx_sems = take(2), take(2)
    core_s, core_r, load, st_sem, sl_sem, pr_sem = take(6)

    spot = Spot()
    scatter = Scatter(spot, parts, rel_a, rel_b, from_x, from_y, line, stage, final, scat_sems)
    totals = Sums(spot, *vecs, sum_sems)
    vec = vecs[0]
    place_out, place_dx = Spread(spot, saved["out"], placed_out, out_sems), Spread(spot, dx, placed_dx, dx_sems)
    seq, width = dout.shape
    hidden = dinner.shape[1]
    half = qkv.shape[1] // 3
    own = seq // 2
    cut = width // LINE
    mine, theirs = spot.col * own, (1 - spot.col) * own

    def rows_of(base, start, size):
        return pl.ds(pl.multiple_of(base + start * size, size), size)

    fetches = {}

    def fetch(name, src, dst):
        fetches[name] = pltpu.make_async_copy(src, dst, load.at[len(fetches)])
        fetches[name].start()

    def to_other(n, src, dst):
        return remote(src, dst, core_s.at[n], core_r.at[n], spot.other_core)

    def wout_grad(f):
        rows = at(f, 512)
        for r in range(LINE):
            parts[0][r, rows, :] = dot(act_t[rows, :], dout[:, pl.ds(r * cut, cut)]).astype(LOW)

    def slope_copy(f):
        slot = f % 2
        return pltpu.make_async_copy(saved["slope"].at[:, at(f, 256)], slope.at[slot], sl_sem.at[slot])

    def inner_grad(f):
        rows = at(f, 256)

        if f + 1 < hidden // 256:
            slope_copy(f + 1).start()

        total = dot_t(dout[:, pl.ds(0, cut)], wout[0, rows, :])
        for r in range(1, LINE):
            total += dot_t(dout[:, pl.ds(r * cut, cut)], wout[r, rows, :])
        slope_copy(f).wait()
        part[:, pl.ds(0, 256)] = total
        part[pl.ds(0, 8), pl.ds(256, 256)] = jnp.zeros((8, 256), F32)

        def block(i):
            here = at(i, 64)
            d = (part[here, pl.ds(0, 256)] * slope[f % 2, here, :]).astype(LOW)
            dinner[here, rows] = d
            part[pl.ds(0, 8), pl.ds(256, 256)] += fold(d.astype(F32))

        loop(seq // 64, block)
        row, col = f // 4, f % 4
        vec[pl.ds(9 + row, 1), at(col, 256)] = jnp.sum(part[pl.ds(0, 8), pl.ds(256, 256)], 0, keepdims=True)

    def hidden_grad(r):
        part[:, at(r, cut)] = dot_t(dinner[...], wi[r])

    def wi_grad(t):
        row = scatter.order[t]

        def chunk(n):
            cols = at(n, 512)
            parts[1][row, :, cols] = dot(h_t[at(row, cut), :], dinner[:, cols]).astype(LOW)

        loop(hidden // 512, chunk)

    def first_norm_back():
        part_sums = jnp.zeros((8, width), F32)

        def block(i, carry):
            b_sum, g_sum, s_sum = carry
            rows, there = at(i, BLOCK), rows_of(mine, i, BLOCK)
            dh = dpre[rows, :] + (part[there, :] + recv1[rows, :])
            one = unit[rows, :]
            s = dh * pars[1:2, :]
            scale = inv[rows, :][:, 0:1]
            d = scale * (s - jnp.mean(s, 1, keepdims=True) - one * jnp.mean(s * one, 1, keepdims=True))
            dpre[rows, :] = d
            d_low = d.astype(LOW)
            dattn[there, :] = d_low
            return b_sum + fold(d_low.astype(F32)), g_sum + fold(dh * one), s_sum + fold(dh)

        b_sum, g_sum, s_sum = lax.fori_loop(0, own // BLOCK, block, (part_sums, part_sums, part_sums))
        for i, v in enumerate((b_sum, g_sum, s_sum)):
            vec[pl.ds(i, 1), :] = jnp.sum(v, 0, keepdims=True)

    def mixed_grad(n):
        rows = at(n, 256)
        total = dot_t(dattn[:, pl.ds(0, cut)], wo[0, rows, :])
        for r in range(1, LINE):
            total += dot_t(dattn[:, pl.ds(r * cut, cut)], wo[r, rows, :])
        dmixed[:, rows] = total.astype(LOW)

    def wo_grad(r):
        parts[2][r] = dot(mixed_t[...], dattn[:, at(r, cut)]).astype(LOW)

    def probs_copy(head):
        return pltpu.make_async_copy(saved["probs"].at[head], probs.at[head % 4], pr_sem.at[head % 4])

    def attend_back(pair, i):
        lanes = pl.ds(pair * LANES, LANES)
        keys_at, values_at = pl.ds(half + pair * LANES, LANES), pl.ds(2 * half + pair * LANES, LANES)
        slots = [(2 * pair + h) % 4 for h in range(2)]

        def block(i):
            rows = at(i, LANES)
            grad = dmixed[rows, lanes]

            def head(h, total):
                dp = dot_t(grad * head_lanes(h, LOW), qkv[:, values_at])
                p = probs[slots[0] + h, rows, :].astype(F32)
                d = (p * (dp - jnp.sum(p * dp, 1, keepdims=True))).astype(LOW)
                ds[h, rows, :] = d
                return total + dot(d, qkv[:, keys_at]) * head_lanes(h, F32)

            total = lax.fori_loop(0, 2, head, jnp.zeros((LANES, LANES), F32))
            dqkv[rows, lanes] = (total * 0.125).astype(LOW)

        if i < seq // LANES:
            block(i)
            return
        queries_t, grad_t = qkv[:, lanes].T, dmixed[:, lanes].T
        dk = jnp.concatenate([dot(queries_t[h * HD : (h + 1) * HD], ds[h]) for h in range(2)], 0)
        dqkv[:, keys_at] = dk.astype(LOW).T
        dv = jnp.concatenate([dot(grad_t[h * HD : (h + 1) * HD], probs[slots[h]]) for h in range(2)], 0)
        dqkv[:, values_at] = dv.astype(LOW).T

    def qkv_sums():
        for i, base in enumerate((0, 2 * half)):
            cols = pl.ds(base, half)

            def block(n, carry):
                return carry + fold(dqkv[at(n, 64), cols].astype(F32))

            v = lax.fori_loop(0, seq // 64, block, jnp.zeros((8, half), F32))
            vec[pl.ds(8, 1), pl.ds(i * half, half)] = jnp.sum(v, 0, keepdims=True)

    def wqkv_grad(t):
        row = scatter.order[t]

        def chunk(n):
            cols = at(n, 512)
            parts[3][row, :, cols] = dot(h_t[at(row, cut), :], dqkv[:, cols]).astype(LOW)

        loop(3 * half // 512, chunk)

    def weight_copy(r):
        return pltpu.make_async_copy(wqkv_h.at[r], wst.at[r % 2], st_sem.at[r % 2])

    def input_grad(r):
        weight_copy(r).wait()
        part[:, pl.ds(r * cut, cut)] = dot_t(dqkv[...], wst[r % 2])
        if r + 2 < LINE:
            weight_copy(r + 2).start()

    def finish_input():
        def block(i):
            rows, there = at(i, BLOCK), rows_of(mine, i, BLOCK)
            dx[rows, :] = (dpre[rows, :] + (part[there, :] + recv2[rows, :])).astype(LOW)

        loop(own // BLOCK, block)

    their_half = part.at[pl.ds(pl.multiple_of(theirs, own), own)]
    my_rows = pl.ds(pl.multiple_of(mine, own), own)

    swap1, swap2 = to_other(0, their_half, recv1), to_other(2, their_half, recv2)
    pass_d = to_other(1, dattn.at[my_rows], dattn.at[my_rows])
    seen = set()

    def once(*what):
        new = what not in seen
        seen.add(what)
        return new

    def need(*names):
        for n in names:
            if once("fetched", n):
                fetches[n].wait()

    def do(what, *n):
        if what == SEND:
            scatter.first(*n)
            scatter.direct(*n)
        elif what == ADD_A:
            scatter.second_a(*n)
        elif what == ADD_B:
            scatter.second_b(*n)
        elif what == SUM_UP:
            scatter.third(*n)
        elif what == LINE_STEP:
            scatter.line_step(*n)
        elif what == BACK_X:
            scatter.fourth_x(*n)
        elif what == BACK_Y:
            scatter.fourth_y(*n)
        elif what == OUTER_W:
            wout_grad(*n)
        elif what == INNER:
            need("wout")
            inner_grad(*n)
        elif what == HIDDEN:
            need("wi")
            hidden_grad(*n)
            if n[0] == LINE - 1:
                swap1.start()
        elif what == INNER_W:
            need("h_t")
            wi_grad(*n)
            if n[0] == LINE - 1:
                fetch("x_t", saved["x_t"], h_t)
        elif what == NORM_BACK:
            need("dpre", "unit", "inv", "pars")
            swap1.wait_recv()
            first_norm_back()
            pass_d.start()
        elif what == MIXED:
            need("wo")
            if once("passed"):
                pass_d.wait_recv()
            mixed_grad(*n)
        elif what == ATTN_W:
            need("mixed_t")
            wo_grad(scatter.order[n[0]])
        elif what == ATTEND:
            need("qkv")
            pair, i = n
            if i == 0:
                for h in range(2):
                    probs_copy(2 * pair + h).wait()
            attend_back(pair, i)
            if i == seq // LANES:
                for h in range(2):
                    if 2 * pair + h + 4 < half // HD:
                        probs_copy(2 * pair + h + 4).start()
        elif what == QKV_W:
            need("x_t")
            wqkv_grad(*n)
        elif what == INPUT:
            if n[0] == 0:
                swap1.wait_send()
            input_grad(*n)
            if n[0] == LINE - 1:
                swap2.start()
        elif what == SUMS:
            qkv_sums()
            totals.step(0)
        elif what in (SUMS_X, SUMS_Y, SUMS_LINE):
            totals.step(1 + what - SUMS_X)
        elif what == INPUT_LAST:
            swap2.wait_recv()
            finish_input()
        elif what == PLACE_OUT:
            place_out.start()
        elif what == PLACE_INPUT:
            place_dx.start()

    fetch("dout", saved["dout"], dout)
    fetch("act_t", saved["act_t"], act_t)
    greet(spot, far=True)
    need("dout", "act_t")
    fetch("wout", wout_h, wout)
    slope_copy(0).start()
    fetch("wi", wi_h, wi)
    fetch("h_t", saved["h_t"], h_t)
    for name, dst in (("dpre", dpre), ("unit", unit), ("inv", inv), ("pars", pars)):
        fetch(name, saved[name], dst)
    fetch("wo", wo_h, wo)
    fetch("mixed_t", saved["mixed_t"], mixed_t)
    fetch("qkv", saved["qkv"], qkv)
    for head in range(4):
        probs_copy(head).start()
    weight_copy(0).start()
    weight_copy(1).start()
    vec[...] = jnp.zeros_like(vec)
    for i in range(3):
        vec[pl.ds(3 + i, 1), :] = jnp.sum(sums2[i], 0, keepdims=True)
    for step in BACKWARD_ORDER:
        do(*step)
    whole = totals.total()
    totals.drain()
    for i in range(8):
        o_bias[pl.ds(i, 1), :] = whole[8 + i : 9 + i, :]
    vecs[-1][0] = whole
    o_norms[...] = vecs[-1][0, pl.ds(0, 8), at(spot.row, cut)]
    for g in range(len(SCATTERED)):
        scatter.fifth(g)
    scatter.drain()
    for c in (swap2, pass_d):
        c.wait_send()
    place_out.wait()
    place_dx.wait()


def backward(weights, saved):
    wqkv, wo, wi, wout = weights
    shapes = [w.shape for w in (wout, wi, wo, wqkv)]
    seq, width = saved["dout"].shape
    half, hidden, own = wo.shape[1], wi.shape[2], seq // 2
    cut = width // LINE

    groups = Scatter.sizes(shapes)

    def each(f):
        return [pltpu.VMEM(f(*s), LOW) for s in groups]

    def like(name):
        return pltpu.VMEM(saved[name].shape, saved[name].dtype)

    placed = jax.ShapeDtypeStruct((2 * seq, cut), LOW)
    scratch = (
        [pltpu.VMEM(w.shape, LOW) for w in (wo, wi, wout)]
        + [pltpu.VMEM((2,) + wqkv.shape[1:], LOW)]
        + [pltpu.VMEM(s, LOW) for s in shapes]
        + each(lambda r, c, n: (n, r // 8, c)) * 2
        + each(lambda r, c, n: (n, r // 4, c)) * 2
        + each(lambda r, c, n: (LINE + 1, r if n == 1 else r // 4, c))
        + each(lambda r, c, n: (r // 4, c))
        + [like(n) for n in ("act_t", "dout", "h_t", "dpre", "unit", "inv", "pars", "mixed_t", "qkv")]
        + [
            pltpu.VMEM((2, seq, 256), F32), pltpu.VMEM((4, seq, seq), LOW), pltpu.VMEM((2, seq, seq), LOW),
            pltpu.VMEM((seq, hidden), LOW), pltpu.VMEM((seq, width), F32), pltpu.VMEM((own, width), F32),
            pltpu.VMEM((own, width), F32), pltpu.VMEM((seq, width), LOW), pltpu.VMEM((seq, half), LOW),
            pltpu.VMEM((seq, 3 * half), LOW), pltpu.VMEM((own, width), LOW),
        ]
        + [pltpu.VMEM(s, F32) for s in ((16, width), (8, width)) + ((16, width),) * 4 + ((LINE, 16, width),)]
        + Scatter.SEMS
        + Sums.SEMS
        + Spread.SEMS * 2
        + [pltpu.SemaphoreType.DMA((n,)) for n in (3, 3, 16, 2, 2, 4)]
    )
    res = pl.pallas_call(
        backward_kernel,
        name="backward",
        out_shape=[jax.ShapeDtypeStruct(s[1:], LOW) for s in shapes]
        + [placed] * 2
        + [jax.ShapeDtypeStruct((8, cut), F32), jax.ShapeDtypeStruct((8, width), F32)],
        in_specs=[ANYWHERE] * (GROUPS + len(SAVED)) + [IN_VMEM],
        out_specs=[ANYWHERE] * (GROUPS + 2) + [IN_VMEM] * 2,
        scratch_shapes=scratch,
        compiler_params=pltpu.CompilerParams(collective_id=1, has_side_effects=True, vmem_limit_bytes=63 * 2**20),
    )(*weights, *[saved[n] for n in SAVED], saved["sums"])
    return res


def finish_kernel(wqkv, wo, wi, wout, out, dx, norms, biases, *outs):
    wq_o, wk_o, wv_o, wo_o, wi_o, wout_o, out_o, dx_o, bq_o, bv_o, bi_o = outs[:11]
    half = wq_o.shape[1]
    for i, o in enumerate((wq_o, wk_o, wv_o)):
        o[...] = wqkv[:, i * half : (i + 1) * half].astype(F32)
    for src, dst in ((wo, wo_o), (wi, wi_o), (wout, wout_o)):
        dst[...] = src[...].astype(F32)
    out_o[...] = out[...]
    dx_o[...] = dx[...]

    @pl.when(pl.program_id(0) == 0)
    def _():
        bq_o[...] = biases[0, 0:half]
        bv_o[...] = biases[0, half : 2 * half]
        wide = biases.shape[1]
        for i in range(bi_o.shape[0] // wide):
            bi_o[i * wide : (i + 1) * wide] = biases[1 + i, :]
        for i, o in enumerate(outs[11:]):
            o[...] = norms[i, :]


def finish(wqkv, wo, wi, wout, out, dx, norms, biases, steps=2):
    half, cut = wqkv.shape[1] // 3, norms.shape[1]
    big = [(wqkv.shape[0], half)] * 3 + [w.shape for w in (wo, wi, wout)]

    def tiled(shape):
        return pl.BlockSpec((shape[0] // steps, shape[1]), lambda i: (i, 0))

    def whole(shape):
        return pl.BlockSpec(shape, lambda i: (0,) * len(shape))

    vectors = [(half,), (half,), (wi.shape[1],)] + [(cut,)] * 6
    return pl.pallas_call(
        finish_kernel,
        name="finish",
        grid=(steps,),
        out_shape=[jax.ShapeDtypeStruct(s, F32) for s in big]
        + [jax.ShapeDtypeStruct(v.shape, LOW) for v in (out, dx)]
        + [jax.ShapeDtypeStruct(s, F32) for s in vectors],
        in_specs=[tiled(v.shape) for v in (wqkv, wo, wi, wout, out, dx)] + [whole(norms.shape), whole(biases.shape)],
        out_specs=[tiled(s) for s in big] + [tiled(out.shape)] * 2 + [whole(s) for s in vectors],
        compiler_params=pltpu.CompilerParams(vmem_limit_bytes=63 * 2**20),
    )(wqkv, wo, wi, wout, out, dx, norms, biases)


def per_chip(
    hidden_in, segment_ids, query_weight, query_bias, key_weight, value_weight, value_bias, attn_out_weight,
    attn_out_bias, norm1_gain, first_norm_offset, inner_weight, inner_bias, outer_weight, outer_bias, norm2_gain,
    second_norm_offset, cotangent,
):
    half = query_weight.shape[1]
    small = (attn_out_bias, norm1_gain, first_norm_offset, outer_bias, norm2_gain, second_norm_offset)
    weights, saved = forward(
        hidden_in, cotangent, query_weight, key_weight, value_weight, attn_out_weight, inner_weight, outer_weight,
        segment_ids, query_bias, value_bias, inner_bias, small,
    )
    wout, wi, wo, wqkv, layer_out, input_grad, norms, biases = backward(weights, saved)
    wq, wk, wv, wo, wi, wout, layer_out, input_grad, bq, bv, bi, bo, g1, b1, bout, g2, b2 = finish(
        wqkv, wo, wi, wout, layer_out, input_grad, norms, biases
    )
    return layer_out, input_grad, wq, bq, wk, wv, bv, wo, bo, g1, b1, wi, bi, wout, bout, g2, b2


def solution(mesh):
    def whole(*args):
        segments, wq = args[1], args[2]
        sizes = tuple(mesh.shape[a] for a in ("dp", "row", "col"))
        fits = sizes == (4, LINE, 2) and segments.shape == (16, SEQ) and wq.shape[0] == MODEL_WIDTH
        body = per_chip if fits else shards
        return jax.shard_map(body, mesh=mesh, in_specs=IN_SPECS, out_specs=OUT_SPECS, check_vma=False)(*args)

    return whole
```
